32 devices in a mesh: dp: 8 (over z, y), mp: 4 (over x, core).
Axes of the slice: x: 2, y: 2, z: 4, core: 2. Of those that a mesh axis runs over, the one named last changes fastest.
Arguments:
- tokens: bfloat16 [8192, 1024], P(('dp', 'mp')), may hold values from -6 to 6
- w_attn: bfloat16 [1024, 4, 1024], P('mp'), may hold values from -4 to 4
- w_ffn: bfloat16 [4096, 2, 1024], P('mp'), may hold values from -4 to 4
- ada_attn: float32 [8, 2, 1024], replicated, may hold values from -2.5 to 2.5
- ada_ffn: float32 [8, 2, 1024], replicated, may hold values from -2.5 to 2.5
- codebook: int32 [8], replicated, may hold values from 0 to 7
- group_sizes: int32 [2], replicated, may hold values from 1 to 6, 8 in all
- partner_pick: int32 [8], replicated, may hold values from 0 to 23
- prompt_start: int32 [8], replicated, may hold values from 0 to 768
- prompt_len: int32 [8], replicated, may hold values from 64 to 256, as said below
- cotangent: bfloat16 [8192, 1024], P(('dp', 'mp')), may hold values from -6 to 6
Outputs:
- output: bfloat16 [8192, 1024], P(('dp', 'mp'))
- grad_tokens: bfloat16 [8192, 1024], P(('dp', 'mp'))
- grad_attn: float32 [1024, 4, 1024], P('mp', None, 'dp')
- grad_ffn: float32 [4096, 2, 1024], P('mp', None, 'dp')
- grad_ada_attn: float32 [8, 2, 1024], P(None, None, ('dp', 'mp'))
- grad_ada_ffn: float32 [8, 2, 1024], P(None, None, ('dp', 'mp'))
The draws below stay inside these ranges and needn't reach their ends.
Inputs may be any that keep to these rules, and one draw needn't show every extreme that they name: `group_sizes`: the sizes sum to 8. `prompt_len`: some row offers exactly 256 frames.
All inputs are finite; a program needn't handle non-finite values.
Results may differ from the reference program's by a relative error of at most 0.019.
Values may be sent and summed in bfloat16 or wider, within the bound.
A program may use at most 128 MiB of HBM per device.

```python
import math
import jax
import jax.numpy as jnp
import numpy as np
from jax import lax

D = 1024
H = 16
HD = 64
FF = 4096
NCB = 8
LEN = 1024
PMAX = 256
GMAX = 6
ROWS = 8
TOKENS = 8192
GROUPS = 2
N_MP = 4


def draw_w_attn(key, part):
    slot_scale = jnp.where(jnp.arange(4) < 3, (1.0 / D) ** 0.5, ((LEN + PMAX) / (3.0 * D)) ** 0.5).astype(jnp.float32)
    raw_draw = jax.random.truncated_normal(key, -4.0, 4.0, (H * HD, 4, D), jnp.float32)
    return (raw_draw * slot_scale[None, :, None]).astype(jnp.bfloat16)


def draw_w_ffn(key, part):
    slot_scale = jnp.array([(1.0 / D) ** 0.5, (2.0 / FF) ** 0.5], jnp.float32)
    raw_draw = jax.random.truncated_normal(key, -4.0, 4.0, (FF, 2, D), jnp.float32)
    return (raw_draw * slot_scale[None, :, None]).astype(jnp.bfloat16)


def draw_prompt_len(key, part):
    first_key, second_key = jax.random.split(key)
    lengths = jax.random.randint(first_key, (ROWS,), PMAX // 4, PMAX + 1, dtype=jnp.int32)
    chosen = jax.random.randint(second_key, (), 0, ROWS, dtype=jnp.int32)
    return lengths.at[chosen].set(PMAX).astype(jnp.int32)


def touch_ends(values, rng, low, largest):
    longest = values.shape.index(max(values.shape))
    spots = []
    for shift in (0, 1):
        where = [jax.random.randint(jax.random.fold_in(rng, axis), (), 0, length) for axis, length in enumerate(values.shape)]
        where[longest] = (where[longest] + shift) % values.shape[longest]
        spots.append(tuple(where))
    return values.at[spots[0]].set(low).at[spots[1]].set(largest)


def steps_of(key, shape, cuts, low, top_value):
    gain = 1.0
    for dim, parts in cuts:
        draws = jax.random.uniform(jax.random.fold_in(jax.random.fold_in(key, 6), dim), (parts,), jnp.float32, low / len(cuts), top_value / len(cuts))
        gain = gain * jnp.repeat(jnp.exp(draws), shape[dim] // parts).reshape((-1,) + (1,) * (len(shape) - 1 - dim))
    return gain


def length_profile(number_of, total, limit, lean):
    weights = [(1 << 20) // math.isqrt(standing ** lean) + 1 for standing in range(2, number_of + 1)]
    spare, given = total - limit - (number_of - 1), [1] * (number_of - 1)
    while spare > 0:
        free = [i for i in range(number_of - 1) if given[i] < limit]
        whole, left = sum([weights[i] for i in free]), spare
        for i in free:
            addition = min(limit - given[i], max(1, left * weights[i] // whole), spare)
            given[i] = given[i] + addition
            spare = spare - addition
    return np.array([limit] + given)


def ragged(stream_key, amount, total, bound, slope):
    if amount == 2:
        one = jax.random.randint(stream_key, (), max(1, total - bound), min(bound, total - 1) + 1)
        return jnp.stack([one, total - one])
    sizes = jnp.asarray(length_profile(amount, total, bound, slope), jnp.int32)
    pairs = (amount - 1) // 2
    giver, taker = sizes[1:1 + 2 * pairs:2], sizes[2:2 + 2 * pairs:2]
    room = jnp.minimum(giver - 1, bound - taker)
    passed = jax.random.randint(jax.random.fold_in(stream_key, 1), (pairs,), 0, 1 << 20) % (room + 1)
    sizes = sizes.at[1:1 + 2 * pairs:2].set(giver - passed).at[2:2 + 2 * pairs:2].set(taker + passed)
    return sizes[jax.random.permutation(jax.random.fold_in(stream_key, 2), amount)]


def normal_values(key, dims, scale, bound, cuts=(), kind=jnp.bfloat16):
    drawn = jax.random.normal(key, dims, jnp.float32) * scale
    if len(cuts) > 0:
        drawn = steps_of(key, dims, cuts, -0.22, 0.18) * drawn
    return jnp.clip(drawn, min=-bound, max=bound).astype(kind)


def setup_inputs(seed: int = 0) -> dict:
    arg_keys = jax.random.split(jax.random.key(seed), 12)
    tokens = normal_values(arg_keys[0], (TOKENS, D), 1.0, 6.0, ((0, 32),))
    w_attn = draw_w_attn(jax.random.fold_in(arg_keys[11], 71), 0)
    w_ffn = draw_w_ffn(jax.random.fold_in(arg_keys[11], 71), 0)
    ada_attn = normal_values(arg_keys[3], (NCB, 2, D), 0.4, 2.5, (), jnp.float32)
    ada_ffn = normal_values(arg_keys[4], (NCB, 2, D), 0.4, 2.5, (), jnp.float32)
    codebook = touch_ends(jax.random.randint(arg_keys[5], (ROWS,), 0, NCB), jax.random.fold_in(arg_keys[5], 1), 0, NCB - 1).astype(jnp.int32)
    group_sizes = ragged(arg_keys[6], GROUPS, ROWS, GMAX, 2).astype(jnp.int32)
    partner_pick = touch_ends(jax.random.randint(arg_keys[7], (ROWS,), 0, 4 * GMAX), jax.random.fold_in(arg_keys[7], 1), 0, (4 * GMAX) - 1).astype(jnp.int32)
    prompt_start = touch_ends(jax.random.randint(arg_keys[8], (ROWS,), 0, LEN - PMAX + 1), jax.random.fold_in(arg_keys[8], 1), 0, LEN - PMAX).astype(jnp.int32)
    prompt_len = draw_prompt_len(jax.random.fold_in(arg_keys[11], 71), 0)
    cotangent = normal_values(arg_keys[10], (TOKENS, D), 1.0, 6.0, ((0, 32),))
    return dict(tokens=tokens, w_attn=w_attn, w_ffn=w_ffn, ada_attn=ada_attn, ada_ffn=ada_ffn, codebook=codebook, group_sizes=group_sizes, partner_pick=partner_pick, prompt_start=prompt_start, prompt_len=prompt_len, cotangent=cotangent)


@jax.custom_vjp
def low(v):
    return lax.optimization_barrier(v.astype(jnp.bfloat16)).astype(jnp.float32)

@jax.custom_vjp
def low_back(v):
    return v

def low_keep(v):
    return (low(v), None)

def low_pass(kept, grad):
    return (grad,)

def back_keep(v):
    return (v, None)

def back_low(kept, grad):
    return (low(grad),)
low.defvjp(low_keep, low_pass)
low_back.defvjp(back_keep, back_low)
epsilon = 1e-05
highest = lax.Precision.HIGHEST

def partner_rows(group_sizes, partner_pick):
    group_end = jnp.cumsum(group_sizes).astype(jnp.int32)
    begins = (group_end - group_sizes).astype(jnp.int32)
    row_ids = jnp.arange(partner_pick.shape[0], dtype=jnp.int32)
    owner_group = lax.optimization_barrier(jnp.sum((group_end[None, :] <= row_ids[:, None]).astype(jnp.int32), axis=1)).astype(jnp.int32)
    member = (owner_group[:, None] == jnp.arange(group_sizes.shape[0], dtype=jnp.int32)[None, :]).astype(jnp.int32)
    first_row = lax.optimization_barrier(jnp.sum(member * begins[None, :], axis=1)).astype(jnp.int32)
    group_len = lax.optimization_barrier(jnp.sum(member * group_sizes[None, :], axis=1)).astype(jnp.int32)
    span_size = jnp.maximum(group_len - 1, 1)
    return (first_row + (row_ids - first_row + 1 + partner_pick % span_size) % group_len).astype(jnp.int32)

def adaptive_norm(inputs, table, token_codes):
    center = inputs - lax.optimization_barrier(jnp.mean(inputs, axis=-1, keepdims=True))
    spread = lax.optimization_barrier(jnp.mean(center * center, axis=-1, keepdims=True))
    normed = center * lax.rsqrt(spread + epsilon)
    return (1.0 + table[token_codes, 0]) * normed + table[token_codes, 1]

def attend_row(packed):
    queries, own_keys, own_values, far_keys, far_values, far_valid = packed
    key_rows = jnp.concatenate([own_keys, far_keys], axis=0)
    value_rows = jnp.concatenate([own_values, far_values], axis=0)
    key_mask = jnp.concatenate([jnp.ones((own_keys.shape[0],), dtype=jnp.bool_), far_valid])
    scores = low_back(jnp.einsum('qhd,khd->hqk', queries, key_rows, precision=highest) * HD ** (-0.5))
    scores = jnp.where(key_mask[None, None, :], scores, -1000000000.0)
    weights = low(jax.nn.softmax(scores, axis=-1))
    return low_back(low(jnp.einsum('hqk,khd->qhd', weights, value_rows, precision=highest)))

def forward(inputs, w_attn, w_ffn, ada_attn, ada_ffn, token_codes, partner, prompt_start, prompt_len):
    head_group = H * HD // N_MP
    ffn_group = FF // N_MP
    normed_attn = low(adaptive_norm(inputs, ada_attn, token_codes))
    pieces = []
    for group in range(N_MP):
        shared = low_back(normed_attn)
        weight_cut = w_attn[group * head_group:(group + 1) * head_group, 0:3, :]
        pieces.append(jnp.einsum('td,jsd->tsj', shared, weight_cut, precision=highest))
    projected = low_back(low(jnp.concatenate(pieces, axis=2)))
    queries = projected[:, 0, :].reshape(ROWS, LEN, H, HD)
    key_all = projected[:, 1, :].reshape(ROWS, LEN, H, HD)
    value_all = projected[:, 2, :].reshape(ROWS, LEN, H, HD)
    take_window = jax.vmap(lambda sequence, offset: lax.dynamic_slice_in_dim(sequence, offset, PMAX, 0))
    far_keys = take_window(key_all, prompt_start)[partner]
    far_values = take_window(value_all, prompt_start)[partner]
    far_valid = jnp.arange(PMAX, dtype=jnp.int32)[None, :] < prompt_len[partner][:, None]
    attended = lax.map(jax.checkpoint(attend_row), (queries, key_all, value_all, far_keys, far_values, far_valid))
    attended = attended.reshape(TOKENS, H * HD)
    branch = jnp.zeros((TOKENS, D), jnp.float32)
    for group in range(N_MP):
        lower_col = group * head_group
        upper_col = lower_col + head_group
        branch = branch + low(jnp.dot(attended[:, lower_col:upper_col], w_attn[lower_col:upper_col, 3, :], precision=highest))
    middle = inputs + low_back(branch)
    normed_ffn = low(adaptive_norm(middle, ada_ffn, token_codes))
    branch = jnp.zeros((TOKENS, D), jnp.float32)
    for group in range(N_MP):
        lower_col = group * ffn_group
        upper_col = lower_col + ffn_group
        shared = low_back(normed_ffn)
        up_part = low_back(jnp.dot(shared, w_ffn[lower_col:upper_col, 0, :].T, precision=highest))
        act_part = low(jax.nn.gelu(up_part, approximate=False))
        branch = branch + low(jnp.dot(act_part, w_ffn[lower_col:upper_col, 1, :], precision=highest))
    return middle + low_back(branch)

def reference(tokens, w_attn, w_ffn, ada_attn, ada_ffn, codebook, group_sizes, partner_pick, prompt_start, prompt_len, cotangent):
    partner = partner_rows(group_sizes, partner_pick)
    token_codes = codebook[(jnp.arange(TOKENS, dtype=jnp.int32) // LEN).astype(jnp.int32)]

    def run_layer(inputs, attn_weights, ffn_weights, attn_table, ffn_table):
        return forward(inputs, attn_weights, ffn_weights, attn_table, ffn_table, token_codes, partner, prompt_start, prompt_len)
    result, pullback = jax.vjp(run_layer, tokens.astype(jnp.float32), w_attn.astype(jnp.float32), w_ffn.astype(jnp.float32), ada_attn, ada_ffn)
    gradients = pullback(cotangent.astype(jnp.float32))
    return (result.astype(jnp.bfloat16), gradients[0].astype(jnp.bfloat16), gradients[1], gradients[2], gradients[3], gradients[4])
```

```python
import functools

import jax
import jax.numpy as jnp
from jax import lax
from jax.experimental import pallas as pl
from jax.experimental.pallas import tpu as pltpu
from jax.sharding import PartitionSpec as P

MESH = pl.DeviceIdType.MESH
F32 = jnp.float32
BF16 = jnp.bfloat16

HD = 64
LEN = 1024
PMAX = 256


epsilon = 1e-05
highest = lax.Precision.HIGHEST


def partner_rows(group_sizes, partner_pick):
    group_end = jnp.cumsum(group_sizes)
    begins = group_end - group_sizes
    row_ids = jnp.arange(partner_pick.shape[0], dtype=jnp.int32)
    owner_group = jnp.sum((group_end[None, :] <= row_ids[:, None]).astype(jnp.int32), axis=1)
    member = (
        owner_group[:, None] == jnp.arange(group_sizes.shape[0], dtype=jnp.int32)[None, :]
    ).astype(jnp.int32)
    first_row = jnp.sum(member * begins[None, :], axis=1)
    group_len = jnp.sum(member * group_sizes[None, :], axis=1)
    span_size = jnp.maximum(group_len - 1, 1)
    return first_row + (row_ids - first_row + 1 + partner_pick % span_size) % group_len


def adaptive_norm(inputs, table, code_hot):
    coefficients = jnp.dot(code_hot, table.reshape(table.shape[0], -1), precision=highest)
    coefficients = coefficients.reshape(inputs.shape[0], 2, inputs.shape[1])
    center = inputs - jnp.mean(inputs, axis=-1, keepdims=True)
    spread = jnp.mean(center * center, axis=-1, keepdims=True)
    normed = center * lax.rsqrt(spread + epsilon)
    return (1.0 + coefficients[:, 0, :]) * normed + coefficients[:, 1, :]


def inner_rows(left, right):
    return lax.dot_general(
        left, right, (((0,), (0,)), ((), ())), preferred_element_type=jnp.float32
    )


def inner_cols(left, right):
    return lax.dot_general(
        left, right, (((1,), (1,)), ((), ())), preferred_element_type=jnp.float32
    )


def row_scores(queries, key_rows, far_valid):
    key_mask = jnp.concatenate([jnp.ones((queries.shape[0],), dtype=jnp.bool_), far_valid])
    scores = jnp.einsum(
        "qhd,khd->hqk", queries, key_rows, preferred_element_type=jnp.float32
    ) * HD ** (-0.5)
    return jnp.where(key_mask[None, None, :], scores, -1000000000.0)


def attend(packed):
    queries, own_keys, own_values, far_keys, far_values, far_valid = packed
    key_rows = jnp.concatenate([own_keys, far_keys], axis=0)
    value_rows = jnp.concatenate([own_values, far_values], axis=0)
    scores = row_scores(queries, key_rows, far_valid)
    row_max = jnp.max(scores, axis=-1, keepdims=True)
    log_total = row_max + jnp.log(jnp.sum(jnp.exp(scores - row_max), axis=-1, keepdims=True))
    prob_low = jnp.exp(scores - log_total).astype(jnp.bfloat16)
    mixed = jnp.einsum("hqk,khd->qhd", prob_low, value_rows, preferred_element_type=jnp.float32)
    return (mixed.astype(jnp.bfloat16), log_total)


def attend_back(packed):
    queries, own_keys, own_values, far_keys, far_values, far_valid, log_total, d_mixed = packed
    key_rows = jnp.concatenate([own_keys, far_keys], axis=0)
    value_rows = jnp.concatenate([own_values, far_values], axis=0)
    scores = row_scores(queries, key_rows, far_valid)
    attn_prob = jnp.exp(scores - log_total)
    prob_low = attn_prob.astype(jnp.bfloat16)
    d_values = jnp.einsum("hqk,qhd->khd", prob_low, d_mixed, preferred_element_type=jnp.float32)
    d_prob = jnp.einsum("qhd,khd->hqk", d_mixed, value_rows, preferred_element_type=jnp.float32)
    row_delta = jnp.sum(attn_prob * d_prob, axis=-1, keepdims=True)
    d_scores = (attn_prob * (d_prob - row_delta)).astype(jnp.bfloat16)
    d_queries = jnp.einsum(
        "hqk,khd->qhd", d_scores, key_rows, preferred_element_type=jnp.float32
    ) * HD ** (-0.5)
    d_keys = jnp.einsum(
        "hqk,qhd->khd", d_scores, queries, preferred_element_type=jnp.float32
    ) * HD ** (-0.5)
    own_len = queries.shape[0]
    return (d_queries, d_keys[:own_len], d_values[:own_len], d_keys[own_len:], d_values[own_len:])


class Links:
    def __init__(self, z_size, send_sem, recv_sem):
        self.dp = lax.axis_index("dp")
        self.mp = lax.axis_index("mp")
        self.z_size = z_size
        self.y = lax.rem(self.dp, 2)
        self.z = self.dp // 2
        self.core = lax.rem(self.mp, 2)
        self.x = self.mp // 2
        self.sib = (self.dp, self.mp + 1 - 2 * self.core)
        self.xpeer = (self.dp, self.mp + 2 - 4 * self.x)
        self.ypeer = (self.dp + 1 - 2 * self.y, self.mp)
        self.right = (self.dp + 2, self.mp)
        self.left = (self.dp - 2, self.mp)
        self.send_sem = send_sem
        self.recv_sem = recv_sem
        self.used = 0
        self.sent = []

    def take(self, count=1):
        first = self.used
        self.used += count
        return first

    def copy(self, src, dst, number, device):
        return pltpu.make_async_remote_copy(
            src_ref=src,
            dst_ref=dst,
            send_sem=self.send_sem.at[number],
            recv_sem=self.recv_sem.at[number],
            device_id=device,
            device_id_type=MESH,
        )

    def barrier(self):
        bar = pltpu.get_barrier_semaphore()
        for device in (self.sib, self.xpeer, self.ypeer):
            pl.semaphore_signal(bar, inc=1, device_id=device, device_id_type=MESH)

        @pl.when(self.z > 0)
        def _():
            pl.semaphore_signal(bar, inc=1, device_id=self.left, device_id_type=MESH)

        @pl.when(self.z < self.z_size - 1)
        def _():
            pl.semaphore_signal(bar, inc=1, device_id=self.right, device_id_type=MESH)

        inner = (self.z > 0).astype(jnp.int32) + (self.z < self.z_size - 1).astype(jnp.int32)
        pl.semaphore_wait(bar, 3 + inner)


class LineReduce:
    def __init__(self, links, local, from_y, held, from_left, from_right):
        self.k = links
        self.local, self.from_y, self.held = local, from_y, held
        self.from_left, self.from_right = from_left, from_right
        n = links.z_size
        self.ny = links.take(n)
        self.nr = links.take(n)
        self.nl = links.take(n)

    def y_copy(self, d):
        k = self.k
        other = 2 * d + 1 - k.y
        return k.copy(self.local.at[other], self.from_y.at[d], self.ny + d, k.ypeer)

    def send_y(self, dests=None):
        for d in dests or range(self.k.z_size):
            self.y_copy(d).start()

    def z_copy(self, d, rightward):
        k = self.k
        if rightward:
            return k.copy(self.held.at[d], self.from_left.at[d], self.nr + d, k.right)
        return k.copy(self.held.at[d], self.from_right.at[d], self.nl + d, k.left)

    def add(self, d, what):
        total = self.held[d].astype(F32) + what[d].astype(F32)
        self.held[d] = total.astype(self.held.dtype)

    def order(self):
        n = self.k.z_size
        return [n - 1, 0] + list(range(1, n - 1))

    def merge_y(self, d):
        k = self.k
        self.y_copy(d).wait_recv()
        total = self.local[2 * d + k.y].astype(F32) + self.from_y[d].astype(F32)
        self.held[d] = total.astype(self.held.dtype)

    def move(self, d):
        k = self.k

        @pl.when(k.z < d)
        def _():
            @pl.when(k.z > 0)
            def _():
                self.z_copy(d, True).wait_recv()
                self.add(d, self.from_left)

            self.z_copy(d, True).start()

        @pl.when(k.z > d)
        def _():
            @pl.when(k.z < k.z_size - 1)
            def _():
                self.z_copy(d, False).wait_recv()
                self.add(d, self.from_right)

            self.z_copy(d, False).start()

    def finish(self, store):
        k = self.k
        n = k.z_size
        for d in range(n):

            @pl.when(k.z == d)
            def _(d=d):
                total = self.held[d].astype(F32)
                if d > 0:
                    self.z_copy(d, True).wait_recv()
                    total = total + self.from_left[d].astype(F32)
                if d < n - 1:
                    self.z_copy(d, False).wait_recv()
                    total = total + self.from_right[d].astype(F32)
                store(total)

    def wait_sends(self):
        k = self.k
        for d in range(k.z_size):
            self.y_copy(d).wait_send()

            @pl.when(k.z < d)
            def _(d=d):
                self.z_copy(d, True).wait_send()

            @pl.when(k.z > d)
            def _(d=d):
                self.z_copy(d, False).wait_send()


def grads_kernel(z_size, heads_rows, ga, gf, ta, out_a, out_f, out_t, *scratch):
    bufs = scratch[:-2]
    k = Links(z_size, *scratch[-2:])
    k.barrier()
    units = []
    for local, at in ((gf, 0), (ga, 4), (ta, 8)):
        units.append(LineReduce(k, local, *bufs[at : at + 4]))
    for unit in units:
        unit.send_y(unit.order())
    for unit in units:
        for d in unit.order():
            unit.merge_y(d)
            unit.move(d)
    half = gf.shape[1] // 2
    quarter = ga.shape[1] // 4

    def store_f(total):
        for s in range(2):
            out_f[pl.ds(s, half, stride=2), :] = total[s * half : (s + 1) * half]

    def store_a(total):
        for s in range(4):
            out_a[pl.ds(s, quarter, stride=4), :] = total[s * quarter : (s + 1) * quarter]

    def store_t(total):
        out_t[...] = total

    for unit, store in zip(units, (store_f, store_a, store_t)):
        unit.finish(store)
    for unit in units:
        unit.wait_sends()


def reduce_grads(ga, gf, ta, dp_size):
    z_size = dp_size // 2
    bufs = []
    for block in (gf, ga, ta):
        bufs += [pltpu.VMEM((z_size,) + block.shape[1:], block.dtype)] * 4
    copies = 3 * 3 * z_size
    return pl.pallas_call(
        functools.partial(grads_kernel, z_size, 4),
        out_shape=(
            jax.ShapeDtypeStruct(ga.shape[1:], F32),
            jax.ShapeDtypeStruct(gf.shape[1:], F32),
            jax.ShapeDtypeStruct(ta.shape[1:], F32),
        ),
        in_specs=[pl.BlockSpec(memory_space=pltpu.VMEM)] * 3,
        out_specs=[pl.BlockSpec(memory_space=pltpu.VMEM)] * 3,
        scratch_shapes=bufs
        + [pltpu.SemaphoreType.DMA((copies,)), pltpu.SemaphoreType.DMA((copies,))],
        compiler_params=pltpu.CompilerParams(
            collective_id=1, has_side_effects=True, vmem_limit_bytes=60 << 20
        ),
    )(ga, gf, ta)


def shards(
    tokens,
    w_attn,
    w_ffn,
    ada_attn,
    ada_ffn,
    codebook,
    group_sizes,
    partner_pick,
    prompt_start,
    prompt_len,
    cotangent,
):
    tok_rows, width = tokens.shape
    mp_size = lax.axis_size("mp")
    dp_index = lax.axis_index("dp")
    mp_index = lax.axis_index("mp")
    block_tokens = tok_rows * mp_size
    seq_here = block_tokens // LEN
    head_cols = w_attn.shape[0]
    heads_here = head_cols // HD
    total_rows = codebook.shape[0]
    partner = partner_rows(group_sizes, partner_pick)
    first_row = dp_index * seq_here
    tok_global = (dp_index * mp_size + mp_index) * tok_rows + jnp.arange(tok_rows, dtype=jnp.int32)
    row_pick = (
        (tok_global // LEN)[:, None] == jnp.arange(total_rows, dtype=jnp.int32)[None, :]
    ).astype(jnp.int32)
    token_codes = jnp.sum(row_pick * codebook[None, :], axis=1)
    code_hot = (
        token_codes[:, None] == jnp.arange(ada_attn.shape[0], dtype=jnp.int32)[None, :]
    ).astype(jnp.float32)
    my_partner = lax.dynamic_slice_in_dim(partner, first_row, seq_here)
    my_starts = lax.dynamic_slice_in_dim(prompt_start, first_row, seq_here)
    partner_hot = (my_partner[:, None] == jnp.arange(total_rows, dtype=jnp.int32)[None, :]).astype(
        jnp.int32
    )
    partner_len = jnp.sum(partner_hot * prompt_len[None, :], axis=1)
    far_valid = jnp.arange(PMAX, dtype=jnp.int32)[None, :] < partner_len[:, None]
    inputs = tokens.astype(jnp.float32)
    normed_attn = adaptive_norm(inputs, ada_attn, code_hot).astype(jnp.bfloat16)
    normed_attn_full = lax.all_gather(normed_attn, "mp", axis=0, tiled=True)
    w_qkv = w_attn[:, 0:3, :]
    w_out = w_attn[:, 3, :]
    qkv_low = jnp.einsum(
        "td,jsd->tsj", normed_attn_full, w_qkv, preferred_element_type=jnp.float32
    ).astype(jnp.bfloat16)
    kv_rows = qkv_low[:, 1:3, :].reshape(seq_here, LEN, 2 * head_cols)
    windows = jax.vmap(
        lambda sequence, offset: lax.dynamic_slice_in_dim(sequence, offset, PMAX, 0)
    )(kv_rows, my_starts)
    shard_rows = lax.all_gather(windows, "dp", axis=0, tiled=True)
    row_ids = jnp.arange(shard_rows.shape[0], dtype=jnp.int32)
    picker = (my_partner[:, None] == row_ids[None, :]).astype(jnp.bfloat16)
    prompt_sum = jnp.einsum("kr,rpc->kpc", picker, shard_rows, preferred_element_type=jnp.float32)
    prompt_kv = prompt_sum.astype(jnp.bfloat16)
    queries = qkv_low[:, 0, :].reshape(seq_here, LEN, heads_here, HD)
    own_keys = qkv_low[:, 1, :].reshape(seq_here, LEN, heads_here, HD)
    own_values = qkv_low[:, 2, :].reshape(seq_here, LEN, heads_here, HD)
    far_keys = prompt_kv[:, :, :head_cols].reshape(seq_here, PMAX, heads_here, HD)
    far_values = prompt_kv[:, :, head_cols:].reshape(seq_here, PMAX, heads_here, HD)
    attended, log_total = lax.map(
        attend, (queries, own_keys, own_values, far_keys, far_values, far_valid)
    )
    attn_flat = attended.reshape(block_tokens, head_cols)
    middle = inputs + lax.psum_scatter(
        jnp.dot(attn_flat, w_out, preferred_element_type=jnp.float32).astype(jnp.bfloat16),
        "mp",
        scatter_dimension=0,
        tiled=True,
    ).astype(jnp.float32)
    normed_ffn = adaptive_norm(middle, ada_ffn, code_hot).astype(jnp.bfloat16)
    normed_ffn_full = lax.all_gather(normed_ffn, "mp", axis=0, tiled=True)
    w_up = w_ffn[:, 0, :]
    w_down = w_ffn[:, 1, :]
    up_proj = inner_cols(normed_ffn_full, w_up)
    activated = jax.nn.gelu(up_proj, approximate=False).astype(jnp.bfloat16)
    output = (
        middle
        + lax.psum_scatter(
            jnp.dot(activated, w_down, preferred_element_type=jnp.float32).astype(jnp.bfloat16),
            "mp",
            scatter_dimension=0,
            tiled=True,
        ).astype(jnp.float32)
    ).astype(jnp.bfloat16)
    shard_rows = lax.all_gather(cotangent, "mp", axis=0, tiled=True)
    rows_grad = inner_cols(shard_rows, w_down)
    d_act = rows_grad
    grad_down = inner_rows(activated, shard_rows)
    _, gelu_pull = jax.vjp(lambda values: jax.nn.gelu(values, approximate=False), up_proj)
    d_up = gelu_pull(d_act)[0].astype(jnp.bfloat16)
    d_normed_ffn = lax.psum_scatter(
        jnp.dot(d_up, w_up, preferred_element_type=jnp.float32).astype(jnp.bfloat16),
        "mp",
        scatter_dimension=0,
        tiled=True,
    ).astype(jnp.float32)
    grad_up = inner_rows(d_up, lax.all_gather(normed_ffn, "mp", axis=0, tiled=True))
    _, norm_ffn_pull = jax.vjp(
        lambda values, table: adaptive_norm(values, table, code_hot), middle, ada_ffn
    )
    d_middle_norm, grad_table_ffn = norm_ffn_pull(d_normed_ffn)
    d_middle = cotangent.astype(jnp.float32) + d_middle_norm
    d_branch = d_middle.astype(jnp.bfloat16)
    shard_rows = lax.all_gather(d_branch, "mp", axis=0, tiled=True)
    rows_grad = inner_cols(shard_rows, w_out)
    grad_out_proj = inner_rows(attn_flat, shard_rows)
    d_mixed = rows_grad.astype(jnp.bfloat16).reshape(seq_here, LEN, heads_here, HD)
    d_queries, d_own_keys, d_own_values, d_far_keys, d_far_values = lax.map(
        attend_back,
        (queries, own_keys, own_values, far_keys, far_values, far_valid, log_total, d_mixed),
    )
    prompt_grad = jnp.concatenate(
        [
            d_far_keys.reshape(seq_here, PMAX, head_cols),
            d_far_values.reshape(seq_here, PMAX, head_cols),
        ],
        axis=2,
    )
    row_ids = jnp.arange(lax.axis_size("dp") * seq_here, dtype=jnp.int32)
    picker = (my_partner[:, None] == row_ids[None, :]).astype(jnp.float32)
    returned_kv = lax.psum_scatter(
        jnp.einsum("kr,kpc->rpc", picker, prompt_grad, precision=highest).astype(jnp.bfloat16),
        "dp",
        scatter_dimension=0,
        tiled=True,
    ).astype(jnp.float32)
    d_kv_rows = jnp.concatenate(
        [
            d_own_keys.reshape(seq_here, LEN, head_cols),
            d_own_values.reshape(seq_here, LEN, head_cols),
        ],
        axis=2,
    )
    d_kv_rows = jax.vmap(
        lambda sequence, window, offset: lax.dynamic_update_slice_in_dim(
            sequence, lax.dynamic_slice_in_dim(sequence, offset, PMAX, 0) + window, offset, 0
        )
    )(d_kv_rows, returned_kv, my_starts)
    d_qkv = jnp.stack(
        [
            d_queries.reshape(block_tokens, head_cols),
            d_kv_rows[:, :, :head_cols].reshape(block_tokens, head_cols),
            d_kv_rows[:, :, head_cols:].reshape(block_tokens, head_cols),
        ],
        axis=1,
    ).astype(jnp.bfloat16)
    d_normed_attn = lax.psum_scatter(
        jnp.einsum("tsj,jsd->td", d_qkv, w_qkv, preferred_element_type=jnp.float32).astype(
            jnp.bfloat16
        ),
        "mp",
        scatter_dimension=0,
        tiled=True,
    ).astype(jnp.float32)
    grad_qkv = jnp.einsum(
        "tsj,td->jsd",
        d_qkv,
        lax.all_gather(normed_attn, "mp", axis=0, tiled=True),
        preferred_element_type=jnp.float32,
    )
    _, norm_attn_pull = jax.vjp(
        lambda values, table: adaptive_norm(values, table, code_hot), inputs, ada_attn
    )
    d_inputs_norm, grad_table_attn = norm_attn_pull(d_normed_attn)
    grad_tokens = (d_middle + d_inputs_norm).astype(jnp.bfloat16)
    dp_size = lax.axis_size("dp")
    lane_block = width // dp_size
    if lane_block == 128 and seq_here == 1 and dp_size % 2 == 0 and mp_size == 4:

        def blocks(parts):
            stacked = jnp.concatenate(parts, axis=0).astype(BF16)
            return jnp.swapaxes(stacked.reshape(-1, dp_size, lane_block), 0, 1)

        tables = jnp.concatenate([grad_table_attn, grad_table_ffn], axis=0)
        tables = jnp.swapaxes(tables.reshape(-1, dp_size, lane_block), 0, 1)
        grad_attn, grad_ffn, tables = reduce_grads(
            blocks([grad_qkv[:, 0], grad_qkv[:, 1], grad_qkv[:, 2], grad_out_proj]),
            blocks([grad_up, grad_down]),
            tables,
            dp_size,
        )
        grad_attn = grad_attn.reshape(w_attn.shape[0], 4, lane_block)
        grad_ffn = grad_ffn.reshape(w_ffn.shape[0], 2, lane_block)
        tables = lax.psum_scatter(
            tables.reshape(2, ada_attn.shape[0], 2, lane_block),
            "mp",
            scatter_dimension=3,
            tiled=True,
        )
        return (output, grad_tokens, grad_attn, grad_ffn, tables[0], tables[1])
    grad_attn_local = jnp.concatenate([grad_qkv, grad_out_proj[:, None, :]], axis=1)
    grad_ffn_local = jnp.stack([grad_up, grad_down], axis=1)
    grad_attn, grad_ffn = (
        lax.psum_scatter(
            grad_attn_local.astype(jnp.bfloat16), "dp", scatter_dimension=2, tiled=True
        ).astype(jnp.float32),
        lax.psum_scatter(
            grad_ffn_local.astype(jnp.bfloat16), "dp", scatter_dimension=2, tiled=True
        ).astype(jnp.float32),
    )
    grad_ada_attn, grad_ada_ffn = (
        lax.psum_scatter(grad_table_attn, ("dp", "mp"), scatter_dimension=2, tiled=True),
        lax.psum_scatter(grad_table_ffn, ("dp", "mp"), scatter_dimension=2, tiled=True),
    )
    return (output, grad_tokens, grad_attn, grad_ffn, grad_ada_attn, grad_ada_ffn)


def solution(mesh):
    in_specs = (
        P(("dp", "mp"), None),
        P("mp", None, None),
        P("mp", None, None),
        P(),
        P(),
        P(),
        P(),
        P(),
        P(),
        P(),
        P(("dp", "mp"), None),
    )
    out_specs = (
        P(("dp", "mp"), None),
        P(("dp", "mp"), None),
        P("mp", None, "dp"),
        P("mp", None, "dp"),
        P(None, None, ("dp", "mp")),
        P(None, None, ("dp", "mp")),
    )
    return jax.shard_map(shards, mesh=mesh, in_specs=in_specs, out_specs=out_specs, check_vma=False)
```

```python
import collections
import functools

import jax
import jax.numpy as jnp
from jax import lax
from jax.experimental import pallas as pl
from jax.experimental.pallas import tpu as pltpu
from jax.sharding import PartitionSpec as P

HD = 64
LEN = 1024
PMAX = 256


epsilon = 1e-05
highest = lax.Precision.HIGHEST


def partner_rows(group_sizes, partner_pick):
    group_end = jnp.cumsum(group_sizes)
    begins = group_end - group_sizes
    row_ids = jnp.arange(partner_pick.shape[0], dtype=jnp.int32)
    owner_group = jnp.sum((group_end[None, :] <= row_ids[:, None]).astype(jnp.int32), axis=1)
    member = (
        owner_group[:, None] == jnp.arange(group_sizes.shape[0], dtype=jnp.int32)[None, :]
    ).astype(jnp.int32)
    first_row = jnp.sum(member * begins[None, :], axis=1)
    group_len = jnp.sum(member * group_sizes[None, :], axis=1)
    span_size = jnp.maximum(group_len - 1, 1)
    return first_row + (row_ids - first_row + 1 + partner_pick % span_size) % group_len


def adaptive_norm(inputs, table, code_hot):
    coefficients = jnp.dot(code_hot, table.reshape(table.shape[0], -1), precision=highest)
    coefficients = coefficients.reshape(inputs.shape[0], 2, inputs.shape[1])
    center = inputs - jnp.mean(inputs, axis=-1, keepdims=True)
    spread = jnp.mean(center * center, axis=-1, keepdims=True)
    normed = center * lax.rsqrt(spread + epsilon)
    return (1.0 + coefficients[:, 0, :]) * normed + coefficients[:, 1, :]


def inner_rows(left, right):
    return lax.dot_general(
        left, right, (((0,), (0,)), ((), ())), preferred_element_type=jnp.float32
    )


def inner_cols(left, right):
    return lax.dot_general(
        left, right, (((1,), (1,)), ((), ())), preferred_element_type=jnp.float32
    )


def row_scores(queries, key_rows, far_valid):
    key_mask = jnp.concatenate([jnp.ones((queries.shape[0],), dtype=jnp.bool_), far_valid])
    scores = jnp.einsum(
        "qhd,khd->hqk", queries, key_rows, preferred_element_type=jnp.float32
    ) * HD ** (-0.5)
    return jnp.where(key_mask[None, None, :], scores, -1000000000.0)


def attend(packed):
    queries, own_keys, own_values, far_keys, far_values, far_valid = packed
    key_rows = jnp.concatenate([own_keys, far_keys], axis=0)
    value_rows = jnp.concatenate([own_values, far_values], axis=0)
    scores = row_scores(queries, key_rows, far_valid)
    row_max = jnp.max(scores, axis=-1, keepdims=True)
    log_total = row_max + jnp.log(jnp.sum(jnp.exp(scores - row_max), axis=-1, keepdims=True))
    prob_low = jnp.exp(scores - log_total).astype(jnp.bfloat16)
    mixed = jnp.einsum("hqk,khd->qhd", prob_low, value_rows, preferred_element_type=jnp.float32)
    return (mixed.astype(jnp.bfloat16), log_total)


def attend_back(packed):
    queries, own_keys, own_values, far_keys, far_values, far_valid, log_total, d_mixed = packed
    key_rows = jnp.concatenate([own_keys, far_keys], axis=0)
    value_rows = jnp.concatenate([own_values, far_values], axis=0)
    scores = row_scores(queries, key_rows, far_valid)
    attn_prob = jnp.exp(scores - log_total)
    prob_low = attn_prob.astype(jnp.bfloat16)
    d_values = jnp.einsum("hqk,qhd->khd", prob_low, d_mixed, preferred_element_type=jnp.float32)
    d_prob = jnp.einsum("qhd,khd->hqk", d_mixed, value_rows, preferred_element_type=jnp.float32)
    row_delta = jnp.sum(attn_prob * d_prob, axis=-1, keepdims=True)
    d_scores = (attn_prob * (d_prob - row_delta)).astype(jnp.bfloat16)
    d_queries = jnp.einsum(
        "hqk,khd->qhd", d_scores, key_rows, preferred_element_type=jnp.float32
    ) * HD ** (-0.5)
    d_keys = jnp.einsum(
        "hqk,qhd->khd", d_scores, queries, preferred_element_type=jnp.float32
    ) * HD ** (-0.5)
    own_len = queries.shape[0]
    return (d_queries, d_keys[:own_len], d_values[:own_len], d_keys[own_len:], d_values[own_len:])


MESH = pl.DeviceIdType.MESH
F32 = jnp.float32
BF16 = jnp.bfloat16
LANES = 128


def dot(left, right, left_dim=1, right_dim=0):
    return lax.dot_general(
        left, right, (((left_dim,), (right_dim,)), ((), ())), preferred_element_type=F32
    )


class Links:
    def __init__(self, z_size, send_sem, recv_sem):
        self.dp = lax.axis_index("dp")
        self.mp = lax.axis_index("mp")
        self.z_size = z_size
        self.y = lax.rem(self.dp, 2)
        self.z = self.dp // 2
        self.core = lax.rem(self.mp, 2)
        self.x = self.mp // 2
        self.sib = (self.dp, self.mp + 1 - 2 * self.core)
        self.xpeer = (self.dp, self.mp + 2 - 4 * self.x)
        self.ypeer = (self.dp + 1 - 2 * self.y, self.mp)
        self.right = (self.dp + 2, self.mp)
        self.left = (self.dp - 2, self.mp)
        self.send_sem = send_sem
        self.recv_sem = recv_sem
        self.used = 0
        self.sent = []
        self.pair_sends = {}

    def take(self, count=1):
        first = self.used
        self.used += count
        return first

    def copy(self, src, dst, number, device):
        return pltpu.make_async_remote_copy(
            src_ref=src,
            dst_ref=dst,
            send_sem=self.send_sem.at[number],
            recv_sem=self.recv_sem.at[number],
            device_id=device,
            device_id_type=MESH,
        )

    def swap(self, src, dst, device):
        made = self.copy(src, dst, self.take(), device)
        self.sent.append(made)
        return made

    def finish(self, made=None):
        for one in list(self.sent):
            if made is None or one is made:
                one.wait_send()
        self.sent = [one for one in self.sent if made is not None and one is not made]

    def barrier(self):
        bar = pltpu.get_barrier_semaphore()
        for device in (self.sib, self.xpeer, self.ypeer):
            pl.semaphore_signal(bar, inc=1, device_id=device, device_id_type=MESH)

        @pl.when(self.z > 0)
        def _():
            pl.semaphore_signal(bar, inc=1, device_id=self.left, device_id_type=MESH)

        @pl.when(self.z < self.z_size - 1)
        def _():
            pl.semaphore_signal(bar, inc=1, device_id=self.right, device_id_type=MESH)

        inner = (self.z > 0).astype(jnp.int32) + (self.z < self.z_size - 1).astype(jnp.int32)
        pl.semaphore_wait(bar, 3 + inner)


class LineReduce:
    def __init__(self, links, held, passing):
        self.setup(links, held, passing)

    def setup(self, links, held, passing):
        self.k = links
        self.held, self.passing = held, passing
        self.nr = links.take(links.z_size)
        self.nl = links.take(links.z_size)

    def order(self):
        n = self.k.z_size
        return [n - 1, 0] + list(range(1, n - 1))

    def z_copy(self, d, rightward):
        k = self.k
        if rightward:
            return k.copy(self.held.at[d], self.passing.at[d], self.nr + d, k.right)
        slot = jnp.where(k.z - 1 == d, k.z_size, d)
        return k.copy(self.held.at[d], self.passing.at[slot], self.nl + d, k.left)

    def add(self, d):
        total = self.held[d].astype(F32) + self.passing[d].astype(F32)
        self.held[d] = total.astype(self.held.dtype)

    def move(self, d):
        k = self.k

        @pl.when(k.z < d)
        def _():
            @pl.when(k.z > 0)
            def _():
                self.z_copy(d, True).wait_recv()
                self.add(d)

            self.z_copy(d, True).start()

        @pl.when(k.z > d)
        def _():
            @pl.when(k.z < k.z_size - 1)
            def _():
                self.z_copy(d, False).wait_recv()
                self.add(d)

            self.z_copy(d, False).start()

    def finish(self, store):
        k = self.k
        n = k.z_size

        @pl.when(k.z > 0)
        def _():
            k.copy(self.held.at[k.z], self.passing.at[k.z], self.nr + k.z, k.left).wait_recv()

        @pl.when(k.z < n - 1)
        def _():
            k.copy(self.held.at[k.z], self.passing.at[n], self.nl + k.z, k.right).wait_recv()

        total = self.held[k.z].astype(F32)
        from_left = jnp.where(k.z > 0, self.passing[k.z].astype(F32), 0.0)
        from_right = jnp.where(k.z < n - 1, self.passing[n].astype(F32), 0.0)
        store(total + from_left + from_right)

    def wait_sends(self):
        k = self.k
        for d in range(k.z_size):

            @pl.when(k.z < d)
            def _(d=d):
                self.z_copy(d, True).wait_send()

            @pl.when(k.z > d)
            def _(d=d):
                self.z_copy(d, False).wait_send()


class GridReduce(LineReduce):
    def __init__(self, links, local, held, passing):
        self.setup(links, held, passing)
        self.local = local
        self.ny = links.take(links.z_size)

    def y_copy(self, d):
        k = self.k
        other = 2 * d + 1 - k.y
        return k.copy(self.local.at[other], self.held.at[d], self.ny + d, k.ypeer)

    def send_y(self):
        for d in self.order():
            self.y_copy(d).start()

    def merge_y(self, d):
        self.y_copy(d).wait_recv()
        total = self.local[2 * d + self.k.y].astype(F32) + self.held[d].astype(F32)
        self.held[d] = total.astype(self.held.dtype)

    def serve(self):
        for d in self.order():
            self.merge_y(d)
            self.move(d)

    def wait_y(self):
        for d in range(self.k.z_size):
            self.y_copy(d).wait_send()


class LineGather:
    def __init__(self, links, slots):
        self.k = links
        self.slots = slots
        self.nr = links.take(links.z_size)
        self.nl = links.take(links.z_size)

    def z_copy(self, slot, rightward):
        k = self.k
        number = (self.nr if rightward else self.nl) + slot
        place = self.slots.at[slot]
        return k.copy(place, place, number, k.right if rightward else k.left)

    def start(self):
        k = self.k

        @pl.when(k.z < k.z_size - 1)
        def _():
            self.z_copy(k.z, True).start()

        @pl.when(k.z > 0)
        def _():
            self.z_copy(k.z, False).start()

    def serve(self, distance):
        k = self.k

        @pl.when(k.z >= distance)
        def _():
            self.z_copy(k.z - distance, True).wait_recv()

            @pl.when(k.z < k.z_size - 1)
            def _():
                self.z_copy(k.z - distance, True).start()

        @pl.when(k.z + distance < k.z_size)
        def _():
            self.z_copy(k.z + distance, False).wait_recv()

            @pl.when(k.z > 0)
            def _():
                self.z_copy(k.z + distance, False).start()

    def wait_sends(self):
        k = self.k
        for slot in range(k.z_size):

            @pl.when(jnp.logical_and(k.z >= slot, k.z < k.z_size - 1))
            def _(slot=slot):
                self.z_copy(slot, True).wait_send()

            @pl.when(jnp.logical_and(k.z <= slot, k.z > 0))
            def _(slot=slot):
                self.z_copy(slot, False).wait_send()


class Exchange:
    def __init__(self, links, pair_out, pair_in, x_out, x_in):
        self.k = links
        self.pair_out, self.pair_in, self.x_out, self.x_in = pair_out, pair_in, x_out, x_in
        self.pair = {}
        self.along_x = {}

    def give(self, r, term, slot=None):
        slot = r if slot is None else slot
        if slot in self.k.pair_sends:
            self.k.finish(self.k.pair_sends[slot])
        self.pair_out[slot] = term.astype(BF16)
        made = self.k.swap(self.pair_out.at[slot], self.pair_in.at[slot], self.k.sib)
        made.start()
        self.k.pair_sends[slot] = made
        self.pair[r] = (made, slot)

    def pair_sum(self, r, term):
        made, slot = self.pair[r]
        made.wait_recv()
        return term + self.pair_in[slot].astype(F32)

    def send_x(self, r, total):
        self.x_out[r] = total.astype(BF16)
        made = self.k.swap(self.x_out.at[r], self.x_in.at[r], self.k.xpeer)
        made.start()
        self.along_x[r] = made

    def total(self, r):
        self.along_x[r].wait_recv()
        return self.x_out[r].astype(F32) + self.x_in[r].astype(F32)


class Settle:
    def __init__(self, exchange, shards, x_out, x_in, term):
        k = exchange.k
        own, sib, across, diag = shards
        exchange.give(2, term(diag), 0)
        x_out[...] = exchange.pair_sum(2, term(across)).astype(BF16)
        self.along_x = k.swap(x_out, x_in, k.xpeer)
        self.along_x.start()
        self.x_in = x_in
        exchange.give(3, term(sib), 1)
        self.kept = exchange.pair_sum(3, term(own))

    def total(self, kept):
        self.along_x.wait_recv()
        return kept + self.x_in[...].astype(F32)


def normalize(values):
    center = values - jnp.mean(values, axis=1, keepdims=True)
    spread = jnp.mean(center * center, axis=1, keepdims=True)
    scale = lax.rsqrt(spread + epsilon)
    return center * scale, scale


def norm_back(values, table, d_normed):
    normed, scale = normalize(values)
    dz = (1.0 + table[0:1, :]) * d_normed
    both = jnp.mean(dz * normed, axis=1, keepdims=True)
    d_values = (dz - jnp.mean(dz, axis=1, keepdims=True) - normed * both) * scale
    d_gain = jnp.sum(d_normed * normed, axis=0, keepdims=True)
    d_shift = jnp.sum(d_normed, axis=0, keepdims=True)
    return d_values, d_gain, d_shift


def layer_kernel(names, z_size, *refs):
    held = dict(zip(names, refs))
    held.update(
        d_mixed=held["act"],
        d_query=held["mixed"],
        d_branch=held["normed_ffn"],
        far_held=held["windows"],
        d_query_low=held["attn_t"],
        d_keys_low=held["keys_t"],
        d_values_low=held["values_t"],
        g_attn=held["g_down"],
    )
    n = collections.namedtuple("Buffers", held)(**held)
    k = Links(z_size, n.send_sem, n.recv_sem)
    mp_size, block, width = n.normed.shape
    seq = mp_size * block
    heads_wide = n.wa.shape[1]
    hidden = n.wf.shape[1]
    heads = heads_wide // HD
    q_wide = heads * block
    tile = block
    far = mp_size
    own_shard = 2 * k.x + k.core
    sib_shard = 2 * k.x + 1 - k.core
    x_shard = 2 * (1 - k.x) + k.core
    diag_shard = 2 * (1 - k.x) + 1 - k.core
    shards = (own_shard, sib_shard, x_shard, diag_shard)

    def mine(r):
        return 2 * r + k.core

    def theirs(r):
        return 2 * r + 1 - k.core

    def span(i, size=tile):
        return pl.ds(pl.multiple_of(i * size, size), size)

    fetches = []

    def fetch(src, dst):
        made = pltpu.make_async_copy(src, dst, n.load_sem.at[len(fetches)])
        made.start()
        fetches.append(made)
        return made

    load_tokens = fetch(n.tokens, n.raw.at[k.x])
    load_wa = fetch(n.w_attn, n.wa)
    load_cot = fetch(n.cotangent, n.cot.at[own_shard])
    load_wf = fetch(n.w_ffn, n.wf)

    def partner_of(row):
        begin, first, count = 0, 0, 1
        for g in range(n.group_sizes.shape[0]):
            size = n.group_sizes[g]
            inside = jnp.logical_and(row >= begin, row < begin + size)
            first = jnp.where(inside, begin, first)
            count = jnp.where(inside, size, count)
            begin = begin + size
        step = lax.rem(n.partner_pick[row], jnp.maximum(count - 1, 1))
        return jnp.clip(first + lax.rem(row - first + 1 + step, count), 0, 2 * z_size - 1)

    k.barrier()
    send_tokens = k.swap(n.tokens, n.raw.at[k.x], k.xpeer)
    send_tokens.start()
    cot_x = k.swap(n.cotangent, n.cot.at[own_shard], k.xpeer)
    cot_x.start()
    cot_sib = k.swap(n.cotangent, n.cot.at[own_shard], k.sib)
    cot_sib.start()

    code = n.codebook[k.dp]
    start = n.prompt_start[k.dp]
    partner = partner_of(k.dp)
    other_partner = partner_of(k.dp + 1 - 2 * k.y)
    part_z, part_y = partner // 2, lax.rem(partner, 2)
    other_z, other_y = other_partner // 2, lax.rem(other_partner, 2)
    far_len = n.prompt_len[partner]
    table_attn = n.ada_attn[code]
    table_ffn = n.ada_ffn[code]

    def adapt(normed, table):
        return ((1.0 + table[0:1, :]) * normed + table[1:2, :]).astype(BF16)

    def project(s):
        normed = n.normed[s]
        query = (dot(normed, n.wa[0], 1, 1) * HD ** (-0.5)).astype(BF16)
        lane = lax.broadcasted_iota(jnp.int32, (block, heads_wide), 1) // HD
        for h in range(heads):
            n.q4[s, h * block : (h + 1) * block, :] = jnp.where(lane == h, query, 0).astype(BF16)
        for ref, turned, w in ((n.keys, n.keys_t, 1), (n.values, n.values_t, 2)):
            made = dot(normed, n.wa[w], 1, 1)
            ref[s] = made.astype(BF16)
            turned[s] = made.T.astype(BF16)

    load_tokens.wait()
    n.normed[own_shard] = adapt(normalize(n.raw[k.x].astype(F32))[0], table_attn)
    normed_own = k.swap(n.normed.at[own_shard], n.normed.at[own_shard], k.sib)
    normed_own.start()
    load_wa.wait()
    normed_own.wait_recv()

    def project_pair(first):
        def body(i, carry):
            project(first + i)
            return carry

        lax.fori_loop(0, 2, body, 0)

    project_pair(2 * k.x)
    send_tokens.wait_recv()
    n.normed[x_shard] = adapt(normalize(n.raw[1 - k.x].astype(F32))[0], table_attn)
    normed_x = k.swap(n.normed.at[x_shard], n.normed.at[x_shard], k.sib)
    normed_x.start()
    normed_x.wait_recv()
    project_pair(2 * (1 - k.x))

    all_keys = n.keys[0:mp_size].reshape(seq, heads_wide)
    all_values = n.values[0:mp_size].reshape(seq, heads_wide)
    from_row = lax.broadcasted_iota(jnp.int32, (block, seq), 1)
    to_row = lax.broadcasted_iota(jnp.int32, (block, seq), 0)
    window = (from_row == to_row + start).astype(F32).astype(BF16)
    n.windows[k.z, 0:block] = dot(window, all_keys).astype(BF16)
    n.windows[k.z, block : 2 * block] = dot(window, all_values).astype(BF16)
    gather = LineGather(k, n.windows)
    gather.start()

    def attend_own(s, carry):
        q4 = n.q4[s]
        top = jnp.full((1, q_wide), -jnp.inf, F32)
        for c in range(mp_size):
            scores = dot(n.keys[c], q4, 1, 1)
            n.wide[c] = scores
            top = jnp.maximum(top, jnp.max(scores, axis=0, keepdims=True))
        total = jnp.zeros((1, q_wide), F32)
        for c in range(mp_size):
            prob = jnp.exp(n.wide[c] - top)
            total = total + jnp.sum(prob, axis=0, keepdims=True)
            low = prob.astype(BF16)
            for h in range(heads):
                rows = slice(h * HD, (h + 1) * HD)
                part = dot(n.values_t[c, rows, :], low[:, h * block : (h + 1) * block])
                n.mixed[s, rows, :] = part if c == 0 else n.mixed[s, rows, :] + part
        n.top[s] = top
        n.total[s] = total
        return carry

    for s in range(mp_size):
        attend_own_s = functools.partial(attend_own)
        lax.fori_loop(s, s + 1, attend_own_s, 0)
        if 0 < s < z_size:
            gather.serve(s)
    for distance in range(mp_size, z_size):
        gather.serve(distance)

    n.y_out[...] = n.windows[other_z]
    y_window = k.swap(n.y_out, n.y_in, k.ypeer)
    y_window.start()
    cot_x.wait_recv()
    cot_pass = k.swap(n.cot.at[x_shard], n.cot.at[x_shard], k.sib)
    cot_pass.start()
    y_window.wait_recv()
    same_y = part_y == k.y
    far_kv = jnp.where(same_y, n.windows[part_z].astype(F32), n.y_in[...].astype(F32))
    n.keys[far] = far_kv[0:block].astype(BF16)
    n.values[far] = far_kv[block:].astype(BF16)
    n.keys_t[far] = far_kv[0:block].T.astype(BF16)
    n.values_t[far] = far_kv[block:].T.astype(BF16)

    def attend_far(s):
        scores = dot(n.keys[far], n.q4[s], 1, 1)
        slot = lax.broadcasted_iota(jnp.int32, scores.shape, 0)
        scores = jnp.where(slot < far_len, scores, -1000000000.0)
        top = jnp.maximum(n.top[s], jnp.max(scores, axis=0, keepdims=True))
        scale = jnp.exp(n.top[s] - top)
        prob = jnp.exp(scores - top)
        total = n.total[s] * scale + jnp.sum(prob, axis=0, keepdims=True)
        low = prob.astype(BF16)
        for h in range(heads):
            rows = slice(h * HD, (h + 1) * HD)
            cols = slice(h * block, (h + 1) * block)
            part = n.mixed[s, rows, :] * scale[:, cols] + dot(n.values_t[far, rows, :], low[:, cols])
            n.attn_t[s, rows, :] = (part / total[:, cols]).astype(BF16)
        n.log_total[s] = top + jnp.log(total)

    def out_part(s):
        attend_far(s)
        return dot(n.attn_t[s], n.wa[3], 0, 0)

    branch = Exchange(k, n.pair_out, n.pair_in, n.x_out, n.x_in)
    for r in range(2):
        branch.give(r, out_part(theirs(r)))
        branch.send_x(r, branch.pair_sum(r, out_part(mine(r))))

    back = Exchange(k, n.pair_out, n.pair_in, n.x_out2, n.x_in2)
    load_cot.wait()
    load_wf.wait()
    cot_sib.wait_recv()
    cot_pass.wait_recv()

    def hidden_part(s):
        normed = n.normed_ffn[s]
        cot = n.cot[s]

        def body(i, carry):
            cols = span(i)
            up = dot(normed, n.wf[0, cols, :], 1, 1)
            d_act = dot(cot, n.wf[1, cols, :], 1, 1)
            cdf = 0.5 + 0.5 * lax.erf(up * (0.5**0.5))
            n.act[s, :, cols] = (up * cdf).astype(BF16)
            slope = cdf + up * (jnp.exp(-0.5 * up * up) * (2.0 * jnp.pi) ** (-0.5))
            n.d_up[s, :, cols] = (slope * d_act).astype(BF16)
            return carry

        lax.fori_loop(0, hidden // tile, body, 0)
        return dot(n.d_up[s], n.wf[0])

    for r in range(2):
        middle = n.raw[r].astype(F32) + branch.total(r)
        n.wide[r] = middle
        n.normed_ffn[mine(r)] = adapt(normalize(middle)[0], table_ffn)
        share = k.swap(n.normed_ffn.at[mine(r)], n.normed_ffn.at[mine(r)], k.sib)
        share.start()
        share.wait_recv()
        back.give(r, hidden_part(theirs(r)))
        back.send_x(r, back.pair_sum(r, hidden_part(mine(r))))

    grid_down = GridReduce(k, n.g_down, n.h_down, n.p_down)
    grid_up = GridReduce(k, n.g_up, n.h_up, n.p_up)

    def spread(target, rows, made):
        for d in range(target.shape[0]):
            target[d, rows, :] = made[:, d * LANES : (d + 1) * LANES].astype(BF16)

    def ffn_grads(target, left, right):
        def body(i, carry):
            lhs = left[:, :, span(i)].reshape(seq, tile)
            spread(target, span(i), dot(lhs, right[...].reshape(seq, width), 0, 0))
            return carry

        lax.fori_loop(0, hidden // tile, body, 0)

    ffn_grads(n.g_down, n.act, n.cot)
    grid_down.send_y()
    ffn_grads(n.g_up, n.d_up, n.normed_ffn)
    grid_up.send_y()

    def down_part(s):
        return dot(n.act[s], n.wf[1])

    k.finish()
    out_sum = Settle(branch, shards, n.x_out.at[0], n.s_in, down_part)
    n.kept[...] = out_sum.kept

    n.d_keys[...] = jnp.zeros_like(n.d_keys)
    n.d_values[...] = jnp.zeros_like(n.d_values)
    table_grad = [jnp.zeros((1, width), F32), jnp.zeros((1, width), F32)]

    def prepare(s):
        d_attn_t = dot(n.wa[3], n.d_branch[s], 1, 1).astype(BF16)
        row = lax.broadcasted_iota(jnp.int32, (heads_wide, block), 0) // HD
        product = d_attn_t.astype(F32) * n.attn_t[s].astype(F32)
        for h in range(heads):
            rows = slice(h * HD, (h + 1) * HD)
            cols = slice(h * block, (h + 1) * block)
            n.delta[s, :, cols] = jnp.sum(product[rows], axis=0, keepdims=True)
            n.d_mixed[s, :, cols] = jnp.where(row == h, d_attn_t, 0).astype(BF16)

    def attend_back(s, first, last):
        q4 = n.q4[s]
        d_mixed = n.d_mixed[s]

        def body(c, carry):
            scores = dot(n.keys[c], q4, 1, 1)
            slot = lax.broadcasted_iota(jnp.int32, scores.shape, 0)
            limit = jnp.where(c == far, far_len, block)
            prob = jnp.where(slot < limit, jnp.exp(scores - n.log_total[s]), 0.0)
            low = prob.astype(BF16)
            d_prob = dot(n.values[c], d_mixed)
            d_scores = (prob * (d_prob - n.delta[s])).astype(BF16)
            n.d_values[c] += dot(low, d_mixed, 1, 1)
            n.d_keys[c] += dot(d_scores, q4)
            for h in range(heads):
                rows = slice(h * HD, (h + 1) * HD)
                n.d_query[s, rows, :] += dot(
                    n.keys_t[c, rows, :], d_scores[:, h * block : (h + 1) * block]
                )
            return carry

        lax.fori_loop(first, last, body, 0)

    n.d_query[...] = jnp.zeros_like(n.d_query)
    for r in range(2):
        d_values, d_gain, d_shift = norm_back(n.wide[r], table_ffn, back.total(r))
        table_grad[0] = table_grad[0] + d_gain
        table_grad[1] = table_grad[1] + d_shift
        d_middle = n.cot[mine(r)].astype(F32) + d_values
        n.wide[2 + r] = d_middle
        n.d_branch[mine(r)] = d_middle.astype(BF16)
        share = k.swap(n.d_branch.at[mine(r)], n.d_branch.at[mine(r)], k.sib)
        share.start()
        share.wait_recv()

        def both(i, carry, r=r):
            prepare(2 * r + i)
            attend_back(2 * r + i, far, far + 1)
            return carry

        lax.fori_loop(0, 2, both, 0)
        if r == 0:

            def rest(i, carry, r=r):
                attend_back(2 * r + i, 0, mp_size)
                return carry

            lax.fori_loop(0, 2, rest, 0)
            grid_down.serve()
            grid_down.wait_y()

    def table_blocks(target, gain, shift):
        row = lax.broadcasted_iota(jnp.int32, (n.t_ffn.shape[1], width), 0)
        both = jnp.where(lax.rem(row, 2) == 0, gain, shift)
        both = jnp.where(row // 2 == code, both, 0.0)
        for d in range(target.shape[0]):
            target[d] = both[:, d * LANES : (d + 1) * LANES]

    far_grad = jnp.concatenate([n.d_keys[far], n.d_values[far]], axis=0)
    n.y_out2[...] = jnp.where(same_y, 0.0, far_grad).astype(BF16)
    y_grads = k.swap(n.y_out2, n.y_in2, k.ypeer)
    y_grads.start()
    table_blocks(n.t_ffn, table_grad[0], table_grad[1])
    grid_t_ffn = GridReduce(k, n.t_ffn, n.ht_ffn, n.pt_ffn)
    grid_t_ffn.send_y()
    gather.wait_sends()
    line = LineReduce(k, n.far_held, n.far_passing)

    def rest_last(i, carry):
        attend_back(2 + i, 0, mp_size)
        return carry

    lax.fori_loop(0, 1, rest_last, 0)
    y_grads.wait_recv()
    back_grad = n.y_in2[...].astype(F32)
    for d in line.order():
        here = jnp.where(jnp.logical_and(same_y, part_z == d), far_grad, 0.0)
        there = jnp.where(jnp.logical_and(other_y == k.y, other_z == d), back_grad, 0.0)
        n.far_held[d] = (here + there).astype(BF16)
        line.move(d)
    lax.fori_loop(1, 2, rest_last, 0)
    grid_up.serve()

    grid_attn = GridReduce(k, n.g_attn, n.h_attn, n.p_attn)

    def add_products(left, right):
        total = dot(left[0], right[0])
        for s in range(1, mp_size):
            total = total + dot(left[s], right[s])
        return total

    spread(n.g_attn, slice(3 * heads_wide, 4 * heads_wide), add_products(n.attn_t, n.d_branch))
    for s in range(mp_size):
        n.d_query_low[s] = (n.d_query[s] * HD ** (-0.5)).astype(BF16)
    spread(n.g_attn, slice(0, heads_wide), add_products(n.d_query_low, n.normed))
    grid_t_ffn.serve()

    def take_back(total):
        n.far_sum[...] = total.astype(BF16)

    line.finish(take_back)
    from_slot = lax.broadcasted_iota(jnp.int32, (seq, block), 1)
    to_frame = lax.broadcasted_iota(jnp.int32, (seq, block), 0)
    unwindow = (to_frame == from_slot + start).astype(F32).astype(BF16)
    for ref, low, rows in (
        (n.d_keys, n.d_keys_low, slice(0, block)),
        (n.d_values, n.d_values_low, slice(block, 2 * block)),
    ):
        own = ref[0:mp_size].reshape(seq, heads_wide)
        total = own + dot(unwindow, n.far_sum[rows, :])
        low[0:mp_size] = total.astype(BF16).reshape(mp_size, block, heads_wide)

    flat_normed = n.normed[...].reshape(seq, width)
    for w, low in ((1, n.d_keys_low), (2, n.d_values_low)):
        made = dot(low[0:mp_size].reshape(seq, heads_wide), flat_normed, 0, 0)
        spread(n.g_attn, slice(w * heads_wide, (w + 1) * heads_wide), made)
    grid_attn.send_y()

    def input_part(s):
        return (
            dot(n.d_query_low[s], n.wa[0], 0, 0)
            + dot(n.d_keys_low[s], n.wa[1])
            + dot(n.d_values_low[s], n.wa[2])
        )

    k.finish()
    n.output[...] = (n.wide[k.x] + out_sum.total(n.kept[...])).astype(BF16)
    in_sum = Settle(back, shards, n.x_out2.at[0], n.x_in.at[0], input_part)
    n.kept[...] = in_sum.kept

    quarter = heads_wide

    def store_ffn(s):
        def store(total):
            n.grad_ffn[pl.ds(s, hidden, stride=2), :] = total

        return store

    def store_attn(total):
        for s in range(4):
            n.grad_attn[pl.ds(s, quarter, stride=4), :] = total[s * quarter : (s + 1) * quarter]

    d_values, d_gain, d_shift = norm_back(n.raw[k.x].astype(F32), table_attn, in_sum.total(n.kept[...]))
    n.grad_tokens[...] = (n.wide[2 + k.x] + d_values).astype(BF16)
    table_blocks(n.t_attn, d_gain, d_shift)
    grid_t_attn = GridReduce(k, n.t_attn, n.ht_attn, n.pt_attn)
    grid_t_attn.send_y()
    grid_attn.serve()
    grid_t_attn.serve()
    grid_down.finish(store_ffn(1))
    grid_up.finish(store_ffn(0))

    def store_table(over_x):
        def store(total):
            n.t_out[over_x, 0] = total
            pair = k.swap(n.t_out.at[over_x, 0], n.t_in.at[over_x, 0], k.sib)
            pair.start()
            pair.wait_recv()
            total = total + n.t_in[over_x, 0]
            if over_x:
                n.t_out[over_x, 1] = total
                along = k.swap(n.t_out.at[over_x, 1], n.t_in.at[over_x, 1], k.xpeer)
                along.start()
                along.wait_recv()
                total = total + n.t_in[over_x, 1]
            piece = LANES // mp_size
            kept = total
            for m in range(1, mp_size):
                turned = pltpu.roll(total, LANES - m * piece, 1)
                kept = jnp.where(k.mp == m, turned, kept)
            n.grad_ada[over_x] = kept

        return store

    grid_t_ffn.finish(store_table(0))
    grid_t_attn.finish(store_table(1))
    grid_attn.finish(store_attn)
    k.finish()
    line.wait_sends()
    for unit in (grid_down, grid_up, grid_attn, grid_t_ffn, grid_t_attn):
        unit.wait_sends()
        if unit is not grid_down:
            unit.wait_y()


def layer(tokens, cotangent, w_attn, w_ffn, ada_attn, ada_ffn, ints, dp_size, mp_size):
    z_size = dp_size // 2
    block, width = tokens.shape
    heads_wide = w_attn.shape[1]
    hidden = w_ffn.shape[1]
    heads = heads_wide // HD
    table_rows = ada_attn.shape[0] * 2
    lane_block = width // dp_size

    inputs = dict(
        tokens=tokens,
        cotangent=cotangent,
        w_attn=w_attn,
        w_ffn=w_ffn,
        ada_attn=ada_attn,
        ada_ffn=ada_ffn,
        **ints,
    )
    spaces = dict.fromkeys(("tokens", "cotangent", "w_attn", "w_ffn"), pl.ANY)
    spaces.update(dict.fromkeys(ints, pltpu.SMEM))
    outputs = dict(
        output=((block, width), BF16),
        grad_tokens=((block, width), BF16),
        grad_attn=((4 * heads_wide, lane_block), F32),
        grad_ffn=((2 * hidden, lane_block), F32),
        grad_ada=((2, table_rows, lane_block), F32),
    )
    wide = (mp_size, block, width)
    two = (2, block, width)
    square = (mp_size + 1, block, heads_wide)
    attn_rows, window = 4 * heads_wide, 2 * block
    low, full = {}, {}
    for name in ("normed", "cot", "normed_ffn", "act", "d_up"):
        low[name] = wide
    low.update(raw=two, wa=w_attn.shape, wf=w_ffn.shape)
    for name in ("keys", "values", "keys_t", "values_t"):
        low[name] = square
    low.update(q4=(mp_size, heads * block, heads_wide), attn_t=(mp_size, heads_wide, block))
    for name in ("pair_out", "pair_in", "x_out", "x_in", "x_out2", "x_in2"):
        low[name] = two
    low.update(s_in=(block, width), windows=(z_size, window, heads_wide))
    low.update(far_passing=(z_size + 1, window, heads_wide), far_sum=(window, heads_wide))
    for name in ("y_out", "y_in", "y_out2", "y_in2"):
        low[name] = (window, heads_wide)
    for name, rows in (("up", hidden), ("down", hidden), ("attn", attn_rows)):
        if name != "attn":
            low["g_" + name] = (dp_size, rows, lane_block)
        low["h_" + name] = (z_size, rows, lane_block)
        low["p_" + name] = (z_size + 1, rows, lane_block)
    for name in ("_ffn", "_attn"):
        full["t" + name] = (dp_size, table_rows, lane_block)
        full["ht" + name] = (z_size, table_rows, lane_block)
        full["pt" + name] = (z_size + 1, table_rows, lane_block)
    full.update(t_out=(2, 2, table_rows, lane_block), t_in=(2, 2, table_rows, lane_block))
    full.update(wide=(mp_size, block, heads * block), kept=(block, width))
    for name in ("top", "total", "log_total", "delta"):
        full[name] = (mp_size, 1, heads * block)
    full.update(mixed=(mp_size, heads_wide, block))
    full.update(d_keys=square, d_values=square)
    scratch = {name: pltpu.VMEM(shape, BF16) for name, shape in low.items()}
    scratch.update({name: pltpu.VMEM(shape, F32) for name, shape in full.items()})
    copies = 160
    scratch.update(
        load_sem=pltpu.SemaphoreType.DMA((4,)),
        send_sem=pltpu.SemaphoreType.DMA((copies,)),
        recv_sem=pltpu.SemaphoreType.DMA((copies,)),
    )
    names = tuple(inputs) + tuple(outputs) + tuple(scratch)
    return pl.pallas_call(
        functools.partial(layer_kernel, names, z_size),
        out_shape=tuple(jax.ShapeDtypeStruct(*shape) for shape in outputs.values()),
        in_specs=[pl.BlockSpec(memory_space=spaces.get(name, pltpu.VMEM)) for name in inputs],
        out_specs=[pl.BlockSpec(memory_space=pltpu.VMEM) for _ in outputs],
        scratch_shapes=list(scratch.values()),
        compiler_params=pltpu.CompilerParams(
            collective_id=1, has_side_effects=True, vmem_limit_bytes=60 << 20
        ),
    )(*inputs.values())


def shards(
    tokens,
    w_attn,
    w_ffn,
    ada_attn,
    ada_ffn,
    codebook,
    group_sizes,
    partner_pick,
    prompt_start,
    prompt_len,
    cotangent,
):
    tok_rows, width = tokens.shape
    mp_size = lax.axis_size("mp")
    dp_index = lax.axis_index("dp")
    mp_index = lax.axis_index("mp")
    block_tokens = tok_rows * mp_size
    seq_here = block_tokens // LEN
    head_cols = w_attn.shape[0]
    heads_here = head_cols // HD
    total_rows = codebook.shape[0]
    dp_size = lax.axis_size("dp")
    fits = width == dp_size * LANES and width == w_ffn.shape[0] == tok_rows * heads_here
    if seq_here == 1 and mp_size == 4 and fits and tok_rows == PMAX:
        ints = dict(
            codebook=codebook,
            group_sizes=group_sizes,
            partner_pick=partner_pick,
            prompt_start=prompt_start,
            prompt_len=prompt_len,
        )
        results = layer(
            tokens,
            cotangent,
            jnp.swapaxes(w_attn, 0, 1),
            jnp.swapaxes(w_ffn, 0, 1),
            ada_attn,
            ada_ffn,
            ints,
            dp_size,
            mp_size,
        )
        output, grad_tokens, grad_attn, grad_ffn, grad_ada = results
        grad_ada = grad_ada[:, :, : width // (dp_size * mp_size)]
        grad_ada = grad_ada.reshape((2,) + ada_attn.shape[:2] + grad_ada.shape[2:])
        return (
            output,
            grad_tokens,
            grad_attn.reshape(head_cols, 4, LANES),
            grad_ffn.reshape(w_ffn.shape[0], 2, LANES),
            grad_ada[1],
            grad_ada[0],
        )
    partner = partner_rows(group_sizes, partner_pick)
    first_row = dp_index * seq_here
    tok_global = (dp_index * mp_size + mp_index) * tok_rows + jnp.arange(tok_rows, dtype=jnp.int32)
    row_pick = (
        (tok_global // LEN)[:, None] == jnp.arange(total_rows, dtype=jnp.int32)[None, :]
    ).astype(jnp.int32)
    token_codes = jnp.sum(row_pick * codebook[None, :], axis=1)
    code_hot = (
        token_codes[:, None] == jnp.arange(ada_attn.shape[0], dtype=jnp.int32)[None, :]
    ).astype(jnp.float32)
    my_partner = lax.dynamic_slice_in_dim(partner, first_row, seq_here)
    my_starts = lax.dynamic_slice_in_dim(prompt_start, first_row, seq_here)
    partner_hot = (my_partner[:, None] == jnp.arange(total_rows, dtype=jnp.int32)[None, :]).astype(
        jnp.int32
    )
    partner_len = jnp.sum(partner_hot * prompt_len[None, :], axis=1)
    far_valid = jnp.arange(PMAX, dtype=jnp.int32)[None, :] < partner_len[:, None]
    inputs = tokens.astype(jnp.float32)
    normed_attn = adaptive_norm(inputs, ada_attn, code_hot).astype(jnp.bfloat16)
    normed_attn_full = lax.all_gather(normed_attn, "mp", axis=0, tiled=True)
    w_qkv = w_attn[:, 0:3, :]
    w_out = w_attn[:, 3, :]
    qkv_low = jnp.einsum(
        "td,jsd->tsj", normed_attn_full, w_qkv, preferred_element_type=jnp.float32
    ).astype(jnp.bfloat16)
    kv_rows = qkv_low[:, 1:3, :].reshape(seq_here, LEN, 2 * head_cols)
    windows = jax.vmap(
        lambda sequence, offset: lax.dynamic_slice_in_dim(sequence, offset, PMAX, 0)
    )(kv_rows, my_starts)
    shard_rows = lax.all_gather(windows, "dp", axis=0, tiled=True)
    row_ids = jnp.arange(shard_rows.shape[0], dtype=jnp.int32)
    picker = (my_partner[:, None] == row_ids[None, :]).astype(jnp.bfloat16)
    prompt_sum = jnp.einsum("kr,rpc->kpc", picker, shard_rows, preferred_element_type=jnp.float32)
    prompt_kv = prompt_sum.astype(jnp.bfloat16)
    queries = qkv_low[:, 0, :].reshape(seq_here, LEN, heads_here, HD)
    own_keys = qkv_low[:, 1, :].reshape(seq_here, LEN, heads_here, HD)
    own_values = qkv_low[:, 2, :].reshape(seq_here, LEN, heads_here, HD)
    far_keys = prompt_kv[:, :, :head_cols].reshape(seq_here, PMAX, heads_here, HD)
    far_values = prompt_kv[:, :, head_cols:].reshape(seq_here, PMAX, heads_here, HD)
    attended, log_total = lax.map(
        attend, (queries, own_keys, own_values, far_keys, far_values, far_valid)
    )
    attn_flat = attended.reshape(block_tokens, head_cols)
    middle = inputs + lax.psum_scatter(
        jnp.dot(attn_flat, w_out, preferred_element_type=jnp.float32).astype(jnp.bfloat16),
        "mp",
        scatter_dimension=0,
        tiled=True,
    ).astype(jnp.float32)
    normed_ffn = adaptive_norm(middle, ada_ffn, code_hot).astype(jnp.bfloat16)
    normed_ffn_full = lax.all_gather(normed_ffn, "mp", axis=0, tiled=True)
    w_up = w_ffn[:, 0, :]
    w_down = w_ffn[:, 1, :]
    up_proj = inner_cols(normed_ffn_full, w_up)
    activated = jax.nn.gelu(up_proj, approximate=False).astype(jnp.bfloat16)
    output = (
        middle
        + lax.psum_scatter(
            jnp.dot(activated, w_down, preferred_element_type=jnp.float32).astype(jnp.bfloat16),
            "mp",
            scatter_dimension=0,
            tiled=True,
        ).astype(jnp.float32)
    ).astype(jnp.bfloat16)
    shard_rows = lax.all_gather(cotangent, "mp", axis=0, tiled=True)
    rows_grad = inner_cols(shard_rows, w_down)
    d_act = rows_grad
    grad_down = inner_rows(activated, shard_rows)
    _, gelu_pull = jax.vjp(lambda values: jax.nn.gelu(values, approximate=False), up_proj)
    d_up = gelu_pull(d_act)[0].astype(jnp.bfloat16)
    d_normed_ffn = lax.psum_scatter(
        jnp.dot(d_up, w_up, preferred_element_type=jnp.float32).astype(jnp.bfloat16),
        "mp",
        scatter_dimension=0,
        tiled=True,
    ).astype(jnp.float32)
    grad_up = inner_rows(d_up, lax.all_gather(normed_ffn, "mp", axis=0, tiled=True))
    _, norm_ffn_pull = jax.vjp(
        lambda values, table: adaptive_norm(values, table, code_hot), middle, ada_ffn
    )
    d_middle_norm, grad_table_ffn = norm_ffn_pull(d_normed_ffn)
    d_middle = cotangent.astype(jnp.float32) + d_middle_norm
    d_branch = d_middle.astype(jnp.bfloat16)
    shard_rows = lax.all_gather(d_branch, "mp", axis=0, tiled=True)
    rows_grad = inner_cols(shard_rows, w_out)
    grad_out_proj = inner_rows(attn_flat, shard_rows)
    d_mixed = rows_grad.astype(jnp.bfloat16).reshape(seq_here, LEN, heads_here, HD)
    d_queries, d_own_keys, d_own_values, d_far_keys, d_far_values = lax.map(
        attend_back,
        (queries, own_keys, own_values, far_keys, far_values, far_valid, log_total, d_mixed),
    )
    prompt_grad = jnp.concatenate(
        [
            d_far_keys.reshape(seq_here, PMAX, head_cols),
            d_far_values.reshape(seq_here, PMAX, head_cols),
        ],
        axis=2,
    )
    row_ids = jnp.arange(lax.axis_size("dp") * seq_here, dtype=jnp.int32)
    picker = (my_partner[:, None] == row_ids[None, :]).astype(jnp.float32)
    returned_kv = lax.psum_scatter(
        jnp.einsum("kr,kpc->rpc", picker, prompt_grad, precision=highest).astype(jnp.bfloat16),
        "dp",
        scatter_dimension=0,
        tiled=True,
    ).astype(jnp.float32)
    d_kv_rows = jnp.concatenate(
        [
            d_own_keys.reshape(seq_here, LEN, head_cols),
            d_own_values.reshape(seq_here, LEN, head_cols),
        ],
        axis=2,
    )
    d_kv_rows = jax.vmap(
        lambda sequence, window, offset: lax.dynamic_update_slice_in_dim(
            sequence, lax.dynamic_slice_in_dim(sequence, offset, PMAX, 0) + window, offset, 0
        )
    )(d_kv_rows, returned_kv, my_starts)
    d_qkv = jnp.stack(
        [
            d_queries.reshape(block_tokens, head_cols),
            d_kv_rows[:, :, :head_cols].reshape(block_tokens, head_cols),
            d_kv_rows[:, :, head_cols:].reshape(block_tokens, head_cols),
        ],
        axis=1,
    ).astype(jnp.bfloat16)
    d_normed_attn = lax.psum_scatter(
        jnp.einsum("tsj,jsd->td", d_qkv, w_qkv, preferred_element_type=jnp.float32).astype(
            jnp.bfloat16
        ),
        "mp",
        scatter_dimension=0,
        tiled=True,
    ).astype(jnp.float32)
    grad_qkv = jnp.einsum(
        "tsj,td->jsd",
        d_qkv,
        lax.all_gather(normed_attn, "mp", axis=0, tiled=True),
        preferred_element_type=jnp.float32,
    )
    _, norm_attn_pull = jax.vjp(
        lambda values, table: adaptive_norm(values, table, code_hot), inputs, ada_attn
    )
    d_inputs_norm, grad_table_attn = norm_attn_pull(d_normed_attn)
    grad_tokens = (d_middle + d_inputs_norm).astype(jnp.bfloat16)
    grad_attn_local = jnp.concatenate([grad_qkv, grad_out_proj[:, None, :]], axis=1)
    grad_ffn_local = jnp.stack([grad_up, grad_down], axis=1)
    grad_attn, grad_ffn = (
        lax.psum_scatter(
            grad_attn_local.astype(jnp.bfloat16), "dp", scatter_dimension=2, tiled=True
        ).astype(jnp.float32),
        lax.psum_scatter(
            grad_ffn_local.astype(jnp.bfloat16), "dp", scatter_dimension=2, tiled=True
        ).astype(jnp.float32),
    )
    grad_ada_attn, grad_ada_ffn = (
        lax.psum_scatter(grad_table_attn, ("dp", "mp"), scatter_dimension=2, tiled=True),
        lax.psum_scatter(grad_table_ffn, ("dp", "mp"), scatter_dimension=2, tiled=True),
    )
    return (output, grad_tokens, grad_attn, grad_ffn, grad_ada_attn, grad_ada_ffn)


def solution(mesh):
    in_specs = (
        P(("dp", "mp"), None),
        P("mp", None, None),
        P("mp", None, None),
        P(),
        P(),
        P(),
        P(),
        P(),
        P(),
        P(),
        P(("dp", "mp"), None),
    )
    out_specs = (
        P(("dp", "mp"), None),
        P(("dp", "mp"), None),
        P("mp", None, "dp"),
        P("mp", None, "dp"),
        P(None, None, ("dp", "mp")),
        P(None, None, ("dp", "mp")),
    )
    return jax.shard_map(shards, mesh=mesh, in_specs=in_specs, out_specs=out_specs, check_vma=False)
```

```python
import collections
import functools

import jax
import jax.numpy as jnp
from jax import lax
from jax.experimental import pallas as pl
from jax.experimental.pallas import tpu as pltpu
from jax.sharding import PartitionSpec as P

HD = 64
LEN = 1024
PMAX = 256


epsilon = 1e-05
highest = lax.Precision.HIGHEST


def partner_rows(group_sizes, partner_pick):
    group_end = jnp.cumsum(group_sizes)
    begins = group_end - group_sizes
    row_ids = jnp.arange(partner_pick.shape[0], dtype=jnp.int32)
    owner_group = jnp.sum((group_end[None, :] <= row_ids[:, None]).astype(jnp.int32), axis=1)
    member = (
        owner_group[:, None] == jnp.arange(group_sizes.shape[0], dtype=jnp.int32)[None, :]
    ).astype(jnp.int32)
    first_row = jnp.sum(member * begins[None, :], axis=1)
    group_len = jnp.sum(member * group_sizes[None, :], axis=1)
    span_size = jnp.maximum(group_len - 1, 1)
    return first_row + (row_ids - first_row + 1 + partner_pick % span_size) % group_len


def adaptive_norm(inputs, table, code_hot):
    coefficients = jnp.dot(code_hot, table.reshape(table.shape[0], -1), precision=highest)
    coefficients = coefficients.reshape(inputs.shape[0], 2, inputs.shape[1])
    center = inputs - jnp.mean(inputs, axis=-1, keepdims=True)
    spread = jnp.mean(center * center, axis=-1, keepdims=True)
    normed = center * lax.rsqrt(spread + epsilon)
    return (1.0 + coefficients[:, 0, :]) * normed + coefficients[:, 1, :]


def inner_rows(left, right):
    return lax.dot_general(
        left, right, (((0,), (0,)), ((), ())), preferred_element_type=jnp.float32
    )


def inner_cols(left, right):
    return lax.dot_general(
        left, right, (((1,), (1,)), ((), ())), preferred_element_type=jnp.float32
    )


def row_scores(queries, key_rows, far_valid):
    key_mask = jnp.concatenate([jnp.ones((queries.shape[0],), dtype=jnp.bool_), far_valid])
    scores = jnp.einsum(
        "qhd,khd->hqk", queries, key_rows, preferred_element_type=jnp.float32
    ) * HD ** (-0.5)
    return jnp.where(key_mask[None, None, :], scores, -1000000000.0)


def attend(packed):
    queries, own_keys, own_values, far_keys, far_values, far_valid = packed
    key_rows = jnp.concatenate([own_keys, far_keys], axis=0)
    value_rows = jnp.concatenate([own_values, far_values], axis=0)
    scores = row_scores(queries, key_rows, far_valid)
    row_max = jnp.max(scores, axis=-1, keepdims=True)
    log_total = row_max + jnp.log(jnp.sum(jnp.exp(scores - row_max), axis=-1, keepdims=True))
    prob_low = jnp.exp(scores - log_total).astype(jnp.bfloat16)
    mixed = jnp.einsum("hqk,khd->qhd", prob_low, value_rows, preferred_element_type=jnp.float32)
    return (mixed.astype(jnp.bfloat16), log_total)


def attend_back(packed):
    queries, own_keys, own_values, far_keys, far_values, far_valid, log_total, d_mixed = packed
    key_rows = jnp.concatenate([own_keys, far_keys], axis=0)
    value_rows = jnp.concatenate([own_values, far_values], axis=0)
    scores = row_scores(queries, key_rows, far_valid)
    attn_prob = jnp.exp(scores - log_total)
    prob_low = attn_prob.astype(jnp.bfloat16)
    d_values = jnp.einsum("hqk,qhd->khd", prob_low, d_mixed, preferred_element_type=jnp.float32)
    d_prob = jnp.einsum("qhd,khd->hqk", d_mixed, value_rows, preferred_element_type=jnp.float32)
    row_delta = jnp.sum(attn_prob * d_prob, axis=-1, keepdims=True)
    d_scores = (attn_prob * (d_prob - row_delta)).astype(jnp.bfloat16)
    d_queries = jnp.einsum(
        "hqk,khd->qhd", d_scores, key_rows, preferred_element_type=jnp.float32
    ) * HD ** (-0.5)
    d_keys = jnp.einsum(
        "hqk,qhd->khd", d_scores, queries, preferred_element_type=jnp.float32
    ) * HD ** (-0.5)
    own_len = queries.shape[0]
    return (d_queries, d_keys[:own_len], d_values[:own_len], d_keys[own_len:], d_values[own_len:])


MESH = pl.DeviceIdType.MESH
F32 = jnp.float32
BF16 = jnp.bfloat16
LANES = 128


def dot(left, right, left_dim=1, right_dim=0):
    return lax.dot_general(
        left, right, (((left_dim,), (right_dim,)), ((), ())), preferred_element_type=F32
    )


class Links:
    def __init__(self, z_size, send_sem, recv_sem):
        self.dp = lax.axis_index("dp")
        self.mp = lax.axis_index("mp")
        self.z_size = z_size
        self.order = (z_size - 1, 0) + tuple(range(1, z_size - 1))
        self.y = lax.rem(self.dp, 2)
        self.z = self.dp // 2
        self.core = lax.rem(self.mp, 2)
        self.x = self.mp // 2
        self.sib = (self.dp, self.mp + 1 - 2 * self.core)
        self.xpeer = (self.dp, self.mp + 2 - 4 * self.x)
        self.ypeer = (self.dp + 1 - 2 * self.y, self.mp)
        self.right = (self.dp + 2, self.mp)
        self.left = (self.dp - 2, self.mp)
        self.send_sem = send_sem
        self.recv_sem = recv_sem
        self.used = 0
        self.sent = []
        self.pair_sends = {}

    def take(self, count=1):
        first = self.used
        self.used += count
        return first

    def copy(self, src, dst, number, device):
        return pltpu.make_async_remote_copy(
            src_ref=src,
            dst_ref=dst,
            send_sem=self.send_sem.at[number],
            recv_sem=self.recv_sem.at[number],
            device_id=device,
            device_id_type=MESH,
        )

    def swap(self, src, dst, device):
        made = self.copy(src, dst, self.take(), device)
        self.sent.append(made)
        return made

    def finish(self, made=None):
        for one in list(self.sent):
            if made is None or one is made:
                one.wait_send()
        self.sent = [one for one in self.sent if made is not None and one is not made]

    def barrier(self):
        bar = pltpu.get_barrier_semaphore()
        for device in (self.sib, self.xpeer, self.ypeer):
            pl.semaphore_signal(bar, inc=1, device_id=device, device_id_type=MESH)

        @pl.when(self.z > 0)
        def _():
            pl.semaphore_signal(bar, inc=1, device_id=self.left, device_id_type=MESH)

        @pl.when(self.z < self.z_size - 1)
        def _():
            pl.semaphore_signal(bar, inc=1, device_id=self.right, device_id_type=MESH)

        inner = (self.z > 0).astype(jnp.int32) + (self.z < self.z_size - 1).astype(jnp.int32)
        pl.semaphore_wait(bar, 3 + inner)


class LineReduce:
    def __init__(self, links, held, passing):
        self.setup(links, held, passing)

    def setup(self, links, held, passing):
        self.k = links
        self.held, self.passing = held, passing
        self.nr = links.take(links.z_size)
        self.nl = links.take(links.z_size)

    def z_copy(self, d, rightward):
        k = self.k
        if rightward:
            return k.copy(self.held.at[d], self.passing.at[d], self.nr + d, k.right)
        slot = jnp.where(k.z - 1 == d, k.z_size, d)
        return k.copy(self.held.at[d], self.passing.at[slot], self.nl + d, k.left)

    def add(self, d):
        total = self.held[d].astype(F32) + self.passing[d].astype(F32)
        self.held[d] = total.astype(self.held.dtype)

    def begin(self, d):
        k = self.k
        last = k.z_size - 1
        if d > 0:

            @pl.when(k.z == 0)
            def _():
                self.z_copy(d, True).start()

        if d < last:

            @pl.when(k.z == last)
            def _():
                self.z_copy(d, False).start()

    def step(self, i):
        k = self.k
        n = k.z_size

        @pl.when(k.z == i)
        def _():
            for d in range(n - 1, i, -1):
                self.z_copy(d, True).wait_recv()
                self.add(d)
                self.z_copy(d, True).start()

        @pl.when(k.z == n - 1 - i)
        def _():
            for d in range(n - 1 - i):
                self.z_copy(d, False).wait_recv()
                self.add(d)
                self.z_copy(d, False).start()

    def finish(self, store):
        k = self.k
        n = k.z_size

        @pl.when(k.z > 0)
        def _():
            k.copy(self.held.at[k.z], self.passing.at[k.z], self.nr + k.z, k.left).wait_recv()

        @pl.when(k.z < n - 1)
        def _():
            k.copy(self.held.at[k.z], self.passing.at[n], self.nl + k.z, k.right).wait_recv()

        total = self.held[k.z].astype(F32)
        from_left = jnp.where(k.z > 0, self.passing[k.z].astype(F32), 0.0)
        from_right = jnp.where(k.z < n - 1, self.passing[n].astype(F32), 0.0)
        store(total + from_left + from_right)

    def wait_sends(self):
        k = self.k
        for d in range(k.z_size):

            @pl.when(k.z < d)
            def _(d=d):
                self.z_copy(d, True).wait_send()

            @pl.when(k.z > d)
            def _(d=d):
                self.z_copy(d, False).wait_send()


class GridReduce(LineReduce):
    def __init__(self, links, local, held, passing):
        self.setup(links, held, passing)
        self.local = local
        self.ny = links.take(links.z_size)

    def y_copy(self, d):
        k = self.k
        other = 2 * d + 1 - k.y
        return k.copy(self.local.at[other], self.held.at[d], self.ny + d, k.ypeer)

    def send_y(self, d):
        self.y_copy(d).start()

    def send_all(self):
        for d in self.k.order:
            self.send_y(d)

    def merge_y(self, d):
        self.y_copy(d).wait_recv()
        total = self.local[2 * d + self.k.y].astype(F32) + self.held[d].astype(F32)
        self.held[d] = total.astype(self.held.dtype)

    def take(self, *dests):
        for d in dests:
            self.merge_y(d)
            self.begin(d)

    def wait_y(self):
        for d in range(self.k.z_size):
            self.y_copy(d).wait_send()


class LineGather:
    def __init__(self, links, slots):
        self.k = links
        self.slots = slots
        self.nr = links.take(links.z_size)
        self.nl = links.take(links.z_size)

    def z_copy(self, slot, rightward):
        k = self.k
        number = (self.nr if rightward else self.nl) + slot
        place = self.slots.at[slot]
        return k.copy(place, place, number, k.right if rightward else k.left)

    def start(self):
        k = self.k

        @pl.when(k.z < k.z_size - 1)
        def _():
            self.z_copy(k.z, True).start()

        @pl.when(k.z > 0)
        def _():
            self.z_copy(k.z, False).start()

    def serve(self, distance):
        k = self.k

        @pl.when(k.z >= distance)
        def _():
            self.z_copy(k.z - distance, True).wait_recv()

            @pl.when(k.z < k.z_size - 1)
            def _():
                self.z_copy(k.z - distance, True).start()

        @pl.when(k.z + distance < k.z_size)
        def _():
            self.z_copy(k.z + distance, False).wait_recv()

            @pl.when(k.z > 0)
            def _():
                self.z_copy(k.z + distance, False).start()

    def wait_sends(self):
        k = self.k
        for slot in range(k.z_size):

            @pl.when(jnp.logical_and(k.z >= slot, k.z < k.z_size - 1))
            def _(slot=slot):
                self.z_copy(slot, True).wait_send()

            @pl.when(jnp.logical_and(k.z <= slot, k.z > 0))
            def _(slot=slot):
                self.z_copy(slot, False).wait_send()


class Exchange:
    def __init__(self, links, pair_out, pair_in, x_out, x_in):
        self.k = links
        self.pair_out, self.pair_in, self.x_out, self.x_in = pair_out, pair_in, x_out, x_in
        self.pair = {}
        self.along_x = {}

    def give(self, r, term, slot=None):
        slot = r if slot is None else slot
        if slot in self.k.pair_sends:
            self.k.finish(self.k.pair_sends[slot])
        self.pair_out[slot] = term.astype(BF16)
        made = self.k.swap(self.pair_out.at[slot], self.pair_in.at[slot], self.k.sib)
        made.start()
        self.k.pair_sends[slot] = made
        self.pair[r] = (made, slot)

    def pair_sum(self, r, term):
        made, slot = self.pair[r]
        made.wait_recv()
        return term + self.pair_in[slot].astype(F32)

    def send_x(self, r, total):
        self.x_out[r] = total.astype(BF16)
        made = self.k.swap(self.x_out.at[r], self.x_in.at[r], self.k.xpeer)
        made.start()
        self.along_x[r] = made

    def total(self, r):
        self.along_x[r].wait_recv()
        return self.x_out[r].astype(F32) + self.x_in[r].astype(F32)


class Settle:
    def __init__(self, exchange, shards, x_out, x_in, term):
        k = exchange.k
        own, sib, across, diag = shards
        exchange.give(2, term(diag), 0)
        x_out[...] = exchange.pair_sum(2, term(across)).astype(BF16)
        self.along_x = k.swap(x_out, x_in, k.xpeer)
        self.along_x.start()
        self.x_in = x_in
        exchange.give(3, term(sib), 1)
        self.kept = exchange.pair_sum(3, term(own))

    def total(self, kept):
        self.along_x.wait_recv()
        return kept + self.x_in[...].astype(F32)


def normalize(values):
    center = values - jnp.mean(values, axis=1, keepdims=True)
    spread = jnp.mean(center * center, axis=1, keepdims=True)
    scale = lax.rsqrt(spread + epsilon)
    return center * scale, scale


def norm_back(values, table, d_normed):
    normed, scale = normalize(values)
    dz = (1.0 + table[0:1, :]) * d_normed
    both = jnp.mean(dz * normed, axis=1, keepdims=True)
    d_values = (dz - jnp.mean(dz, axis=1, keepdims=True) - normed * both) * scale
    d_gain = jnp.sum(d_normed * normed, axis=0, keepdims=True)
    d_shift = jnp.sum(d_normed, axis=0, keepdims=True)
    return d_values, d_gain, d_shift


def layer_kernel(names, z_size, *refs):
    held = dict(zip(names, refs))
    held.update(
        d_mixed=held["act"],
        d_query=held["mixed"],
        d_branch=held["normed_ffn"],
        d_query_low=held["attn_t"],
        d_keys_low=held["keys_t"],
        d_values_low=held["values_t"],
        g_attn=held["g_down"],
    )
    n = collections.namedtuple("Buffers", held)(**held)
    k = Links(z_size, n.send_sem, n.recv_sem)
    mp_size, block, width = n.normed.shape
    seq = mp_size * block
    heads_wide = n.wa.shape[1]
    hidden = n.wf.shape[1]
    heads = heads_wide // HD
    q_wide = heads * block
    tile = block
    far = mp_size
    own_shard = 2 * k.x + k.core
    sib_shard = 2 * k.x + 1 - k.core
    x_shard = 2 * (1 - k.x) + k.core
    diag_shard = 2 * (1 - k.x) + 1 - k.core
    shards = (own_shard, sib_shard, x_shard, diag_shard)

    def mine(r):
        return 2 * r + k.core

    def theirs(r):
        return 2 * r + 1 - k.core

    def span(i, size=tile):
        return pl.ds(pl.multiple_of(i * size, size), size)

    fetches = []

    def fetch(src, dst):
        made = pltpu.make_async_copy(src, dst, n.load_sem.at[len(fetches)])
        made.start()
        fetches.append(made)
        return made

    load_tokens = fetch(n.tokens, n.raw.at[k.x])
    load_wa = fetch(n.w_attn, n.wa)
    load_cot = fetch(n.cotangent, n.cot.at[own_shard])
    load_wf = fetch(n.w_ffn, n.wf)

    def partner_of(row):
        begin, first, count = 0, 0, 1
        for g in range(n.group_sizes.shape[0]):
            size = n.group_sizes[g]
            inside = jnp.logical_and(row >= begin, row < begin + size)
            first = jnp.where(inside, begin, first)
            count = jnp.where(inside, size, count)
            begin = begin + size
        step = lax.rem(n.partner_pick[row], jnp.maximum(count - 1, 1))
        return jnp.clip(first + lax.rem(row - first + 1 + step, count), 0, 2 * z_size - 1)

    k.barrier()
    send_tokens = k.swap(n.tokens, n.raw.at[k.x], k.xpeer)
    send_tokens.start()
    cot_x = k.swap(n.cotangent, n.cot.at[own_shard], k.xpeer)
    cot_x.start()
    cot_sib = k.swap(n.cotangent, n.cot.at[own_shard], k.sib)
    cot_sib.start()

    code = n.codebook[k.dp]
    start = n.prompt_start[k.dp]
    partner = partner_of(k.dp)
    other_partner = partner_of(k.dp + 1 - 2 * k.y)
    part_z, part_y = partner // 2, lax.rem(partner, 2)
    other_z, other_y = other_partner // 2, lax.rem(other_partner, 2)
    far_len = n.prompt_len[partner]
    table_attn = n.ada_attn[code]
    table_ffn = n.ada_ffn[code]

    def adapt(normed, table):
        return ((1.0 + table[0:1, :]) * normed + table[1:2, :]).astype(BF16)

    def project(s):
        normed = n.normed[s]
        query = (dot(normed, n.wa[0], 1, 1) * HD ** (-0.5)).astype(BF16)
        lane = lax.broadcasted_iota(jnp.int32, (block, heads_wide), 1) // HD
        for h in range(heads):
            n.q4[s, h * block : (h + 1) * block, :] = jnp.where(lane == h, query, 0).astype(BF16)
        for ref, turned, w in ((n.keys, n.keys_t, 1), (n.values, n.values_t, 2)):
            made = dot(normed, n.wa[w], 1, 1)
            ref[s] = made.astype(BF16)
            turned[s] = made.T.astype(BF16)

    load_tokens.wait()
    n.normed[own_shard] = adapt(normalize(n.raw[k.x].astype(F32))[0], table_attn)
    normed_own = k.swap(n.normed.at[own_shard], n.normed.at[own_shard], k.sib)
    normed_own.start()
    load_wa.wait()
    normed_own.wait_recv()

    def project_pair(first):
        def body(i, carry):
            project(first + i)
            return carry

        lax.fori_loop(0, 2, body, 0)

    project_pair(2 * k.x)
    send_tokens.wait_recv()
    n.normed[x_shard] = adapt(normalize(n.raw[1 - k.x].astype(F32))[0], table_attn)
    normed_x = k.swap(n.normed.at[x_shard], n.normed.at[x_shard], k.sib)
    normed_x.start()
    normed_x.wait_recv()
    project_pair(2 * (1 - k.x))

    all_keys = n.keys[0:mp_size].reshape(seq, heads_wide)
    all_values = n.values[0:mp_size].reshape(seq, heads_wide)
    from_row = lax.broadcasted_iota(jnp.int32, (block, seq), 1)
    to_row = lax.broadcasted_iota(jnp.int32, (block, seq), 0)
    window = (from_row == to_row + start).astype(F32).astype(BF16)
    gathers = []
    for half, source in ((n.windows_k, all_keys), (n.windows_v, all_values)):
        half[k.z] = dot(window, source).astype(BF16)
        gathers.append(LineGather(k, half))
        gathers[-1].start()

    def attend_own(s, carry):
        q4 = n.q4[s]
        top = jnp.full((1, q_wide), -jnp.inf, F32)
        for c in range(mp_size):
            scores = dot(n.keys[c], q4, 1, 1)
            n.wide[c] = scores
            top = jnp.maximum(top, jnp.max(scores, axis=0, keepdims=True))
        total = jnp.zeros((1, q_wide), F32)
        for c in range(mp_size):
            prob = jnp.exp(n.wide[c] - top)
            total = total + jnp.sum(prob, axis=0, keepdims=True)
            low = prob.astype(BF16)
            for h in range(heads):
                rows = slice(h * HD, (h + 1) * HD)
                part = dot(n.values_t[c, rows, :], low[:, h * block : (h + 1) * block])
                n.mixed[s, rows, :] = part if c == 0 else n.mixed[s, rows, :] + part
        n.top[s] = top
        n.total[s] = total
        return carry

    y_windows = []
    for s in range(mp_size):
        lax.fori_loop(s, s + 1, attend_own, 0)
        if 0 < s < z_size:
            for half in range(2):
                gathers[half].serve(s)
                if s == z_size - 1:
                    n.y_out[half] = gathers[half].slots[other_z]
                    y_windows.append(k.swap(n.y_out.at[half], n.y_in.at[half], k.ypeer))
                    y_windows[-1].start()

    cot_x.wait_recv()
    cot_pass = k.swap(n.cot.at[x_shard], n.cot.at[x_shard], k.sib)
    cot_pass.start()
    same_y = part_y == k.y
    for half, (ref, turned) in enumerate(((n.keys, n.keys_t), (n.values, n.values_t))):
        y_windows[half].wait_recv()
        here = gathers[half].slots[part_z].astype(F32)
        far_rows = jnp.where(same_y, here, n.y_in[half].astype(F32))
        ref[far] = far_rows.astype(BF16)
        turned[far] = far_rows.T.astype(BF16)

    def attend_far(s):
        scores = dot(n.keys[far], n.q4[s], 1, 1)
        slot = lax.broadcasted_iota(jnp.int32, scores.shape, 0)
        scores = jnp.where(slot < far_len, scores, -1000000000.0)
        top = jnp.maximum(n.top[s], jnp.max(scores, axis=0, keepdims=True))
        scale = jnp.exp(n.top[s] - top)
        prob = jnp.exp(scores - top)
        total = n.total[s] * scale + jnp.sum(prob, axis=0, keepdims=True)
        low = prob.astype(BF16)
        for h in range(heads):
            rows = slice(h * HD, (h + 1) * HD)
            cols = slice(h * block, (h + 1) * block)
            part = n.mixed[s, rows, :] * scale[:, cols] + dot(n.values_t[far, rows, :], low[:, cols])
            n.attn_t[s, rows, :] = (part / total[:, cols]).astype(BF16)
        n.log_total[s] = top + jnp.log(total)

    def out_part(s):
        attend_far(s)
        return dot(n.attn_t[s], n.wa[3], 0, 0)

    branch = Exchange(k, n.pair_out, n.pair_in, n.x_out, n.x_in)
    for r in range(2):
        branch.give(r, out_part(theirs(r)))
        branch.send_x(r, branch.pair_sum(r, out_part(mine(r))))

    back = Exchange(k, n.pair_out, n.pair_in, n.x_out2, n.x_in2)
    load_cot.wait()
    load_wf.wait()
    cot_sib.wait_recv()
    cot_pass.wait_recv()

    def hidden_part(s):
        normed = n.normed_ffn[s]
        cot = n.cot[s]

        def body(i, carry):
            cols = span(i)
            up = dot(normed, n.wf[0, cols, :], 1, 1)
            d_act = dot(cot, n.wf[1, cols, :], 1, 1)
            cdf = 0.5 + 0.5 * lax.erf(up * (0.5**0.5))
            n.act[s, :, cols] = (up * cdf).astype(BF16)
            slope = cdf + up * (jnp.exp(-0.5 * up * up) * (2.0 * jnp.pi) ** (-0.5))
            n.d_up[s, :, cols] = (slope * d_act).astype(BF16)
            return carry

        lax.fori_loop(0, hidden // tile, body, 0)
        return dot(n.d_up[s], n.wf[0])

    shares = []
    for r in range(2):
        middle = n.raw[r].astype(F32) + branch.total(r)
        n.wide[r] = middle
        n.normed_ffn[mine(r)] = adapt(normalize(middle)[0], table_ffn)
        share = k.swap(n.normed_ffn.at[mine(r)], n.normed_ffn.at[mine(r)], k.sib)
        share.start()
        shares.append(share)
        share.wait_recv()
        back.give(r, hidden_part(theirs(r)))
        back.send_x(r, back.pair_sum(r, hidden_part(mine(r))))

    grid_down = GridReduce(k, n.g_down, n.h_down, n.p_down)
    grid_up = GridReduce(k, n.g_up, n.h_up, n.p_up)

    def spread(target, rows, made):
        for d in range(target.shape[0]):
            target[d, rows, :] = made[:, d * LANES : (d + 1) * LANES].astype(BF16)

    def ffn_grads(target, left, right):
        def body(i, carry):
            lhs = left[:, :, span(i)].reshape(seq, tile)
            spread(target, span(i), dot(lhs, right[...].reshape(seq, width), 0, 0))
            return carry

        lax.fori_loop(0, hidden // tile, body, 0)

    ffn_grads(n.g_down, n.act, n.cot)
    grid_down.send_all()
    ffn_grads(n.g_up, n.d_up, n.normed_ffn)

    def down_part(s):
        return dot(n.act[s], n.wf[1])

    k.finish(branch.along_x[0])
    out_sum = Settle(branch, shards, n.x_out.at[0], n.s_in, down_part)
    n.kept[...] = out_sum.kept

    n.d_keys[...] = jnp.zeros_like(n.d_keys)
    n.d_values[...] = jnp.zeros_like(n.d_values)
    table_grad = [jnp.zeros((1, width), F32), jnp.zeros((1, width), F32)]

    def prepare(s):
        d_attn_t = dot(n.wa[3], n.d_branch[s], 1, 1).astype(BF16)
        row = lax.broadcasted_iota(jnp.int32, (heads_wide, block), 0) // HD
        product = d_attn_t.astype(F32) * n.attn_t[s].astype(F32)
        for h in range(heads):
            rows = slice(h * HD, (h + 1) * HD)
            cols = slice(h * block, (h + 1) * block)
            n.delta[s, :, cols] = jnp.sum(product[rows], axis=0, keepdims=True)
            n.d_mixed[s, :, cols] = jnp.where(row == h, d_attn_t, 0).astype(BF16)

    def attend_back(s, first, last):
        q4 = n.q4[s]
        d_mixed = n.d_mixed[s]

        def body(c, carry):
            scores = dot(n.keys[c], q4, 1, 1)
            slot = lax.broadcasted_iota(jnp.int32, scores.shape, 0)
            limit = jnp.where(c == far, far_len, block)
            prob = jnp.where(slot < limit, jnp.exp(scores - n.log_total[s]), 0.0)
            low = prob.astype(BF16)
            d_prob = dot(n.values[c], d_mixed)
            d_scores = (prob * (d_prob - n.delta[s])).astype(BF16)
            n.d_values[c] += dot(low, d_mixed, 1, 1)
            n.d_keys[c] += dot(d_scores, q4)
            for h in range(heads):
                rows = slice(h * HD, (h + 1) * HD)
                n.d_query[s, rows, :] += dot(
                    n.keys_t[c, rows, :], d_scores[:, h * block : (h + 1) * block]
                )
            return carry

        lax.fori_loop(first, last, body, 0)

    n.d_query[...] = jnp.zeros_like(n.d_query)
    for r in range(2):
        d_values, d_gain, d_shift = norm_back(n.wide[r], table_ffn, back.total(r))
        table_grad[0] = table_grad[0] + d_gain
        table_grad[1] = table_grad[1] + d_shift
        d_middle = n.cot[mine(r)].astype(F32) + d_values
        n.wide[2 + r] = d_middle
        k.finish(shares[r])
        n.d_branch[mine(r)] = d_middle.astype(BF16)
        share = k.swap(n.d_branch.at[mine(r)], n.d_branch.at[mine(r)], k.sib)
        share.start()
        share.wait_recv()

        def both(i, carry, r=r):
            prepare(2 * r + i)
            attend_back(2 * r + i, far, far + 1)
            return carry

        lax.fori_loop(0, 2, both, 0)
        if r == 0:

            def rest(i, carry, r=r):
                attend_back(2 * r + i, 0, mp_size)
                return carry

            lax.fori_loop(0, 1, rest, 0)
            grid_down.take(k.order[0])
            lax.fori_loop(1, 2, rest, 0)
            grid_down.take(k.order[1])

    def table_blocks(target, gain, shift):
        row = lax.broadcasted_iota(jnp.int32, (n.t_ffn.shape[1], width), 0)
        both = jnp.where(lax.rem(row, 2) == 0, gain, shift)
        both = jnp.where(row // 2 == code, both, 0.0)
        for d in range(target.shape[0]):
            target[d] = both[:, d * LANES : (d + 1) * LANES]

    y_grads = []
    for half, ref in enumerate((n.d_keys, n.d_values)):
        k.finish(y_windows[half])
        n.y_out[half] = jnp.where(same_y, 0.0, ref[far]).astype(BF16)
        y_grads.append(k.swap(n.y_out.at[half], n.y_in.at[half], k.ypeer))
        y_grads[half].start()
    table_blocks(n.t_ffn, table_grad[0], table_grad[1])
    grid_t_ffn = GridReduce(k, n.t_ffn, n.ht_ffn, n.pt_ffn)
    grid_t_ffn.send_all()
    grid_up.send_all()
    lines = []
    for gather, held, passing in (
        (gathers[0], n.windows_k, n.passing_k),
        (gathers[1], n.windows_v, n.passing_v),
    ):
        gather.wait_sends()
        lines.append(LineReduce(k, held, passing))

    def rest_last(i, carry):
        attend_back(2 + i, 0, mp_size)
        return carry

    lax.fori_loop(0, 1, rest_last, 0)
    for half, ref in enumerate((n.d_keys, n.d_values)):
        y_grads[half].wait_recv()
        back_grad = n.y_in[half].astype(F32)
        for d in k.order:
            here = jnp.where(jnp.logical_and(same_y, part_z == d), ref[far], 0.0)
            there = jnp.where(jnp.logical_and(other_y == k.y, other_z == d), back_grad, 0.0)
            lines[half].held[d] = (here + there).astype(BF16)
            lines[half].begin(d)
    lax.fori_loop(1, 2, rest_last, 0)
    for line in lines:
        line.step(1)
    grid_down.take(*k.order[2:])
    grid_down.wait_y()

    grid_oq = GridReduce(k, n.g_attn.at[:, 0 : 2 * heads_wide], n.h_oq, n.p_oq)
    grid_kv = GridReduce(k, n.g_attn.at[:, 2 * heads_wide : 4 * heads_wide], n.h_kv, n.p_kv)

    def add_products(left, right):
        total = dot(left[0], right[0])
        for s in range(1, mp_size):
            total = total + dot(left[s], right[s])
        return total

    spread(n.g_attn, slice(0, heads_wide), add_products(n.attn_t, n.d_branch))
    for line in lines:
        line.step(2)
    for s in range(mp_size):
        n.d_query_low[s] = (n.d_query[s] * HD ** (-0.5)).astype(BF16)
    spread(n.g_attn, slice(heads_wide, 2 * heads_wide), add_products(n.d_query_low, n.normed))
    grid_oq.send_all()
    grid_t_ffn.take(*k.order)
    grid_down.step(1)

    def take_back(half):
        def store(total):
            n.far_sum[half] = total.astype(BF16)

        return store

    for half in range(2):
        lines[half].finish(take_back(half))
    from_slot = lax.broadcasted_iota(jnp.int32, (seq, block), 1)
    to_frame = lax.broadcasted_iota(jnp.int32, (seq, block), 0)
    unwindow = (to_frame == from_slot + start).astype(F32).astype(BF16)
    for half, (ref, low) in enumerate(((n.d_keys, n.d_keys_low), (n.d_values, n.d_values_low))):
        own = ref[0:mp_size].reshape(seq, heads_wide)
        total = own + dot(unwindow, n.far_sum[half])
        low[0:mp_size] = total.astype(BF16).reshape(mp_size, block, heads_wide)

    flat_normed = n.normed[...].reshape(seq, width)
    for w, low in ((2, n.d_keys_low), (3, n.d_values_low)):
        made = dot(low[0:mp_size].reshape(seq, heads_wide), flat_normed, 0, 0)
        spread(n.g_attn, slice(w * heads_wide, (w + 1) * heads_wide), made)
    grid_kv.send_all()

    def input_part(s):
        return (
            dot(n.d_query_low[s], n.wa[0], 0, 0)
            + dot(n.d_keys_low[s], n.wa[1])
            + dot(n.d_values_low[s], n.wa[2])
        )

    k.finish(back.along_x[0])
    n.output[...] = (n.wide[k.x] + out_sum.total(n.kept[...])).astype(BF16)
    in_sum = Settle(back, shards, n.x_out2.at[0], n.x_in.at[0], input_part)
    n.kept[...] = in_sum.kept
    grid_t_ffn.step(1)
    grid_down.step(2)
    grid_up.take(*k.order)
    grid_t_ffn.step(2)

    quarter = heads_wide

    def store_ffn(s):
        def store(total):
            n.grad_ffn[pl.ds(s, hidden, stride=2), :] = total

        return store

    def store_attn(*places):
        def store(total):
            for i, s in enumerate(places):
                rows = total[i * quarter : (i + 1) * quarter]
                n.grad_attn[pl.ds(s, quarter, stride=4), :] = rows

        return store

    d_values, d_gain, d_shift = norm_back(n.raw[k.x].astype(F32), table_attn, in_sum.total(n.kept[...]))
    n.grad_tokens[...] = (n.wide[2 + k.x] + d_values).astype(BF16)
    table_blocks(n.t_attn, d_gain, d_shift)
    grid_t_attn = GridReduce(k, n.t_attn, n.ht_attn, n.pt_attn)
    grid_t_attn.send_all()
    grid_down.finish(store_ffn(1))
    grid_oq.take(*k.order)
    grid_up.step(1)
    grid_t_attn.take(*k.order)
    grid_oq.step(1)
    grid_up.step(2)
    grid_t_attn.step(1)
    grid_kv.take(*k.order)
    grid_oq.step(2)
    grid_t_attn.step(2)
    grid_up.finish(store_ffn(0))

    def store_table(over_x):
        def store(total):
            n.t_out[over_x, 0] = total
            pair = k.swap(n.t_out.at[over_x, 0], n.t_in.at[over_x, 0], k.sib)
            pair.start()
            pair.wait_recv()
            total = total + n.t_in[over_x, 0]
            if over_x:
                n.t_out[over_x, 1] = total
                along = k.swap(n.t_out.at[over_x, 1], n.t_in.at[over_x, 1], k.xpeer)
                along.start()
                along.wait_recv()
                total = total + n.t_in[over_x, 1]
            piece = LANES // mp_size
            kept = total
            for m in range(1, mp_size):
                turned = pltpu.roll(total, LANES - m * piece, 1)
                kept = jnp.where(k.mp == m, turned, kept)
            n.grad_ada[over_x] = kept

        return store

    grid_t_ffn.finish(store_table(0))
    grid_kv.step(1)
    grid_t_attn.finish(store_table(1))
    grid_oq.finish(store_attn(3, 0))
    grid_kv.step(2)
    grid_kv.finish(store_attn(1, 2))
    k.finish()
    for line in lines:
        line.wait_sends()
    for unit in (grid_down, grid_up, grid_oq, grid_kv, grid_t_ffn, grid_t_attn):
        unit.wait_sends()
        if unit is not grid_down:
            unit.wait_y()


def layer(tokens, cotangent, w_attn, w_ffn, ada_attn, ada_ffn, ints, dp_size, mp_size):
    z_size = dp_size // 2
    block, width = tokens.shape
    heads_wide = w_attn.shape[1]
    hidden = w_ffn.shape[1]
    heads = heads_wide // HD
    table_rows = ada_attn.shape[0] * 2
    lane_block = width // dp_size

    inputs = dict(
        tokens=tokens,
        cotangent=cotangent,
        w_attn=w_attn,
        w_ffn=w_ffn,
        ada_attn=ada_attn,
        ada_ffn=ada_ffn,
        **ints,
    )
    spaces = dict.fromkeys(("tokens", "cotangent", "w_attn", "w_ffn"), pl.ANY)
    spaces.update(dict.fromkeys(ints, pltpu.SMEM))
    outputs = dict(
        output=((block, width), BF16),
        grad_tokens=((block, width), BF16),
        grad_attn=((4 * heads_wide, lane_block), F32),
        grad_ffn=((2 * hidden, lane_block), F32),
        grad_ada=((2, table_rows, lane_block), F32),
    )
    wide = (mp_size, block, width)
    two = (2, block, width)
    square = (mp_size + 1, block, heads_wide)
    low, full = {}, {}
    for name in ("normed", "cot", "normed_ffn", "act", "d_up"):
        low[name] = wide
    low.update(raw=two, wa=w_attn.shape, wf=w_ffn.shape)
    for name in ("keys", "values", "keys_t", "values_t"):
        low[name] = square
    low.update(q4=(mp_size, heads * block, heads_wide), attn_t=(mp_size, heads_wide, block))
    for name in ("pair_out", "pair_in", "x_out", "x_in", "x_out2", "x_in2"):
        low[name] = two
    low.update(s_in=(block, width))
    for name in ("far_sum", "y_out", "y_in"):
        low[name] = (2, block, heads_wide)
    for name in ("k", "v"):
        low["windows_" + name] = (z_size, block, heads_wide)
        low["passing_" + name] = (z_size + 1, block, heads_wide)
    for name in ("up", "down"):
        low["g_" + name] = (dp_size, hidden, lane_block)
    half = 2 * heads_wide
    for name, rows in (("up", hidden), ("down", hidden), ("oq", half), ("kv", half)):
        low["h_" + name] = (z_size, rows, lane_block)
        low["p_" + name] = (z_size + 1, rows, lane_block)
    for name in ("_ffn", "_attn"):
        full["t" + name] = (dp_size, table_rows, lane_block)
        full["ht" + name] = (z_size, table_rows, lane_block)
        full["pt" + name] = (z_size + 1, table_rows, lane_block)
    full.update(t_out=(2, 2, table_rows, lane_block), t_in=(2, 2, table_rows, lane_block))
    full.update(wide=(mp_size, block, heads * block), kept=(block, width))
    for name in ("top", "total", "log_total", "delta"):
        full[name] = (mp_size, 1, heads * block)
    full.update(mixed=(mp_size, heads_wide, block))
    full.update(d_keys=square, d_values=square)
    scratch = {name: pltpu.VMEM(shape, BF16) for name, shape in low.items()}
    scratch.update({name: pltpu.VMEM(shape, F32) for name, shape in full.items()})
    copies = 200
    scratch.update(
        load_sem=pltpu.SemaphoreType.DMA((4,)),
        send_sem=pltpu.SemaphoreType.DMA((copies,)),
        recv_sem=pltpu.SemaphoreType.DMA((copies,)),
    )
    names = tuple(inputs) + tuple(outputs) + tuple(scratch)
    return pl.pallas_call(
        functools.partial(layer_kernel, names, z_size),
        out_shape=tuple(jax.ShapeDtypeStruct(*shape) for shape in outputs.values()),
        in_specs=[pl.BlockSpec(memory_space=spaces.get(name, pltpu.VMEM)) for name in inputs],
        out_specs=[pl.BlockSpec(memory_space=pltpu.VMEM) for _ in outputs],
        scratch_shapes=list(scratch.values()),
        compiler_params=pltpu.CompilerParams(
            collective_id=1, has_side_effects=True, vmem_limit_bytes=60 << 20
        ),
    )(*inputs.values())


def place_kernel(count, *refs):
    moves = []
    for i in range(count):
        moves.append(pltpu.make_async_copy(refs[i], refs[count + i], refs[-1].at[i]))
        moves[i].start()
    for move in moves:
        move.wait()


def place(arrays):
    return pl.pallas_call(
        functools.partial(place_kernel, len(arrays)),
        out_shape=tuple(jax.ShapeDtypeStruct(a.shape, a.dtype) for a in arrays),
        in_specs=[pl.BlockSpec(memory_space=pltpu.VMEM)] * len(arrays),
        out_specs=[pl.BlockSpec(memory_space=pl.ANY)] * len(arrays),
        scratch_shapes=[pltpu.SemaphoreType.DMA((len(arrays),))],
    )(*arrays)


def shards(
    tokens,
    w_attn,
    w_ffn,
    ada_attn,
    ada_ffn,
    codebook,
    group_sizes,
    partner_pick,
    prompt_start,
    prompt_len,
    cotangent,
):
    tok_rows, width = tokens.shape
    mp_size = lax.axis_size("mp")
    dp_index = lax.axis_index("dp")
    mp_index = lax.axis_index("mp")
    block_tokens = tok_rows * mp_size
    seq_here = block_tokens // LEN
    head_cols = w_attn.shape[0]
    heads_here = head_cols // HD
    total_rows = codebook.shape[0]
    dp_size = lax.axis_size("dp")
    fits = width == dp_size * LANES and width == w_ffn.shape[0] == tok_rows * heads_here
    if seq_here == 1 and mp_size == 4 and fits and tok_rows == PMAX:
        ints = dict(
            codebook=codebook,
            group_sizes=group_sizes,
            partner_pick=partner_pick,
            prompt_start=prompt_start,
            prompt_len=prompt_len,
        )
        results = layer(
            tokens,
            cotangent,
            jnp.swapaxes(w_attn, 0, 1),
            jnp.swapaxes(w_ffn, 0, 1),
            ada_attn,
            ada_ffn,
            ints,
            dp_size,
            mp_size,
        )
        output, grad_tokens, grad_attn, grad_ffn = place(results[:4])
        grad_ada = results[4]
        grad_ada = grad_ada[:, :, : width // (dp_size * mp_size)]
        grad_ada = grad_ada.reshape((2,) + ada_attn.shape[:2] + grad_ada.shape[2:])
        return (
            output,
            grad_tokens,
            grad_attn.reshape(head_cols, 4, LANES),
            grad_ffn.reshape(w_ffn.shape[0], 2, LANES),
            grad_ada[1],
            grad_ada[0],
        )
    partner = partner_rows(group_sizes, partner_pick)
    first_row = dp_index * seq_here
    tok_global = (dp_index * mp_size + mp_index) * tok_rows + jnp.arange(tok_rows, dtype=jnp.int32)
    row_pick = (
        (tok_global // LEN)[:, None] == jnp.arange(total_rows, dtype=jnp.int32)[None, :]
    ).astype(jnp.int32)
    token_codes = jnp.sum(row_pick * codebook[None, :], axis=1)
    code_hot = (
        token_codes[:, None] == jnp.arange(ada_attn.shape[0], dtype=jnp.int32)[None, :]
    ).astype(jnp.float32)
    my_partner = lax.dynamic_slice_in_dim(partner, first_row, seq_here)
    my_starts = lax.dynamic_slice_in_dim(prompt_start, first_row, seq_here)
    partner_hot = (my_partner[:, None] == jnp.arange(total_rows, dtype=jnp.int32)[None, :]).astype(
        jnp.int32
    )
    partner_len = jnp.sum(partner_hot * prompt_len[None, :], axis=1)
    far_valid = jnp.arange(PMAX, dtype=jnp.int32)[None, :] < partner_len[:, None]
    inputs = tokens.astype(jnp.float32)
    normed_attn = adaptive_norm(inputs, ada_attn, code_hot).astype(jnp.bfloat16)
    normed_attn_full = lax.all_gather(normed_attn, "mp", axis=0, tiled=True)
    w_qkv = w_attn[:, 0:3, :]
    w_out = w_attn[:, 3, :]
    qkv_low = jnp.einsum(
        "td,jsd->tsj", normed_attn_full, w_qkv, preferred_element_type=jnp.float32
    ).astype(jnp.bfloat16)
    kv_rows = qkv_low[:, 1:3, :].reshape(seq_here, LEN, 2 * head_cols)
    windows = jax.vmap(
        lambda sequence, offset: lax.dynamic_slice_in_dim(sequence, offset, PMAX, 0)
    )(kv_rows, my_starts)
    shard_rows = lax.all_gather(windows, "dp", axis=0, tiled=True)
    row_ids = jnp.arange(shard_rows.shape[0], dtype=jnp.int32)
    picker = (my_partner[:, None] == row_ids[None, :]).astype(jnp.bfloat16)
    prompt_sum = jnp.einsum("kr,rpc->kpc", picker, shard_rows, preferred_element_type=jnp.float32)
    prompt_kv = prompt_sum.astype(jnp.bfloat16)
    queries = qkv_low[:, 0, :].reshape(seq_here, LEN, heads_here, HD)
    own_keys = qkv_low[:, 1, :].reshape(seq_here, LEN, heads_here, HD)
    own_values = qkv_low[:, 2, :].reshape(seq_here, LEN, heads_here, HD)
    far_keys = prompt_kv[:, :, :head_cols].reshape(seq_here, PMAX, heads_here, HD)
    far_values = prompt_kv[:, :, head_cols:].reshape(seq_here, PMAX, heads_here, HD)
    attended, log_total = lax.map(
        attend, (queries, own_keys, own_values, far_keys, far_values, far_valid)
    )
    attn_flat = attended.reshape(block_tokens, head_cols)
    middle = inputs + lax.psum_scatter(
        jnp.dot(attn_flat, w_out, preferred_element_type=jnp.float32).astype(jnp.bfloat16),
        "mp",
        scatter_dimension=0,
        tiled=True,
    ).astype(jnp.float32)
    normed_ffn = adaptive_norm(middle, ada_ffn, code_hot).astype(jnp.bfloat16)
    normed_ffn_full = lax.all_gather(normed_ffn, "mp", axis=0, tiled=True)
    w_up = w_ffn[:, 0, :]
    w_down = w_ffn[:, 1, :]
    up_proj = inner_cols(normed_ffn_full, w_up)
    activated = jax.nn.gelu(up_proj, approximate=False).astype(jnp.bfloat16)
    output = (
        middle
        + lax.psum_scatter(
            jnp.dot(activated, w_down, preferred_element_type=jnp.float32).astype(jnp.bfloat16),
            "mp",
            scatter_dimension=0,
            tiled=True,
        ).astype(jnp.float32)
    ).astype(jnp.bfloat16)
    shard_rows = lax.all_gather(cotangent, "mp", axis=0, tiled=True)
    rows_grad = inner_cols(shard_rows, w_down)
    d_act = rows_grad
    grad_down = inner_rows(activated, shard_rows)
    _, gelu_pull = jax.vjp(lambda values: jax.nn.gelu(values, approximate=False), up_proj)
    d_up = gelu_pull(d_act)[0].astype(jnp.bfloat16)
    d_normed_ffn = lax.psum_scatter(
        jnp.dot(d_up, w_up, preferred_element_type=jnp.float32).astype(jnp.bfloat16),
        "mp",
        scatter_dimension=0,
        tiled=True,
    ).astype(jnp.float32)
    grad_up = inner_rows(d_up, lax.all_gather(normed_ffn, "mp", axis=0, tiled=True))
    _, norm_ffn_pull = jax.vjp(
        lambda values, table: adaptive_norm(values, table, code_hot), middle, ada_ffn
    )
    d_middle_norm, grad_table_ffn = norm_ffn_pull(d_normed_ffn)
    d_middle = cotangent.astype(jnp.float32) + d_middle_norm
    d_branch = d_middle.astype(jnp.bfloat16)
    shard_rows = lax.all_gather(d_branch, "mp", axis=0, tiled=True)
    rows_grad = inner_cols(shard_rows, w_out)
    grad_out_proj = inner_rows(attn_flat, shard_rows)
    d_mixed = rows_grad.astype(jnp.bfloat16).reshape(seq_here, LEN, heads_here, HD)
    d_queries, d_own_keys, d_own_values, d_far_keys, d_far_values = lax.map(
        attend_back,
        (queries, own_keys, own_values, far_keys, far_values, far_valid, log_total, d_mixed),
    )
    prompt_grad = jnp.concatenate(
        [
            d_far_keys.reshape(seq_here, PMAX, head_cols),
            d_far_values.reshape(seq_here, PMAX, head_cols),
        ],
        axis=2,
    )
    row_ids = jnp.arange(lax.axis_size("dp") * seq_here, dtype=jnp.int32)
    picker = (my_partner[:, None] == row_ids[None, :]).astype(jnp.float32)
    returned_kv = lax.psum_scatter(
        jnp.einsum("kr,kpc->rpc", picker, prompt_grad, precision=highest).astype(jnp.bfloat16),
        "dp",
        scatter_dimension=0,
        tiled=True,
    ).astype(jnp.float32)
    d_kv_rows = jnp.concatenate(
        [
            d_own_keys.reshape(seq_here, LEN, head_cols),
            d_own_values.reshape(seq_here, LEN, head_cols),
        ],
        axis=2,
    )
    d_kv_rows = jax.vmap(
        lambda sequence, window, offset: lax.dynamic_update_slice_in_dim(
            sequence, lax.dynamic_slice_in_dim(sequence, offset, PMAX, 0) + window, offset, 0
        )
    )(d_kv_rows, returned_kv, my_starts)
    d_qkv = jnp.stack(
        [
            d_queries.reshape(block_tokens, head_cols),
            d_kv_rows[:, :, :head_cols].reshape(block_tokens, head_cols),
            d_kv_rows[:, :, head_cols:].reshape(block_tokens, head_cols),
        ],
        axis=1,
    ).astype(jnp.bfloat16)
    d_normed_attn = lax.psum_scatter(
        jnp.einsum("tsj,jsd->td", d_qkv, w_qkv, preferred_element_type=jnp.float32).astype(
            jnp.bfloat16
        ),
        "mp",
        scatter_dimension=0,
        tiled=True,
    ).astype(jnp.float32)
    grad_qkv = jnp.einsum(
        "tsj,td->jsd",
        d_qkv,
        lax.all_gather(normed_attn, "mp", axis=0, tiled=True),
        preferred_element_type=jnp.float32,
    )
    _, norm_attn_pull = jax.vjp(
        lambda values, table: adaptive_norm(values, table, code_hot), inputs, ada_attn
    )
    d_inputs_norm, grad_table_attn = norm_attn_pull(d_normed_attn)
    grad_tokens = (d_middle + d_inputs_norm).astype(jnp.bfloat16)
    grad_attn_local = jnp.concatenate([grad_qkv, grad_out_proj[:, None, :]], axis=1)
    grad_ffn_local = jnp.stack([grad_up, grad_down], axis=1)
    grad_attn, grad_ffn = (
        lax.psum_scatter(
            grad_attn_local.astype(jnp.bfloat16), "dp", scatter_dimension=2, tiled=True
        ).astype(jnp.float32),
        lax.psum_scatter(
            grad_ffn_local.astype(jnp.bfloat16), "dp", scatter_dimension=2, tiled=True
        ).astype(jnp.float32),
    )
    grad_ada_attn, grad_ada_ffn = (
        lax.psum_scatter(grad_table_attn, ("dp", "mp"), scatter_dimension=2, tiled=True),
        lax.psum_scatter(grad_table_ffn, ("dp", "mp"), scatter_dimension=2, tiled=True),
    )
    return (output, grad_tokens, grad_attn, grad_ffn, grad_ada_attn, grad_ada_ffn)


def solution(mesh):
    in_specs = (
        P(("dp", "mp"), None),
        P("mp", None, None),
        P("mp", None, None),
        P(),
        P(),
        P(),
        P(),
        P(),
        P(),
        P(),
        P(("dp", "mp"), None),
    )
    out_specs = (
        P(("dp", "mp"), None),
        P(("dp", "mp"), None),
        P("mp", None, "dp"),
        P("mp", None, "dp"),
        P(None, None, ("dp", "mp")),
        P(None, None, ("dp", "mp")),
    )
    return jax.shard_map(shards, mesh=mesh, in_specs=in_specs, out_specs=out_specs, check_vma=False)
```

```python
import collections
import functools

import jax
import jax.numpy as jnp
from jax import lax
from jax.experimental import pallas as pl
from jax.experimental.pallas import tpu as pltpu
from jax.sharding import PartitionSpec as P

HD = 64
LEN = 1024
PMAX = 256


epsilon = 1e-05
highest = lax.Precision.HIGHEST


def partner_rows(group_sizes, partner_pick):
    group_end = jnp.cumsum(group_sizes)
    begins = group_end - group_sizes
    row_ids = jnp.arange(partner_pick.shape[0], dtype=jnp.int32)
    owner_group = jnp.sum((group_end[None, :] <= row_ids[:, None]).astype(jnp.int32), axis=1)
    member = (
        owner_group[:, None] == jnp.arange(group_sizes.shape[0], dtype=jnp.int32)[None, :]
    ).astype(jnp.int32)
    first_row = jnp.sum(member * begins[None, :], axis=1)
    group_len = jnp.sum(member * group_sizes[None, :], axis=1)
    span_size = jnp.maximum(group_len - 1, 1)
    return first_row + (row_ids - first_row + 1 + partner_pick % span_size) % group_len


def adaptive_norm(inputs, table, code_hot):
    coefficients = jnp.dot(code_hot, table.reshape(table.shape[0], -1), precision=highest)
    coefficients = coefficients.reshape(inputs.shape[0], 2, inputs.shape[1])
    center = inputs - jnp.mean(inputs, axis=-1, keepdims=True)
    spread = jnp.mean(center * center, axis=-1, keepdims=True)
    normed = center * lax.rsqrt(spread + epsilon)
    return (1.0 + coefficients[:, 0, :]) * normed + coefficients[:, 1, :]


def inner_rows(left, right):
    return lax.dot_general(
        left, right, (((0,), (0,)), ((), ())), preferred_element_type=jnp.float32
    )


def inner_cols(left, right):
    return lax.dot_general(
        left, right, (((1,), (1,)), ((), ())), preferred_element_type=jnp.float32
    )


def row_scores(queries, key_rows, far_valid):
    key_mask = jnp.concatenate([jnp.ones((queries.shape[0],), dtype=jnp.bool_), far_valid])
    scores = jnp.einsum(
        "qhd,khd->hqk", queries, key_rows, preferred_element_type=jnp.float32
    ) * HD ** (-0.5)
    return jnp.where(key_mask[None, None, :], scores, -1000000000.0)


def attend(packed):
    queries, own_keys, own_values, far_keys, far_values, far_valid = packed
    key_rows = jnp.concatenate([own_keys, far_keys], axis=0)
    value_rows = jnp.concatenate([own_values, far_values], axis=0)
    scores = row_scores(queries, key_rows, far_valid)
    row_max = jnp.max(scores, axis=-1, keepdims=True)
    log_total = row_max + jnp.log(jnp.sum(jnp.exp(scores - row_max), axis=-1, keepdims=True))
    prob_low = jnp.exp(scores - log_total).astype(jnp.bfloat16)
    mixed = jnp.einsum("hqk,khd->qhd", prob_low, value_rows, preferred_element_type=jnp.float32)
    return (mixed.astype(jnp.bfloat16), log_total)


def attend_back(packed):
    queries, own_keys, own_values, far_keys, far_values, far_valid, log_total, d_mixed = packed
    key_rows = jnp.concatenate([own_keys, far_keys], axis=0)
    value_rows = jnp.concatenate([own_values, far_values], axis=0)
    scores = row_scores(queries, key_rows, far_valid)
    attn_prob = jnp.exp(scores - log_total)
    prob_low = attn_prob.astype(jnp.bfloat16)
    d_values = jnp.einsum("hqk,qhd->khd", prob_low, d_mixed, preferred_element_type=jnp.float32)
    d_prob = jnp.einsum("qhd,khd->hqk", d_mixed, value_rows, preferred_element_type=jnp.float32)
    row_delta = jnp.sum(attn_prob * d_prob, axis=-1, keepdims=True)
    d_scores = (attn_prob * (d_prob - row_delta)).astype(jnp.bfloat16)
    d_queries = jnp.einsum(
        "hqk,khd->qhd", d_scores, key_rows, preferred_element_type=jnp.float32
    ) * HD ** (-0.5)
    d_keys = jnp.einsum(
        "hqk,qhd->khd", d_scores, queries, preferred_element_type=jnp.float32
    ) * HD ** (-0.5)
    own_len = queries.shape[0]
    return (d_queries, d_keys[:own_len], d_values[:own_len], d_keys[own_len:], d_values[own_len:])


MESH = pl.DeviceIdType.MESH
F32 = jnp.float32
BF16 = jnp.bfloat16
LANES = 128


def dot(left, right, left_dim=1, right_dim=0):
    return lax.dot_general(
        left, right, (((left_dim,), (right_dim,)), ((), ())), preferred_element_type=F32
    )


class Links:
    def __init__(self, z_size, send_sem, recv_sem):
        self.dp = lax.axis_index("dp")
        self.mp = lax.axis_index("mp")
        self.z_size = z_size
        self.order = (z_size - 1, 0) + tuple(range(1, z_size - 1))
        self.y = lax.rem(self.dp, 2)
        self.z = self.dp // 2
        self.core = lax.rem(self.mp, 2)
        self.x = self.mp // 2
        self.sib = (self.dp, self.mp + 1 - 2 * self.core)
        self.xpeer = (self.dp, self.mp + 2 - 4 * self.x)
        self.ypeer = (self.dp + 1 - 2 * self.y, self.mp)
        self.right = (self.dp + 2, self.mp)
        self.left = (self.dp - 2, self.mp)
        self.send_sem = send_sem
        self.recv_sem = recv_sem
        self.used = 0
        self.sent = []
        self.pair_sends = {}

    def take(self, count=1):
        first = self.used
        self.used += count
        return first

    def copy(self, src, dst, number, device, landing=None):
        return pltpu.make_async_remote_copy(
            src_ref=src,
            dst_ref=dst,
            send_sem=self.send_sem.at[number],
            recv_sem=self.recv_sem.at[number if landing is None else landing],
            device_id=device,
            device_id_type=MESH,
        )

    def swap(self, src, dst, device):
        made = self.copy(src, dst, self.take(), device)
        self.sent.append(made)
        return made

    def finish(self, made=None):
        for one in list(self.sent):
            if made is None or one is made:
                one.wait_send()
        self.sent = [one for one in self.sent if made is not None and one is not made]

    def barrier(self):
        bar = pltpu.get_barrier_semaphore()
        for device in (self.sib, self.xpeer, self.ypeer):
            pl.semaphore_signal(bar, inc=1, device_id=device, device_id_type=MESH)

        @pl.when(self.z > 0)
        def _():
            pl.semaphore_signal(bar, inc=1, device_id=self.left, device_id_type=MESH)

        @pl.when(self.z < self.z_size - 1)
        def _():
            pl.semaphore_signal(bar, inc=1, device_id=self.right, device_id_type=MESH)

        inner = (self.z > 0).astype(jnp.int32) + (self.z < self.z_size - 1).astype(jnp.int32)
        pl.semaphore_wait(bar, 3 + inner)


class LineReduce:
    def __init__(self, links, held, passing):
        self.setup(links, held, passing)

    def setup(self, links, held, passing):
        self.k = links
        self.held, self.passing = held, passing
        self.nr = links.take(links.z_size)
        self.nl = links.take(links.z_size)

    def z_copy(self, d, rightward):
        k = self.k
        if rightward:
            return k.copy(self.held.at[d], self.passing.at[d], self.nr + d, k.right)
        landing = jnp.where(k.z - 1 == d, k.z_size, d)
        return k.copy(self.held.at[d], self.passing.at[landing], self.nl + d, k.left)

    def add(self, d):
        total = self.held[d].astype(F32) + self.passing[d].astype(F32)
        self.held[d] = total.astype(self.held.dtype)

    def begin(self, d):
        k = self.k
        last = k.z_size - 1
        if d > 0:

            @pl.when(k.z == 0)
            def _():
                self.z_copy(d, True).start()

        if d < last:

            @pl.when(k.z == last)
            def _():
                self.z_copy(d, False).start()

    def step(self, i):
        k = self.k
        n = k.z_size

        @pl.when(k.z == i)
        def _():
            for d in range(n - 1, i, -1):
                self.z_copy(d, True).wait_recv()
                self.add(d)
                self.z_copy(d, True).start()

        @pl.when(k.z == n - 1 - i)
        def _():
            for d in range(n - 1 - i):
                self.z_copy(d, False).wait_recv()
                self.add(d)
                self.z_copy(d, False).start()

    def finish(self, store):
        k = self.k
        n = k.z_size

        @pl.when(k.z > 0)
        def _():
            k.copy(self.held.at[k.z], self.passing.at[k.z], self.nr + k.z, k.left).wait_recv()

        @pl.when(k.z < n - 1)
        def _():
            k.copy(self.held.at[k.z], self.passing.at[n], self.nl + k.z, k.right).wait_recv()

        total = self.held[k.z].astype(F32)
        from_left = jnp.where(k.z > 0, self.passing[k.z].astype(F32), 0.0)
        from_right = jnp.where(k.z < n - 1, self.passing[n].astype(F32), 0.0)
        store(total + from_left + from_right)

    def wait_sends(self):
        k = self.k
        for d in range(k.z_size):

            @pl.when(k.z < d)
            def _(d=d):
                self.z_copy(d, True).wait_send()

            @pl.when(k.z > d)
            def _(d=d):
                self.z_copy(d, False).wait_send()


class GridReduce:
    def __init__(self, links, local, held, passing):
        n = links.z_size
        self.k = links
        self.local, self.held, self.passing = local, held, passing
        self.ny, self.ns, self.nr = links.take(n), links.take(n), links.take(n)
        self.inner = {n - 1: 1, 0: n - 2}

    def y_copy(self, d):
        k = self.k
        other = 2 * d + 1 - k.y
        return k.copy(self.local.at[other], self.held.at[d], self.ny + d, k.ypeer)

    def send_y(self, *dests):
        for d in dests or self.k.order:
            self.y_copy(d).start()

    def z_copy(self, d):
        k = self.k
        to = d
        if d in self.inner:
            to = jnp.where(k.z == k.z_size - 1 - d, self.inner[d], d)
        slot = jnp.where(to == d, k.z, to)
        device = (2 * to + k.y, k.mp)
        return k.copy(self.held.at[d], self.passing.at[slot], self.ns + d, device, self.nr + slot)

    def landed(self, slot):
        self.k.copy(self.held.at[0], self.passing.at[slot], self.ns, self.k.ypeer, self.nr + slot).wait_recv()

    def take(self, *dests):
        k = self.k
        for d in dests or k.order:
            self.y_copy(d).wait_recv()
            total = self.local[2 * d + k.y].astype(F32) + self.held[d].astype(F32)
            self.held[d] = total.astype(self.held.dtype)
            ready = k.z != d
            if d in self.inner:
                ready = jnp.logical_and(ready, k.z != self.inner[d])

            @pl.when(ready)
            def _(d=d):
                self.z_copy(d).start()

    def step(self):
        for d, at in self.inner.items():

            @pl.when(self.k.z == at)
            def _(d=d, at=at):
                self.landed(at)
                total = self.held[d].astype(F32) + self.passing[at].astype(F32)
                self.held[d] = total.astype(self.held.dtype)
                self.z_copy(d).start()

    def finish(self, store):
        k = self.k
        n = k.z_size
        total = self.held[k.z].astype(F32)
        for source in range(n):
            apart = jnp.abs(k.z - source)
            sends = jnp.logical_and(apart != 0, apart != n - 1)

            @pl.when(sends)
            def _(source=source):
                self.landed(source)

            total = total + jnp.where(sends, self.passing[source].astype(F32), 0.0)
        store(total)

    def wait_sends(self):
        for d in range(self.k.z_size):

            @pl.when(self.k.z != d)
            def _(d=d):
                self.z_copy(d).wait_send()

    def wait_y(self):
        for d in range(self.k.z_size):
            self.y_copy(d).wait_send()


class LineGather:
    def __init__(self, links, slots):
        self.k = links
        self.slots = slots
        self.nr = links.take(links.z_size)
        self.nl = links.take(links.z_size)

    def z_copy(self, slot, rightward):
        k = self.k
        number = (self.nr if rightward else self.nl) + slot
        place = self.slots.at[slot]
        return k.copy(place, place, number, k.right if rightward else k.left)

    def start(self):
        k = self.k

        @pl.when(k.z < k.z_size - 1)
        def _():
            self.z_copy(k.z, True).start()

        @pl.when(k.z > 0)
        def _():
            self.z_copy(k.z, False).start()

    def serve(self, distance):
        k = self.k

        @pl.when(k.z >= distance)
        def _():
            self.z_copy(k.z - distance, True).wait_recv()

            @pl.when(k.z < k.z_size - 1)
            def _():
                self.z_copy(k.z - distance, True).start()

        @pl.when(k.z + distance < k.z_size)
        def _():
            self.z_copy(k.z + distance, False).wait_recv()

            @pl.when(k.z > 0)
            def _():
                self.z_copy(k.z + distance, False).start()

    def wait_sends(self):
        k = self.k
        for slot in range(k.z_size):

            @pl.when(jnp.logical_and(k.z >= slot, k.z < k.z_size - 1))
            def _(slot=slot):
                self.z_copy(slot, True).wait_send()

            @pl.when(jnp.logical_and(k.z <= slot, k.z > 0))
            def _(slot=slot):
                self.z_copy(slot, False).wait_send()


class Exchange:
    def __init__(self, links, pair_out, pair_in, x_out, x_in):
        self.k = links
        self.pair_out, self.pair_in, self.x_out, self.x_in = pair_out, pair_in, x_out, x_in
        self.pair = {}
        self.along_x = {}

    def give(self, r, term, slot=None):
        slot = r if slot is None else slot
        if slot in self.k.pair_sends:
            self.k.finish(self.k.pair_sends[slot])
        self.pair_out[slot] = term.astype(BF16)
        made = self.k.swap(self.pair_out.at[slot], self.pair_in.at[slot], self.k.sib)
        made.start()
        self.k.pair_sends[slot] = made
        self.pair[r] = (made, slot)

    def pair_sum(self, r, term):
        made, slot = self.pair[r]
        made.wait_recv()
        return term + self.pair_in[slot].astype(F32)

    def send_x(self, r, total):
        self.x_out[r] = total.astype(BF16)
        made = self.k.swap(self.x_out.at[r], self.x_in.at[r], self.k.xpeer)
        made.start()
        self.along_x[r] = made

    def total(self, r):
        self.along_x[r].wait_recv()
        return self.x_out[r].astype(F32) + self.x_in[r].astype(F32)


class Settle:
    def __init__(self, exchange, shards, x_out, x_in, term):
        k = exchange.k
        own, sib, across, diag = shards
        exchange.give(2, term(diag), 0)
        x_out[...] = exchange.pair_sum(2, term(across)).astype(BF16)
        self.along_x = k.swap(x_out, x_in, k.xpeer)
        self.along_x.start()
        self.x_in = x_in
        exchange.give(3, term(sib), 1)
        self.kept = exchange.pair_sum(3, term(own))

    def total(self):
        self.along_x.wait_recv()
        return self.x_in[...].astype(F32)


def normalize(values):
    center = values - jnp.mean(values, axis=1, keepdims=True)
    spread = jnp.mean(center * center, axis=1, keepdims=True)
    scale = lax.rsqrt(spread + epsilon)
    return center * scale, scale


def norm_back(values, table, d_normed):
    normed, scale = normalize(values)
    dz = (1.0 + table[0:1, :]) * d_normed
    both = jnp.mean(dz * normed, axis=1, keepdims=True)
    d_values = (dz - jnp.mean(dz, axis=1, keepdims=True) - normed * both) * scale
    d_gain = jnp.sum(d_normed * normed, axis=0, keepdims=True)
    d_shift = jnp.sum(d_normed, axis=0, keepdims=True)
    return d_values, d_gain, d_shift


def layer_kernel(names, z_size, *refs):
    held = dict(zip(names, refs))
    held.update(
        d_mixed=held["act"],
        d_query=held["mixed"],
        d_branch=held["normed_ffn"],
        d_query_low=held["attn_t"],
        d_keys_low=held["keys_t"],
        d_values_low=held["values_t"],
        g_attn=held["g_down"],
    )
    n = collections.namedtuple("Buffers", held)(**held)
    k = Links(z_size, n.send_sem, n.recv_sem)
    mp_size, block, width = n.normed.shape
    seq = mp_size * block
    heads_wide = n.wa.shape[1]
    hidden = n.wf.shape[1]
    heads = heads_wide // HD
    q_wide = heads * block
    tile = block
    far = mp_size
    own_shard = 2 * k.x + k.core
    sib_shard = 2 * k.x + 1 - k.core
    x_shard = 2 * (1 - k.x) + k.core
    diag_shard = 2 * (1 - k.x) + 1 - k.core
    shards = (own_shard, sib_shard, x_shard, diag_shard)

    def mine(r):
        return 2 * r + k.core

    def theirs(r):
        return 2 * r + 1 - k.core

    def span(i, size=tile):
        return pl.ds(pl.multiple_of(i * size, size), size)

    fetches = []

    def fetch(src, dst):
        made = pltpu.make_async_copy(src, dst, n.load_sem.at[len(fetches)])
        made.start()
        fetches.append(made)
        return made

    load_tokens = fetch(n.tokens, n.raw.at[k.x])
    load_wa = fetch(n.w_attn, n.wa)
    load_cot = fetch(n.cotangent, n.cot.at[own_shard])
    load_wf = fetch(n.w_ffn, n.wf)

    def partner_of(row):
        begin, first, count = 0, 0, 1
        for g in range(n.group_sizes.shape[0]):
            size = n.group_sizes[g]
            inside = jnp.logical_and(row >= begin, row < begin + size)
            first = jnp.where(inside, begin, first)
            count = jnp.where(inside, size, count)
            begin = begin + size
        step = lax.rem(n.partner_pick[row], jnp.maximum(count - 1, 1))
        return jnp.clip(first + lax.rem(row - first + 1 + step, count), 0, 2 * z_size - 1)

    k.barrier()
    send_tokens = k.swap(n.tokens, n.raw.at[k.x], k.xpeer)
    send_tokens.start()
    cot_x = k.swap(n.cotangent, n.cot.at[own_shard], k.xpeer)
    cot_x.start()
    cot_sib = k.swap(n.cotangent, n.cot.at[own_shard], k.sib)
    cot_sib.start()

    code = n.codebook[k.dp]
    start = n.prompt_start[k.dp]
    partner = partner_of(k.dp)
    other_partner = partner_of(k.dp + 1 - 2 * k.y)
    part_z, part_y = partner // 2, lax.rem(partner, 2)
    line_partners = []
    for d in range(z_size):
        row = partner_of(2 * d + k.y)
        line_partners.append((row // 2 == k.z, lax.rem(row, 2) == k.y))
    other_z, other_y = other_partner // 2, lax.rem(other_partner, 2)
    far_len = n.prompt_len[partner]
    table_attn = n.ada_attn[code]
    table_ffn = n.ada_ffn[code]

    def adapt(normed, table):
        return ((1.0 + table[0:1, :]) * normed + table[1:2, :]).astype(BF16)

    def project(s):
        normed = n.normed[s]
        query = (dot(normed, n.wa[0], 1, 1) * HD ** (-0.5)).astype(BF16)
        lane = lax.broadcasted_iota(jnp.int32, (block, heads_wide), 1) // HD
        for h in range(heads):
            n.q4[s, h * block : (h + 1) * block, :] = jnp.where(lane == h, query, 0).astype(BF16)
        for ref, turned, w in ((n.keys, n.keys_t, 1), (n.values, n.values_t, 2)):
            made = dot(normed, n.wa[w], 1, 1)
            ref[s] = made.astype(BF16)
            turned[s] = made.T.astype(BF16)

    load_tokens.wait()
    n.normed[own_shard] = adapt(normalize(n.raw[k.x].astype(F32))[0], table_attn)
    normed_own = k.swap(n.normed.at[own_shard], n.normed.at[own_shard], k.sib)
    normed_own.start()
    load_wa.wait()
    normed_own.wait_recv()

    def project_pair(first):
        def body(i, carry):
            project(first + i)
            return carry

        lax.fori_loop(0, 2, body, 0)

    project_pair(2 * k.x)
    send_tokens.wait_recv()
    n.normed[x_shard] = adapt(normalize(n.raw[1 - k.x].astype(F32))[0], table_attn)
    normed_x = k.swap(n.normed.at[x_shard], n.normed.at[x_shard], k.sib)
    normed_x.start()
    normed_x.wait_recv()
    project_pair(2 * (1 - k.x))

    all_keys = n.keys[0:mp_size].reshape(seq, heads_wide)
    all_values = n.values[0:mp_size].reshape(seq, heads_wide)
    from_row = lax.broadcasted_iota(jnp.int32, (block, seq), 1)
    to_row = lax.broadcasted_iota(jnp.int32, (block, seq), 0)
    window = (from_row == to_row + start).astype(F32).astype(BF16)
    n.windows_k[k.z] = dot(window, all_keys).astype(BF16)
    gather = LineGather(k, n.windows_k)
    gather.start()
    n.y_out[1] = dot(window, all_values).astype(BF16)
    y_value = k.swap(n.y_out.at[1], n.y_in.at[1], k.ypeer)
    y_value.start()
    line_value = LineReduce(k, n.windows_v, n.passing_v)

    def attend_own(s, carry):
        q4 = n.q4[s]
        top = jnp.full((1, q_wide), -jnp.inf, F32)
        for c in range(mp_size):
            scores = dot(n.keys[c], q4, 1, 1)
            n.wide[c] = scores
            top = jnp.maximum(top, jnp.max(scores, axis=0, keepdims=True))
        total = jnp.zeros((1, q_wide), F32)
        for c in range(mp_size):
            prob = jnp.exp(n.wide[c] - top)
            total = total + jnp.sum(prob, axis=0, keepdims=True)
            low = prob.astype(BF16)
            for h in range(heads):
                rows = slice(h * HD, (h + 1) * HD)
                part = dot(n.values_t[c, rows, :], low[:, h * block : (h + 1) * block])
                n.mixed[s, rows, :] = part if c == 0 else n.mixed[s, rows, :] + part
        n.top[s] = top
        n.total[s] = total
        return carry

    def own(s):
        lax.fori_loop(s, s + 1, attend_own, 0)

    own(0)
    y_value.wait_recv()
    ours, others = n.y_out[1].astype(F32), n.y_in[1].astype(F32)
    for d in k.order:
        here, same_row = line_partners[d]
        chosen = jnp.where(same_row, ours, others)
        n.windows_v[d] = jnp.where(here, chosen, 0.0).astype(BF16)
        line_value.begin(d)
    gather.serve(1)
    own(1)
    line_value.step(1)
    gather.serve(2)
    own(2)
    line_value.step(2)
    gather.serve(3)
    n.y_out[0] = n.windows_k[other_z]
    y_key = k.swap(n.y_out.at[0], n.y_in.at[0], k.ypeer)
    y_key.start()
    own(3)

    cot_x.wait_recv()
    cot_pass = k.swap(n.cot.at[x_shard], n.cot.at[x_shard], k.sib)
    cot_pass.start()
    same_y = part_y == k.y

    def take_far(ref, turned):
        def store(rows):
            ref[far] = rows.astype(BF16)
            turned[far] = rows.T.astype(BF16)

        return store

    line_value.finish(take_far(n.values, n.values_t))
    y_key.wait_recv()
    far_keys = jnp.where(same_y, n.windows_k[part_z].astype(F32), n.y_in[0].astype(F32))
    take_far(n.keys, n.keys_t)(far_keys)

    def attend_far(s):
        scores = dot(n.keys[far], n.q4[s], 1, 1)
        slot = lax.broadcasted_iota(jnp.int32, scores.shape, 0)
        scores = jnp.where(slot < far_len, scores, -1000000000.0)
        top = jnp.maximum(n.top[s], jnp.max(scores, axis=0, keepdims=True))
        scale = jnp.exp(n.top[s] - top)
        prob = jnp.exp(scores - top)
        total = n.total[s] * scale + jnp.sum(prob, axis=0, keepdims=True)
        low = prob.astype(BF16)
        for h in range(heads):
            rows = slice(h * HD, (h + 1) * HD)
            cols = slice(h * block, (h + 1) * block)
            part = n.mixed[s, rows, :] * scale[:, cols] + dot(n.values_t[far, rows, :], low[:, cols])
            n.attn_t[s, rows, :] = (part / total[:, cols]).astype(BF16)
        n.log_total[s] = top + jnp.log(total)

    def out_part(s):
        attend_far(s)
        return dot(n.attn_t[s], n.wa[3], 0, 0)

    branch = Exchange(k, n.pair_out, n.pair_in, n.x_out, n.x_in)
    for r in range(2):
        branch.give(r, out_part(theirs(r)))
        branch.send_x(r, branch.pair_sum(r, out_part(mine(r))))

    back = Exchange(k, n.pair_out, n.pair_in, n.x_out2, n.x_in2)
    load_cot.wait()
    load_wf.wait()
    cot_sib.wait_recv()
    cot_pass.wait_recv()

    def hidden_part(s):
        normed = n.normed_ffn[s]
        cot = n.cot[s]

        def body(i, carry):
            cols = span(i)
            up = dot(normed, n.wf[0, cols, :], 1, 1)
            d_act = dot(cot, n.wf[1, cols, :], 1, 1)
            cdf = 0.5 + 0.5 * lax.erf(up * (0.5**0.5))
            n.act[s, :, cols] = (up * cdf).astype(BF16)
            slope = cdf + up * (jnp.exp(-0.5 * up * up) * (2.0 * jnp.pi) ** (-0.5))
            n.d_up[s, :, cols] = (slope * d_act).astype(BF16)
            return carry

        lax.fori_loop(0, hidden // tile, body, 0)
        return dot(n.d_up[s], n.wf[0])

    shares = []
    for r in range(2):
        middle = n.raw[r].astype(F32) + branch.total(r)
        n.wide[r] = middle
        n.normed_ffn[mine(r)] = adapt(normalize(middle)[0], table_ffn)
        share = k.swap(n.normed_ffn.at[mine(r)], n.normed_ffn.at[mine(r)], k.sib)
        share.start()
        shares.append(share)
        share.wait_recv()
        back.give(r, hidden_part(theirs(r)))
        back.send_x(r, back.pair_sum(r, hidden_part(mine(r))))

    grid_down = GridReduce(k, n.g_down, n.h_down, n.p_down)
    grid_up = GridReduce(k, n.g_up, n.h_up, n.p_up)

    def spread(target, rows, made):
        for d in range(target.shape[0]):
            target[d, rows, :] = made[:, d * LANES : (d + 1) * LANES].astype(BF16)

    def ffn_grads(target, left, right):
        def body(i, carry):
            lhs = left[:, :, span(i)].reshape(seq, tile)
            spread(target, span(i), dot(lhs, right[...].reshape(seq, width), 0, 0))
            return carry

        lax.fori_loop(0, hidden // tile, body, 0)

    ffn_grads(n.g_down, n.act, n.cot)
    grid_down.send_y(*k.order[:3])
    ffn_grads(n.g_up, n.d_up, n.normed_ffn)

    def down_part(s):
        return dot(n.act[s], n.wf[1])

    k.finish(branch.along_x[0])
    out_sum = Settle(branch, shards, n.x_out.at[0], n.s_in, down_part)
    n.kept[...] = out_sum.kept

    n.d_keys[...] = jnp.zeros_like(n.d_keys)
    n.d_values[...] = jnp.zeros_like(n.d_values)
    table_grad = [jnp.zeros((1, width), F32), jnp.zeros((1, width), F32)]

    def prepare(s):
        d_attn_t = dot(n.wa[3], n.d_branch[s], 1, 1).astype(BF16)
        row = lax.broadcasted_iota(jnp.int32, (heads_wide, block), 0) // HD
        product = d_attn_t.astype(F32) * n.attn_t[s].astype(F32)
        for h in range(heads):
            rows = slice(h * HD, (h + 1) * HD)
            cols = slice(h * block, (h + 1) * block)
            n.delta[s, :, cols] = jnp.sum(product[rows], axis=0, keepdims=True)
            n.d_mixed[s, :, cols] = jnp.where(row == h, d_attn_t, 0).astype(BF16)

    def attend_back(s, first, last):
        q4 = n.q4[s]
        d_mixed = n.d_mixed[s]

        def body(c, carry):
            scores = dot(n.keys[c], q4, 1, 1)
            slot = lax.broadcasted_iota(jnp.int32, scores.shape, 0)
            limit = jnp.where(c == far, far_len, block)
            prob = jnp.where(slot < limit, jnp.exp(scores - n.log_total[s]), 0.0)
            low = prob.astype(BF16)
            d_prob = dot(n.values[c], d_mixed)
            d_scores = (prob * (d_prob - n.delta[s])).astype(BF16)
            n.d_values[c] += dot(low, d_mixed, 1, 1)
            n.d_keys[c] += dot(d_scores, q4)
            for h in range(heads):
                rows = slice(h * HD, (h + 1) * HD)
                n.d_query[s, rows, :] += dot(
                    n.keys_t[c, rows, :], d_scores[:, h * block : (h + 1) * block]
                )
            return carry

        lax.fori_loop(first, last, body, 0)

    n.d_query[...] = jnp.zeros_like(n.d_query)
    for r in range(2):
        d_values, d_gain, d_shift = norm_back(n.wide[r], table_ffn, back.total(r))
        table_grad[0] = table_grad[0] + d_gain
        table_grad[1] = table_grad[1] + d_shift
        d_middle = n.cot[mine(r)].astype(F32) + d_values
        n.wide[2 + r] = d_middle
        k.finish(shares[r])
        n.d_branch[mine(r)] = d_middle.astype(BF16)
        share = k.swap(n.d_branch.at[mine(r)], n.d_branch.at[mine(r)], k.sib)
        share.start()
        share.wait_recv()

        def both(i, carry, r=r):
            prepare(2 * r + i)
            attend_back(2 * r + i, far, far + 1)
            return carry

        lax.fori_loop(0, 2, both, 0)
        if r == 0:
            grid_down.take(k.order[0])

    def table_blocks(target, gain, shift):
        row = lax.broadcasted_iota(jnp.int32, (n.t_ffn.shape[1], width), 0)
        both = jnp.where(lax.rem(row, 2) == 0, gain, shift)
        both = jnp.where(row // 2 == code, both, 0.0)
        for d in range(target.shape[0]):
            target[d] = both[:, d * LANES : (d + 1) * LANES]

    n.packets[k.z] = n.d_values[far].astype(BF16)
    packets = LineGather(k, n.packets)
    packets.start()
    k.finish(y_key)
    n.y_out[0] = jnp.where(same_y, 0.0, n.d_keys[far]).astype(BF16)
    y_key = k.swap(n.y_out.at[0], n.y_in.at[0], k.ypeer)
    y_key.start()
    table_blocks(n.t_ffn, table_grad[0], table_grad[1])
    grid_t_ffn = GridReduce(k, n.t_ffn, n.ht_ffn, n.pt_ffn)
    grid_t_ffn.send_y()
    grid_down.send_y(k.order[3])
    gather.wait_sends()
    line_key = LineReduce(k, n.windows_k, n.passing_k)

    def rest(s):
        def body(s, carry):
            attend_back(s, 0, mp_size)
            return carry

        lax.fori_loop(s, s + 1, body, 0)

    rest(0)
    packets.serve(1)
    y_key.wait_recv()
    back_grad = n.y_in[0].astype(F32)
    for d in k.order:
        here = jnp.where(jnp.logical_and(same_y, part_z == d), n.d_keys[far], 0.0)
        there = jnp.where(jnp.logical_and(other_y == k.y, other_z == d), back_grad, 0.0)
        n.windows_k[d] = (here + there).astype(BF16)
        line_key.begin(d)
    rest(1)
    packets.serve(2)
    line_key.step(1)
    rest(2)
    packets.serve(3)
    ours = jnp.zeros((block, heads_wide), F32)
    others = jnp.zeros((block, heads_wide), F32)
    for d in range(z_size):
        here, same_row = line_partners[d]
        packet = n.packets[d].astype(F32)
        ours = ours + jnp.where(jnp.logical_and(here, same_row), packet, 0.0)
        others = others + jnp.where(jnp.logical_and(here, jnp.logical_not(same_row)), packet, 0.0)
    k.finish(y_value)
    n.y_out[1] = others.astype(BF16)
    y_value = k.swap(n.y_out.at[1], n.y_in.at[1], k.ypeer)
    y_value.start()
    n.d_values[far] = ours
    line_key.step(2)
    grid_up.send_y(*k.order[:2])
    rest(3)
    grid_down.take(*k.order[1:])
    grid_down.wait_y()

    half_rows = 2 * heads_wide
    grid_oq = GridReduce(k, n.g_attn.at[:, 0:half_rows], n.h_oq, n.p_oq)
    grid_kv = GridReduce(k, n.g_attn.at[:, half_rows : 2 * half_rows], n.h_kv, n.p_kv)

    def add_products(left, right):
        total = dot(left[0], right[0])
        for s in range(1, mp_size):
            total = total + dot(left[s], right[s])
        return total

    spread(n.g_attn, slice(0, heads_wide), add_products(n.attn_t, n.d_branch))
    for s in range(mp_size):
        n.d_query_low[s] = (n.d_query[s] * HD ** (-0.5)).astype(BF16)
    spread(n.g_attn, slice(heads_wide, 2 * heads_wide), add_products(n.d_query_low, n.normed))

    def take_back(total):
        n.keys_t[far] = total.astype(BF16)

    line_key.finish(take_back)
    y_value.wait_recv()
    n.values_t[far] = (n.d_values[far] + n.y_in[1].astype(F32)).astype(BF16)
    from_slot = lax.broadcasted_iota(jnp.int32, (seq, block), 1)
    to_frame = lax.broadcasted_iota(jnp.int32, (seq, block), 0)
    unwindow = (to_frame == from_slot + start).astype(F32).astype(BF16)
    for ref, low in ((n.d_keys, n.d_keys_low), (n.d_values, n.d_values_low)):
        own = ref[0:mp_size].reshape(seq, heads_wide)
        total = own + dot(unwindow, low[far])
        low[0:mp_size] = total.astype(BF16).reshape(mp_size, block, heads_wide)

    flat_normed = n.normed[...].reshape(seq, width)
    for w, low in ((2, n.d_keys_low), (3, n.d_values_low)):
        made = dot(low[0:mp_size].reshape(seq, heads_wide), flat_normed, 0, 0)
        spread(n.g_attn, slice(w * heads_wide, (w + 1) * heads_wide), made)

    def input_part(s):
        return (
            dot(n.d_query_low[s], n.wa[0], 0, 0)
            + dot(n.d_keys_low[s], n.wa[1])
            + dot(n.d_values_low[s], n.wa[2])
        )

    k.finish(back.along_x[0])
    n.output[...] = (n.wide[k.x] + n.kept[...] + out_sum.total()).astype(BF16)
    in_sum = Settle(back, shards, n.x_out2.at[0], n.x_in.at[0], input_part)
    n.kept[...] = in_sum.kept

    table_grad = [jnp.zeros((1, width), F32), jnp.zeros((1, width), F32)]
    for term, at in ((n.x_out2[0].astype(F32), 1 - k.x), (in_sum.kept, k.x)):
        normed = normalize(n.raw[at].astype(F32))[0]
        table_grad[0] = table_grad[0] + jnp.sum(term * normed, axis=0, keepdims=True)
        table_grad[1] = table_grad[1] + jnp.sum(term, axis=0, keepdims=True)
    table_blocks(n.t_attn, *table_grad)
    grid_t_attn = GridReduce(k, n.t_attn, n.ht_attn, n.pt_attn)
    grid_t_attn.send_y()
    grid_kv.send_y()
    grid_up.send_y(*k.order[2:])
    grid_oq.send_y()
    grid_t_ffn.take()
    grid_down.step()
    grid_t_ffn.step()
    grid_up.take(*k.order[:2])

    quarter = heads_wide

    def store_ffn(s):
        def store(total):
            n.grad_ffn[pl.ds(s, hidden, stride=2), :] = total

        return store

    def store_attn(*places):
        def store(total):
            for i, s in enumerate(places):
                at = pl.ds(s, quarter, stride=4)
                rows = total[i * quarter : (i + 1) * quarter]
                n.grad_attn[at, :] = rows

        return store

    d_values, _, _ = norm_back(n.raw[k.x].astype(F32), table_attn, n.kept[...] + in_sum.total())
    n.grad_tokens[...] = (n.wide[2 + k.x] + d_values).astype(BF16)
    grid_t_attn.take()
    grid_kv.take()
    grid_down.finish(store_ffn(1))
    grid_t_attn.step()
    grid_kv.step()

    def store_table(over_x):
        def store(total):
            n.t_out[over_x, 0] = total
            pair = k.swap(n.t_out.at[over_x, 0], n.t_in.at[over_x, 0], k.sib)
            pair.start()
            pair.wait_recv()
            total = total + n.t_in[over_x, 0]
            if over_x:
                n.t_out[over_x, 1] = total
                along = k.swap(n.t_out.at[over_x, 1], n.t_in.at[over_x, 1], k.xpeer)
                along.start()
                along.wait_recv()
                total = total + n.t_in[over_x, 1]
            piece = LANES // mp_size
            kept = total
            for m in range(1, mp_size):
                turned = pltpu.roll(total, LANES - m * piece, 1)
                kept = jnp.where(k.mp == m, turned, kept)
            n.grad_ada[over_x] = kept

        return store

    grid_t_ffn.finish(store_table(0))
    grid_up.take(*k.order[2:])
    grid_up.step()
    grid_t_attn.finish(store_table(1))
    grid_kv.finish(store_attn(1, 2))
    grid_oq.take()
    grid_up.finish(store_ffn(0))
    grid_oq.step()
    grid_oq.finish(store_attn(3, 0))
    k.finish()
    packets.wait_sends()
    for unit in (line_value, line_key):
        unit.wait_sends()
    for unit in (grid_down, grid_up, grid_oq, grid_kv, grid_t_ffn, grid_t_attn):
        unit.wait_sends()
        if unit is not grid_down:
            unit.wait_y()


def layer(tokens, cotangent, w_attn, w_ffn, ada_attn, ada_ffn, ints, dp_size, mp_size):
    z_size = dp_size // 2
    block, width = tokens.shape
    heads_wide = w_attn.shape[1]
    hidden = w_ffn.shape[1]
    heads = heads_wide // HD
    table_rows = ada_attn.shape[0] * 2
    lane_block = width // dp_size

    inputs = dict(
        tokens=tokens,
        cotangent=cotangent,
        w_attn=w_attn,
        w_ffn=w_ffn,
        ada_attn=ada_attn,
        ada_ffn=ada_ffn,
        **ints,
    )
    spaces = dict.fromkeys(("tokens", "cotangent", "w_attn", "w_ffn"), pl.ANY)
    spaces.update(dict.fromkeys(ints, pltpu.SMEM))
    outputs = dict(
        output=((block, width), BF16),
        grad_tokens=((block, width), BF16),
        grad_attn=((4 * heads_wide, lane_block), F32),
        grad_ffn=((2 * hidden, lane_block), F32),
        grad_ada=((2, table_rows, lane_block), F32),
    )
    wide = (mp_size, block, width)
    two = (2, block, width)
    square = (mp_size + 1, block, heads_wide)
    low, full = {}, {}
    for name in ("normed", "cot", "normed_ffn", "act", "d_up"):
        low[name] = wide
    low.update(raw=two, wa=w_attn.shape, wf=w_ffn.shape)
    for name in ("keys", "values", "keys_t", "values_t"):
        low[name] = square
    low.update(q4=(mp_size, heads * block, heads_wide), attn_t=(mp_size, heads_wide, block))
    for name in ("pair_out", "pair_in", "x_out", "x_in", "x_out2", "x_in2"):
        low[name] = two
    low.update(s_in=(block, width))
    for name in ("y_out", "y_in"):
        low[name] = (2, block, heads_wide)
    for name in ("k", "v"):
        low["windows_" + name] = (z_size, block, heads_wide)
        low["passing_" + name] = (z_size + 1, block, heads_wide)
    for name in ("up", "down"):
        low["g_" + name] = (dp_size, hidden, lane_block)
    half = 2 * heads_wide
    low.update(packets=(z_size, block, heads_wide))
    for name, rows in (("up", hidden), ("down", hidden), ("oq", half), ("kv", half)):
        low["h_" + name] = (z_size, rows, lane_block)
        low["p_" + name] = (z_size, rows, lane_block)
    for name in ("_ffn", "_attn"):
        full["t" + name] = (dp_size, table_rows, lane_block)
        full["ht" + name] = (z_size, table_rows, lane_block)
        full["pt" + name] = (z_size, table_rows, lane_block)
    full.update(t_out=(2, 2, table_rows, lane_block), t_in=(2, 2, table_rows, lane_block))
    full.update(wide=(mp_size, block, heads * block), kept=(block, width))
    for name in ("top", "total", "log_total", "delta"):
        full[name] = (mp_size, 1, heads * block)
    full.update(mixed=(mp_size, heads_wide, block))
    full.update(d_keys=square, d_values=square)
    scratch = {name: pltpu.VMEM(shape, BF16) for name, shape in low.items()}
    scratch.update({name: pltpu.VMEM(shape, F32) for name, shape in full.items()})
    copies = 200
    scratch.update(
        load_sem=pltpu.SemaphoreType.DMA((4,)),
        send_sem=pltpu.SemaphoreType.DMA((copies,)),
        recv_sem=pltpu.SemaphoreType.DMA((copies,)),
    )
    names = tuple(inputs) + tuple(outputs) + tuple(scratch)
    return pl.pallas_call(
        functools.partial(layer_kernel, names, z_size),
        out_shape=tuple(jax.ShapeDtypeStruct(*shape) for shape in outputs.values()),
        in_specs=[pl.BlockSpec(memory_space=spaces.get(name, pltpu.VMEM)) for name in inputs],
        out_specs=[pl.BlockSpec(memory_space=pltpu.VMEM) for _ in outputs],
        scratch_shapes=list(scratch.values()),
        compiler_params=pltpu.CompilerParams(
            collective_id=1, has_side_effects=True, vmem_limit_bytes=60 << 20
        ),
    )(*inputs.values())


def place_kernel(count, *refs):
    moves = []
    for i in range(count):
        moves.append(pltpu.make_async_copy(refs[i], refs[count + i], refs[-1].at[i]))
        moves[i].start()
    for move in moves:
        move.wait()


def place(arrays):
    return pl.pallas_call(
        functools.partial(place_kernel, len(arrays)),
        out_shape=tuple(jax.ShapeDtypeStruct(a.shape, a.dtype) for a in arrays),
        in_specs=[pl.BlockSpec(memory_space=pltpu.VMEM)] * len(arrays),
        out_specs=[pl.BlockSpec(memory_space=pl.ANY)] * len(arrays),
        scratch_shapes=[pltpu.SemaphoreType.DMA((len(arrays),))],
    )(*arrays)


def shards(
    tokens,
    w_attn,
    w_ffn,
    ada_attn,
    ada_ffn,
    codebook,
    group_sizes,
    partner_pick,
    prompt_start,
    prompt_len,
    cotangent,
):
    tok_rows, width = tokens.shape
    mp_size = lax.axis_size("mp")
    dp_index = lax.axis_index("dp")
    mp_index = lax.axis_index("mp")
    block_tokens = tok_rows * mp_size
    seq_here = block_tokens // LEN
    head_cols = w_attn.shape[0]
    heads_here = head_cols // HD
    total_rows = codebook.shape[0]
    dp_size = lax.axis_size("dp")
    fits = width == dp_size * LANES and width == w_ffn.shape[0] == tok_rows * heads_here
    if seq_here == 1 and mp_size == 4 and fits and tok_rows == PMAX:
        ints = dict(
            codebook=codebook,
            group_sizes=group_sizes,
            partner_pick=partner_pick,
            prompt_start=prompt_start,
            prompt_len=prompt_len,
        )
        results = layer(
            tokens,
            cotangent,
            jnp.swapaxes(w_attn, 0, 1),
            jnp.swapaxes(w_ffn, 0, 1),
            ada_attn,
            ada_ffn,
            ints,
            dp_size,
            mp_size,
        )
        output, grad_tokens, grad_attn, grad_ffn = place(results[:4])
        grad_ada = results[4]
        grad_ada = grad_ada[:, :, : width // (dp_size * mp_size)]
        grad_ada = grad_ada.reshape((2,) + ada_attn.shape[:2] + grad_ada.shape[2:])
        return (
            output,
            grad_tokens,
            grad_attn.reshape(head_cols, 4, LANES),
            grad_ffn.reshape(w_ffn.shape[0], 2, LANES),
            grad_ada[1],
            grad_ada[0],
        )
    partner = partner_rows(group_sizes, partner_pick)
    first_row = dp_index * seq_here
    tok_global = (dp_index * mp_size + mp_index) * tok_rows + jnp.arange(tok_rows, dtype=jnp.int32)
    row_pick = (
        (tok_global // LEN)[:, None] == jnp.arange(total_rows, dtype=jnp.int32)[None, :]
    ).astype(jnp.int32)
    token_codes = jnp.sum(row_pick * codebook[None, :], axis=1)
    code_hot = (
        token_codes[:, None] == jnp.arange(ada_attn.shape[0], dtype=jnp.int32)[None, :]
    ).astype(jnp.float32)
    my_partner = lax.dynamic_slice_in_dim(partner, first_row, seq_here)
    my_starts = lax.dynamic_slice_in_dim(prompt_start, first_row, seq_here)
    partner_hot = (my_partner[:, None] == jnp.arange(total_rows, dtype=jnp.int32)[None, :]).astype(
        jnp.int32
    )
    partner_len = jnp.sum(partner_hot * prompt_len[None, :], axis=1)
    far_valid = jnp.arange(PMAX, dtype=jnp.int32)[None, :] < partner_len[:, None]
    inputs = tokens.astype(jnp.float32)
    normed_attn = adaptive_norm(inputs, ada_attn, code_hot).astype(jnp.bfloat16)
    normed_attn_full = lax.all_gather(normed_attn, "mp", axis=0, tiled=True)
    w_qkv = w_attn[:, 0:3, :]
    w_out = w_attn[:, 3, :]
    qkv_low = jnp.einsum(
        "td,jsd->tsj", normed_attn_full, w_qkv, preferred_element_type=jnp.float32
    ).astype(jnp.bfloat16)
    kv_rows = qkv_low[:, 1:3, :].reshape(seq_here, LEN, 2 * head_cols)
    windows = jax.vmap(
        lambda sequence, offset: lax.dynamic_slice_in_dim(sequence, offset, PMAX, 0)
    )(kv_rows, my_starts)
    shard_rows = lax.all_gather(windows, "dp", axis=0, tiled=True)
    row_ids = jnp.arange(shard_rows.shape[0], dtype=jnp.int32)
    picker = (my_partner[:, None] == row_ids[None, :]).astype(jnp.bfloat16)
    prompt_sum = jnp.einsum("kr,rpc->kpc", picker, shard_rows, preferred_element_type=jnp.float32)
    prompt_kv = prompt_sum.astype(jnp.bfloat16)
    queries = qkv_low[:, 0, :].reshape(seq_here, LEN, heads_here, HD)
    own_keys = qkv_low[:, 1, :].reshape(seq_here, LEN, heads_here, HD)
    own_values = qkv_low[:, 2, :].reshape(seq_here, LEN, heads_here, HD)
    far_keys = prompt_kv[:, :, :head_cols].reshape(seq_here, PMAX, heads_here, HD)
    far_values = prompt_kv[:, :, head_cols:].reshape(seq_here, PMAX, heads_here, HD)
    attended, log_total = lax.map(
        attend, (queries, own_keys, own_values, far_keys, far_values, far_valid)
    )
    attn_flat = attended.reshape(block_tokens, head_cols)
    middle = inputs + lax.psum_scatter(
        jnp.dot(attn_flat, w_out, preferred_element_type=jnp.float32).astype(jnp.bfloat16),
        "mp",
        scatter_dimension=0,
        tiled=True,
    ).astype(jnp.float32)
    normed_ffn = adaptive_norm(middle, ada_ffn, code_hot).astype(jnp.bfloat16)
    normed_ffn_full = lax.all_gather(normed_ffn, "mp", axis=0, tiled=True)
    w_up = w_ffn[:, 0, :]
    w_down = w_ffn[:, 1, :]
    up_proj = inner_cols(normed_ffn_full, w_up)
    activated = jax.nn.gelu(up_proj, approximate=False).astype(jnp.bfloat16)
    output = (
        middle
        + lax.psum_scatter(
            jnp.dot(activated, w_down, preferred_element_type=jnp.float32).astype(jnp.bfloat16),
            "mp",
            scatter_dimension=0,
            tiled=True,
        ).astype(jnp.float32)
    ).astype(jnp.bfloat16)
    shard_rows = lax.all_gather(cotangent, "mp", axis=0, tiled=True)
    rows_grad = inner_cols(shard_rows, w_down)
    d_act = rows_grad
    grad_down = inner_rows(activated, shard_rows)
    _, gelu_pull = jax.vjp(lambda values: jax.nn.gelu(values, approximate=False), up_proj)
    d_up = gelu_pull(d_act)[0].astype(jnp.bfloat16)
    d_normed_ffn = lax.psum_scatter(
        jnp.dot(d_up, w_up, preferred_element_type=jnp.float32).astype(jnp.bfloat16),
        "mp",
        scatter_dimension=0,
        tiled=True,
    ).astype(jnp.float32)
    grad_up = inner_rows(d_up, lax.all_gather(normed_ffn, "mp", axis=0, tiled=True))
    _, norm_ffn_pull = jax.vjp(
        lambda values, table: adaptive_norm(values, table, code_hot), middle, ada_ffn
    )
    d_middle_norm, grad_table_ffn = norm_ffn_pull(d_normed_ffn)
    d_middle = cotangent.astype(jnp.float32) + d_middle_norm
    d_branch = d_middle.astype(jnp.bfloat16)
    shard_rows = lax.all_gather(d_branch, "mp", axis=0, tiled=True)
    rows_grad = inner_cols(shard_rows, w_out)
    grad_out_proj = inner_rows(attn_flat, shard_rows)
    d_mixed = rows_grad.astype(jnp.bfloat16).reshape(seq_here, LEN, heads_here, HD)
    d_queries, d_own_keys, d_own_values, d_far_keys, d_far_values = lax.map(
        attend_back,
        (queries, own_keys, own_values, far_keys, far_values, far_valid, log_total, d_mixed),
    )
    prompt_grad = jnp.concatenate(
        [
            d_far_keys.reshape(seq_here, PMAX, head_cols),
            d_far_values.reshape(seq_here, PMAX, head_cols),
        ],
        axis=2,
    )
    row_ids = jnp.arange(lax.axis_size("dp") * seq_here, dtype=jnp.int32)
    picker = (my_partner[:, None] == row_ids[None, :]).astype(jnp.float32)
    returned_kv = lax.psum_scatter(
        jnp.einsum("kr,kpc->rpc", picker, prompt_grad, precision=highest).astype(jnp.bfloat16),
        "dp",
        scatter_dimension=0,
        tiled=True,
    ).astype(jnp.float32)
    d_kv_rows = jnp.concatenate(
        [
            d_own_keys.reshape(seq_here, LEN, head_cols),
            d_own_values.reshape(seq_here, LEN, head_cols),
        ],
        axis=2,
    )
    d_kv_rows = jax.vmap(
        lambda sequence, window, offset: lax.dynamic_update_slice_in_dim(
            sequence, lax.dynamic_slice_in_dim(sequence, offset, PMAX, 0) + window, offset, 0
        )
    )(d_kv_rows, returned_kv, my_starts)
    d_qkv = jnp.stack(
        [
            d_queries.reshape(block_tokens, head_cols),
            d_kv_rows[:, :, :head_cols].reshape(block_tokens, head_cols),
            d_kv_rows[:, :, head_cols:].reshape(block_tokens, head_cols),
        ],
        axis=1,
    ).astype(jnp.bfloat16)
    d_normed_attn = lax.psum_scatter(
        jnp.einsum("tsj,jsd->td", d_qkv, w_qkv, preferred_element_type=jnp.float32).astype(
            jnp.bfloat16
        ),
        "mp",
        scatter_dimension=0,
        tiled=True,
    ).astype(jnp.float32)
    grad_qkv = jnp.einsum(
        "tsj,td->jsd",
        d_qkv,
        lax.all_gather(normed_attn, "mp", axis=0, tiled=True),
        preferred_element_type=jnp.float32,
    )
    _, norm_attn_pull = jax.vjp(
        lambda values, table: adaptive_norm(values, table, code_hot), inputs, ada_attn
    )
    d_inputs_norm, grad_table_attn = norm_attn_pull(d_normed_attn)
    grad_tokens = (d_middle + d_inputs_norm).astype(jnp.bfloat16)
    grad_attn_local = jnp.concatenate([grad_qkv, grad_out_proj[:, None, :]], axis=1)
    grad_ffn_local = jnp.stack([grad_up, grad_down], axis=1)
    grad_attn, grad_ffn = (
        lax.psum_scatter(
            grad_attn_local.astype(jnp.bfloat16), "dp", scatter_dimension=2, tiled=True
        ).astype(jnp.float32),
        lax.psum_scatter(
            grad_ffn_local.astype(jnp.bfloat16), "dp", scatter_dimension=2, tiled=True
        ).astype(jnp.float32),
    )
    grad_ada_attn, grad_ada_ffn = (
        lax.psum_scatter(grad_table_attn, ("dp", "mp"), scatter_dimension=2, tiled=True),
        lax.psum_scatter(grad_table_ffn, ("dp", "mp"), scatter_dimension=2, tiled=True),
    )
    return (output, grad_tokens, grad_attn, grad_ffn, grad_ada_attn, grad_ada_ffn)


def solution(mesh):
    in_specs = (
        P(("dp", "mp"), None),
        P("mp", None, None),
        P("mp", None, None),
        P(),
        P(),
        P(),
        P(),
        P(),
        P(),
        P(),
        P(("dp", "mp"), None),
    )
    out_specs = (
        P(("dp", "mp"), None),
        P(("dp", "mp"), None),
        P("mp", None, "dp"),
        P("mp", None, "dp"),
        P(None, None, ("dp", "mp")),
        P(None, None, ("dp", "mp")),
    )
    return jax.shard_map(shards, mesh=mesh, in_specs=in_specs, out_specs=out_specs, check_vma=False)
```

```python
import collections
import functools

import jax
import jax.numpy as jnp
from jax import lax
from jax.experimental import pallas as pl
from jax.experimental.pallas import tpu as pltpu
from jax.sharding import PartitionSpec as P

HD = 64
LEN = 1024
PMAX = 256


epsilon = 1e-05
highest = lax.Precision.HIGHEST


def partner_rows(group_sizes, partner_pick):
    group_end = jnp.cumsum(group_sizes)
    begins = group_end - group_sizes
    row_ids = jnp.arange(partner_pick.shape[0], dtype=jnp.int32)
    owner_group = jnp.sum((group_end[None, :] <= row_ids[:, None]).astype(jnp.int32), axis=1)
    member = (
        owner_group[:, None] == jnp.arange(group_sizes.shape[0], dtype=jnp.int32)[None, :]
    ).astype(jnp.int32)
    first_row = jnp.sum(member * begins[None, :], axis=1)
    group_len = jnp.sum(member * group_sizes[None, :], axis=1)
    span_size = jnp.maximum(group_len - 1, 1)
    return first_row + (row_ids - first_row + 1 + partner_pick % span_size) % group_len


def adaptive_norm(inputs, table, code_hot):
    coefficients = jnp.dot(code_hot, table.reshape(table.shape[0], -1), precision=highest)
    coefficients = coefficients.reshape(inputs.shape[0], 2, inputs.shape[1])
    center = inputs - jnp.mean(inputs, axis=-1, keepdims=True)
    spread = jnp.mean(center * center, axis=-1, keepdims=True)
    normed = center * lax.rsqrt(spread + epsilon)
    return (1.0 + coefficients[:, 0, :]) * normed + coefficients[:, 1, :]


def inner_rows(left, right):
    return lax.dot_general(
        left, right, (((0,), (0,)), ((), ())), preferred_element_type=jnp.float32
    )


def inner_cols(left, right):
    return lax.dot_general(
        left, right, (((1,), (1,)), ((), ())), preferred_element_type=jnp.float32
    )


def row_scores(queries, key_rows, far_valid):
    key_mask = jnp.concatenate([jnp.ones((queries.shape[0],), dtype=jnp.bool_), far_valid])
    scores = jnp.einsum(
        "qhd,khd->hqk", queries, key_rows, preferred_element_type=jnp.float32
    ) * HD ** (-0.5)
    return jnp.where(key_mask[None, None, :], scores, -1000000000.0)


def attend(packed):
    queries, own_keys, own_values, far_keys, far_values, far_valid = packed
    key_rows = jnp.concatenate([own_keys, far_keys], axis=0)
    value_rows = jnp.concatenate([own_values, far_values], axis=0)
    scores = row_scores(queries, key_rows, far_valid)
    row_max = jnp.max(scores, axis=-1, keepdims=True)
    log_total = row_max + jnp.log(jnp.sum(jnp.exp(scores - row_max), axis=-1, keepdims=True))
    prob_low = jnp.exp(scores - log_total).astype(jnp.bfloat16)
    mixed = jnp.einsum("hqk,khd->qhd", prob_low, value_rows, preferred_element_type=jnp.float32)
    return (mixed.astype(jnp.bfloat16), log_total)


def attend_back(packed):
    queries, own_keys, own_values, far_keys, far_values, far_valid, log_total, d_mixed = packed
    key_rows = jnp.concatenate([own_keys, far_keys], axis=0)
    value_rows = jnp.concatenate([own_values, far_values], axis=0)
    scores = row_scores(queries, key_rows, far_valid)
    attn_prob = jnp.exp(scores - log_total)
    prob_low = attn_prob.astype(jnp.bfloat16)
    d_values = jnp.einsum("hqk,qhd->khd", prob_low, d_mixed, preferred_element_type=jnp.float32)
    d_prob = jnp.einsum("qhd,khd->hqk", d_mixed, value_rows, preferred_element_type=jnp.float32)
    row_delta = jnp.sum(attn_prob * d_prob, axis=-1, keepdims=True)
    d_scores = (attn_prob * (d_prob - row_delta)).astype(jnp.bfloat16)
    d_queries = jnp.einsum(
        "hqk,khd->qhd", d_scores, key_rows, preferred_element_type=jnp.float32
    ) * HD ** (-0.5)
    d_keys = jnp.einsum(
        "hqk,qhd->khd", d_scores, queries, preferred_element_type=jnp.float32
    ) * HD ** (-0.5)
    own_len = queries.shape[0]
    return (d_queries, d_keys[:own_len], d_values[:own_len], d_keys[own_len:], d_values[own_len:])


MESH = pl.DeviceIdType.MESH
F32 = jnp.float32
BF16 = jnp.bfloat16
LANES = 128


def dot(left, right, left_dim=1, right_dim=0):
    return lax.dot_general(
        left, right, (((left_dim,), (right_dim,)), ((), ())), preferred_element_type=F32
    )


class Links:
    def __init__(self, z_size, send_sem, recv_sem):
        self.dp = lax.axis_index("dp")
        self.mp = lax.axis_index("mp")
        self.z_size = z_size
        self.order = (z_size - 1, 0) + tuple(range(1, z_size - 1))
        self.y = lax.rem(self.dp, 2)
        self.z = self.dp // 2
        self.core = lax.rem(self.mp, 2)
        self.x = self.mp // 2
        self.sib = (self.dp, self.mp + 1 - 2 * self.core)
        self.xpeer = (self.dp, self.mp + 2 - 4 * self.x)
        self.ypeer = (self.dp + 1 - 2 * self.y, self.mp)
        self.right = (self.dp + 2, self.mp)
        self.left = (self.dp - 2, self.mp)
        self.send_sem = send_sem
        self.recv_sem = recv_sem
        self.used = 0
        self.sent = []
        self.pair_sends = {}

    def take(self, count=1):
        first = self.used
        self.used += count
        return first

    def copy(self, src, dst, number, device, landing=None):
        return pltpu.make_async_remote_copy(
            src_ref=src,
            dst_ref=dst,
            send_sem=self.send_sem.at[number],
            recv_sem=self.recv_sem.at[number if landing is None else landing],
            device_id=device,
            device_id_type=MESH,
        )

    def swap(self, src, dst, device):
        made = self.copy(src, dst, self.take(), device)
        self.sent.append(made)
        return made

    def finish(self, made=None):
        for one in list(self.sent):
            if made is None or one is made:
                one.wait_send()
        self.sent = [one for one in self.sent if made is not None and one is not made]

    def barrier(self):
        bar = pltpu.get_barrier_semaphore()
        for device in (self.sib, self.xpeer, self.ypeer):
            pl.semaphore_signal(bar, inc=1, device_id=device, device_id_type=MESH)

        @pl.when(self.z > 0)
        def _():
            pl.semaphore_signal(bar, inc=1, device_id=self.left, device_id_type=MESH)

        @pl.when(self.z < self.z_size - 1)
        def _():
            pl.semaphore_signal(bar, inc=1, device_id=self.right, device_id_type=MESH)

        inner = (self.z > 0).astype(jnp.int32) + (self.z < self.z_size - 1).astype(jnp.int32)
        pl.semaphore_wait(bar, 3 + inner)


class LineReduce:
    def __init__(self, links, held, passing):
        self.setup(links, held, passing)

    def setup(self, links, held, passing):
        self.k = links
        self.held, self.passing = held, passing
        self.nr = links.take(links.z_size)
        self.nl = links.take(links.z_size)

    def z_copy(self, d, rightward):
        k = self.k
        if rightward:
            return k.copy(self.held.at[d], self.passing.at[d], self.nr + d, k.right)
        landing = jnp.where(k.z - 1 == d, k.z_size, d)
        return k.copy(self.held.at[d], self.passing.at[landing], self.nl + d, k.left)

    def add(self, d):
        total = self.held[d].astype(F32) + self.passing[d].astype(F32)
        self.held[d] = total.astype(self.held.dtype)

    def begin(self, d):
        k = self.k
        last = k.z_size - 1
        if d > 0:

            @pl.when(k.z == 0)
            def _():
                self.z_copy(d, True).start()

        if d < last:

            @pl.when(k.z == last)
            def _():
                self.z_copy(d, False).start()

    def step(self, i):
        k = self.k
        n = k.z_size

        @pl.when(k.z == i)
        def _():
            for d in range(n - 1, i, -1):
                self.z_copy(d, True).wait_recv()
                self.add(d)
                self.z_copy(d, True).start()

        @pl.when(k.z == n - 1 - i)
        def _():
            for d in range(n - 1 - i):
                self.z_copy(d, False).wait_recv()
                self.add(d)
                self.z_copy(d, False).start()

    def finish(self, store):
        k = self.k
        n = k.z_size

        @pl.when(k.z > 0)
        def _():
            k.copy(self.held.at[k.z], self.passing.at[k.z], self.nr + k.z, k.left).wait_recv()

        @pl.when(k.z < n - 1)
        def _():
            k.copy(self.held.at[k.z], self.passing.at[n], self.nl + k.z, k.right).wait_recv()

        total = self.held[k.z].astype(F32)
        from_left = jnp.where(k.z > 0, self.passing[k.z].astype(F32), 0.0)
        from_right = jnp.where(k.z < n - 1, self.passing[n].astype(F32), 0.0)
        store(total + from_left + from_right)

    def wait_sends(self):
        k = self.k
        for d in range(k.z_size):

            @pl.when(k.z < d)
            def _(d=d):
                self.z_copy(d, True).wait_send()

            @pl.when(k.z > d)
            def _(d=d):
                self.z_copy(d, False).wait_send()


class GridReduce:
    def __init__(self, links, local, held, passing):
        n = links.z_size
        self.k = links
        self.local, self.held, self.passing = local, held, passing
        self.ny, self.ns, self.nr = links.take(n), links.take(n), links.take(n)
        self.inner = {n - 1: 1, 0: n - 2}

    def part(self, d):
        return self.held.at[d]

    def y_copy(self, d):
        k = self.k
        other = 2 * d + 1 - k.y
        return k.copy(self.local.at[other], self.held.at[d], self.ny + d, k.ypeer)

    def send_y(self, *dests):
        for d in dests or self.k.order:
            self.y_copy(d).start()

    def z_copy(self, d):
        k = self.k
        to = d
        if d in self.inner:
            to = jnp.where(k.z == k.z_size - 1 - d, self.inner[d], d)
        slot = jnp.where(to == d, k.z, to)
        device = (2 * to + k.y, k.mp)
        return k.copy(self.part(d), self.passing.at[slot], self.ns + d, device, self.nr + slot)

    def landed(self, slot):
        self.k.copy(self.part(0), self.passing.at[slot], self.ns, self.k.ypeer, self.nr + slot).wait_recv()

    def take(self, *dests):
        k = self.k
        for d in dests or k.order:
            self.y_copy(d).wait_recv()
            total = self.local[2 * d + k.y].astype(F32) + self.held[d].astype(F32)
            self.held[d] = total.astype(self.held.dtype)
            self.send_z(d)

    def send_z(self, d):
        ready = self.k.z != d
        if d in self.inner:
            ready = jnp.logical_and(ready, self.k.z != self.inner[d])

        @pl.when(ready)
        def _():
            self.z_copy(d).start()

    def step(self):
        for d, at in self.inner.items():

            @pl.when(self.k.z == at)
            def _(d=d, at=at):
                self.landed(at)
                part = self.part(d)
                part[...] = (part[...].astype(F32) + self.passing[at].astype(F32)).astype(part.dtype)
                self.z_copy(d).start()

    def finish(self, store):
        k = self.k
        n = k.z_size
        total = self.part(k.z)[...].astype(F32)
        for source in range(n):
            apart = jnp.abs(k.z - source)
            sends = jnp.logical_and(apart != 0, apart != n - 1)

            @pl.when(sends)
            def _(source=source):
                self.landed(source)

            total = total + jnp.where(sends, self.passing[source].astype(F32), 0.0)
        store(total)

    def wait_sends(self):
        for d in range(self.k.z_size):

            @pl.when(self.k.z != d)
            def _(d=d):
                self.z_copy(d).wait_send()

    def wait_y(self):
        for d in range(self.k.z_size):
            self.y_copy(d).wait_send()


class GridReduceZ(GridReduce):
    def __init__(self, links, local, rows, passing, y_out, y_in):
        n = links.z_size
        self.k = links
        self.local, self.rows, self.passing = local, rows, passing
        self.ns, self.nr = links.take(n), links.take(n)
        self.inner = {n - 1: 1, 0: n - 2}
        self.y_out, self.y_in = y_out, y_in

    def part(self, d):
        return self.local.at[pl.ds(2 * d, 2), self.rows]

    def start(self):
        for d in self.k.order:
            self.send_z(d)

    def turn(self, store):
        k = self.k

        def split(total):
            low = k.y == 0
            store(jnp.where(low, total[0], total[1]))
            self.y_out[...] = jnp.where(low, total[1], total[0]).astype(BF16)

        self.finish(split)
        self.along_y = k.swap(self.y_out, self.y_in, k.ypeer)
        self.along_y.start()

    def done(self, add):
        self.along_y.wait_recv()
        add(self.y_in[...].astype(F32))


class LineGather:
    def __init__(self, links, slots):
        self.k = links
        self.slots = slots
        self.nr = links.take(links.z_size)
        self.nl = links.take(links.z_size)

    def z_copy(self, slot, rightward):
        k = self.k
        number = (self.nr if rightward else self.nl) + slot
        place = self.slots.at[slot]
        return k.copy(place, place, number, k.right if rightward else k.left)

    def start(self):
        k = self.k

        @pl.when(k.z < k.z_size - 1)
        def _():
            self.z_copy(k.z, True).start()

        @pl.when(k.z > 0)
        def _():
            self.z_copy(k.z, False).start()

    def serve(self, distance):
        k = self.k

        @pl.when(k.z >= distance)
        def _():
            self.z_copy(k.z - distance, True).wait_recv()

            @pl.when(k.z < k.z_size - 1)
            def _():
                self.z_copy(k.z - distance, True).start()

        @pl.when(k.z + distance < k.z_size)
        def _():
            self.z_copy(k.z + distance, False).wait_recv()

            @pl.when(k.z > 0)
            def _():
                self.z_copy(k.z + distance, False).start()

    def wait_sends(self):
        k = self.k
        for slot in range(k.z_size):

            @pl.when(jnp.logical_and(k.z >= slot, k.z < k.z_size - 1))
            def _(slot=slot):
                self.z_copy(slot, True).wait_send()

            @pl.when(jnp.logical_and(k.z <= slot, k.z > 0))
            def _(slot=slot):
                self.z_copy(slot, False).wait_send()


class Exchange:
    def __init__(self, links, pair_out, pair_in, x_out, x_in):
        self.k = links
        self.pair_out, self.pair_in, self.x_out, self.x_in = pair_out, pair_in, x_out, x_in
        self.pair = {}
        self.along_x = {}

    def give(self, r, term, slot=None):
        slot = r if slot is None else slot
        if slot in self.k.pair_sends:
            self.k.finish(self.k.pair_sends[slot])
        self.pair_out[slot] = term.astype(BF16)
        made = self.k.swap(self.pair_out.at[slot], self.pair_in.at[slot], self.k.sib)
        made.start()
        self.k.pair_sends[slot] = made
        self.pair[r] = (made, slot)

    def pair_sum(self, r, term):
        made, slot = self.pair[r]
        made.wait_recv()
        return term + self.pair_in[slot].astype(F32)

    def send_x(self, r, total):
        self.x_out[r] = total.astype(BF16)
        made = self.k.swap(self.x_out.at[r], self.x_in.at[r], self.k.xpeer)
        made.start()
        self.along_x[r] = made

    def total(self, r):
        self.along_x[r].wait_recv()
        return self.x_out[r].astype(F32) + self.x_in[r].astype(F32)


class Settle:
    def __init__(self, exchange, shards, x_out, x_in, term):
        k = exchange.k
        own, sib, across, diag = shards
        exchange.give(2, term(diag), 0)
        x_out[...] = exchange.pair_sum(2, term(across)).astype(BF16)
        self.along_x = k.swap(x_out, x_in, k.xpeer)
        self.along_x.start()
        self.x_in = x_in
        exchange.give(3, term(sib), 1)
        self.kept = exchange.pair_sum(3, term(own))

    def total(self):
        self.along_x.wait_recv()
        return self.x_in[...].astype(F32)


def normalize(values):
    center = values - jnp.mean(values, axis=1, keepdims=True)
    spread = jnp.mean(center * center, axis=1, keepdims=True)
    scale = lax.rsqrt(spread + epsilon)
    return center * scale, scale


def norm_back(values, table, d_normed):
    normed, scale = normalize(values)
    dz = (1.0 + table[0:1, :]) * d_normed
    both = jnp.mean(dz * normed, axis=1, keepdims=True)
    d_values = (dz - jnp.mean(dz, axis=1, keepdims=True) - normed * both) * scale
    d_gain = jnp.sum(d_normed * normed, axis=0, keepdims=True)
    d_shift = jnp.sum(d_normed, axis=0, keepdims=True)
    return d_values, d_gain, d_shift


def layer_kernel(names, z_size, *refs):
    held = dict(zip(names, refs))
    held.update(
        d_mixed=held["act"],
        d_query=held["mixed"],
        d_branch=held["normed_ffn"],
        d_query_low=held["attn_t"],
        d_keys_low=held["keys_t"],
        d_values_low=held["values_t"],
        g_attn=held["g_down"],
    )
    n = collections.namedtuple("Buffers", held)(**held)
    k = Links(z_size, n.send_sem, n.recv_sem)
    mp_size, block, width = n.normed.shape
    seq = mp_size * block
    heads_wide = n.wa.shape[1]
    hidden = n.wf.shape[1]
    heads = heads_wide // HD
    q_wide = heads * block
    tile = block
    far = mp_size
    own_shard = 2 * k.x + k.core
    sib_shard = 2 * k.x + 1 - k.core
    x_shard = 2 * (1 - k.x) + k.core
    diag_shard = 2 * (1 - k.x) + 1 - k.core
    shards = (own_shard, sib_shard, x_shard, diag_shard)

    def mine(r):
        return 2 * r + k.core

    def theirs(r):
        return 2 * r + 1 - k.core

    def span(i, size=tile):
        return pl.ds(pl.multiple_of(i * size, size), size)

    fetches = []

    def fetch(src, dst):
        made = pltpu.make_async_copy(src, dst, n.load_sem.at[len(fetches)])
        made.start()
        fetches.append(made)
        return made

    load_tokens = fetch(n.tokens, n.raw.at[k.x])
    load_cot = fetch(n.cotangent, n.cot.at[own_shard])

    def unpack(source, stage, sems, target, first, last):
        rows = stage.shape[1]

        def piece(i):
            slot = lax.rem(i, 2)
            return pltpu.make_async_copy(
                source.at[pl.ds(i * rows, rows)], stage.at[slot], sems.at[slot]
            )

        piece(jnp.int32(first)).start()

        def body(i, carry):
            @pl.when(i + 1 < last)
            def _():
                piece(i + 1).start()

            piece(i).wait()
            for s in range(target.shape[0]):
                target[s, span(i, rows), :] = stage[lax.rem(i, 2), :, s, :]
            return carry

        lax.fori_loop(first, last, body, 0)

    pieces_a = heads_wide // n.stage_a.shape[1]
    pieces_f = hidden // n.stage_f.shape[1]

    def unpack_ffn(part, parts):
        first, last = part * pieces_f // parts, (part + 1) * pieces_f // parts
        unpack(n.w_ffn, n.stage_f, n.stage_sem_f, n.wf, first, last)

    def partner_of(row):
        begin, first, count = 0, 0, 1
        for g in range(n.group_sizes.shape[0]):
            size = n.group_sizes[g]
            inside = jnp.logical_and(row >= begin, row < begin + size)
            first = jnp.where(inside, begin, first)
            count = jnp.where(inside, size, count)
            begin = begin + size
        step = lax.rem(n.partner_pick[row], jnp.maximum(count - 1, 1))
        return jnp.clip(first + lax.rem(row - first + 1 + step, count), 0, 2 * z_size - 1)

    k.barrier()
    send_tokens = k.swap(n.tokens, n.raw.at[k.x], k.xpeer)
    send_tokens.start()
    cot_x = k.swap(n.cotangent, n.cot.at[own_shard], k.xpeer)
    cot_x.start()
    cot_sib = k.swap(n.cotangent, n.cot.at[own_shard], k.sib)
    cot_sib.start()

    code = n.codebook[k.dp]
    start = n.prompt_start[k.dp]
    partner = partner_of(k.dp)
    other_partner = partner_of(k.dp + 1 - 2 * k.y)
    part_z, part_y = partner // 2, lax.rem(partner, 2)
    line_partners = []
    for d in range(z_size):
        row = partner_of(2 * d + k.y)
        line_partners.append((row // 2 == k.z, lax.rem(row, 2) == k.y))
    other_z, other_y = other_partner // 2, lax.rem(other_partner, 2)
    far_len = n.prompt_len[partner]
    table_attn = n.ada_attn[code]
    table_ffn = n.ada_ffn[code]

    def adapt(normed, table):
        return ((1.0 + table[0:1, :]) * normed + table[1:2, :]).astype(BF16)

    def project(s):
        normed = n.normed[s]
        query = (dot(normed, n.wa[0], 1, 1) * HD ** (-0.5)).astype(BF16)
        lane = lax.broadcasted_iota(jnp.int32, (block, heads_wide), 1) // HD
        for h in range(heads):
            n.q4[s, h * block : (h + 1) * block, :] = jnp.where(lane == h, query, 0).astype(BF16)
        for ref, turned, w in ((n.keys, n.keys_t, 1), (n.values, n.values_t, 2)):
            made = dot(normed, n.wa[w], 1, 1)
            ref[s] = made.astype(BF16)
            turned[s] = made.T.astype(BF16)

    load_tokens.wait()
    n.normed[own_shard] = adapt(normalize(n.raw[k.x].astype(F32))[0], table_attn)
    normed_own = k.swap(n.normed.at[own_shard], n.normed.at[own_shard], k.sib)
    normed_own.start()
    unpack(n.w_attn, n.stage_a, n.stage_sem_a, n.wa, 0, pieces_a)
    normed_own.wait_recv()

    def project_pair(first):
        def body(i, carry):
            project(first + i)
            return carry

        lax.fori_loop(0, 2, body, 0)

    project_pair(2 * k.x)
    send_tokens.wait_recv()
    n.normed[x_shard] = adapt(normalize(n.raw[1 - k.x].astype(F32))[0], table_attn)
    normed_x = k.swap(n.normed.at[x_shard], n.normed.at[x_shard], k.sib)
    normed_x.start()
    normed_x.wait_recv()
    project_pair(2 * (1 - k.x))

    all_keys = n.keys[0:mp_size].reshape(seq, heads_wide)
    all_values = n.values[0:mp_size].reshape(seq, heads_wide)
    from_row = lax.broadcasted_iota(jnp.int32, (block, seq), 1)
    to_row = lax.broadcasted_iota(jnp.int32, (block, seq), 0)
    window = (from_row == to_row + start).astype(F32).astype(BF16)
    n.windows_k[k.z] = dot(window, all_keys).astype(BF16)
    gather = LineGather(k, n.windows_k)
    gather.start()
    n.y_out[1] = dot(window, all_values).astype(BF16)
    y_value = k.swap(n.y_out.at[1], n.y_in.at[1], k.ypeer)
    y_value.start()
    line_value = LineReduce(k, n.windows_v, n.passing_v)

    def attend_own(s, carry):
        q4 = n.q4[s]
        top = jnp.full((1, q_wide), -jnp.inf, F32)
        for c in range(mp_size):
            scores = dot(n.keys[c], q4, 1, 1)
            n.wide[c] = scores
            top = jnp.maximum(top, jnp.max(scores, axis=0, keepdims=True))
        total = jnp.zeros((1, q_wide), F32)
        for c in range(mp_size):
            prob = jnp.exp(n.wide[c] - top)
            total = total + jnp.sum(prob, axis=0, keepdims=True)
            low = prob.astype(BF16)
            for h in range(heads):
                rows = slice(h * HD, (h + 1) * HD)
                part = dot(n.values_t[c, rows, :], low[:, h * block : (h + 1) * block])
                n.mixed[s, rows, :] = part if c == 0 else n.mixed[s, rows, :] + part
        n.top[s] = top
        n.total[s] = total
        return carry

    def own(s):
        lax.fori_loop(s, s + 1, attend_own, 0)

    own(0)
    y_value.wait_recv()
    ours, others = n.y_out[1].astype(F32), n.y_in[1].astype(F32)
    for d in k.order:
        here, same_row = line_partners[d]
        chosen = jnp.where(same_row, ours, others)
        n.windows_v[d] = jnp.where(here, chosen, 0.0).astype(BF16)
        line_value.begin(d)
    gather.serve(1)
    own(1)
    line_value.step(1)
    gather.serve(2)
    own(2)
    unpack_ffn(0, 2)
    line_value.step(2)
    gather.serve(3)
    n.y_out[0] = n.windows_k[other_z]
    y_key = k.swap(n.y_out.at[0], n.y_in.at[0], k.ypeer)
    y_key.start()
    own(3)
    unpack_ffn(1, 2)

    cot_x.wait_recv()
    cot_pass = k.swap(n.cot.at[x_shard], n.cot.at[x_shard], k.sib)
    cot_pass.start()
    same_y = part_y == k.y

    def take_far(ref, turned):
        def store(rows):
            ref[far] = rows.astype(BF16)
            turned[far] = rows.T.astype(BF16)

        return store

    line_value.finish(take_far(n.values, n.values_t))
    y_key.wait_recv()
    far_keys = jnp.where(same_y, n.windows_k[part_z].astype(F32), n.y_in[0].astype(F32))
    take_far(n.keys, n.keys_t)(far_keys)

    def attend_far(s):
        scores = dot(n.keys[far], n.q4[s], 1, 1)
        slot = lax.broadcasted_iota(jnp.int32, scores.shape, 0)
        scores = jnp.where(slot < far_len, scores, -1000000000.0)
        top = jnp.maximum(n.top[s], jnp.max(scores, axis=0, keepdims=True))
        scale = jnp.exp(n.top[s] - top)
        prob = jnp.exp(scores - top)
        total = n.total[s] * scale + jnp.sum(prob, axis=0, keepdims=True)
        low = prob.astype(BF16)
        for h in range(heads):
            rows = slice(h * HD, (h + 1) * HD)
            cols = slice(h * block, (h + 1) * block)
            part = n.mixed[s, rows, :] * scale[:, cols] + dot(n.values_t[far, rows, :], low[:, cols])
            n.attn_t[s, rows, :] = (part / total[:, cols]).astype(BF16)
        n.log_total[s] = top + jnp.log(total)

    def out_part(s):
        attend_far(s)
        return dot(n.attn_t[s], n.wa[3], 0, 0)

    branch = Exchange(k, n.pair_out, n.pair_in, n.x_out, n.x_in)
    for r in range(2):
        branch.give(r, out_part(theirs(r)))
        branch.send_x(r, branch.pair_sum(r, out_part(mine(r))))

    back = Exchange(k, n.pair_out, n.pair_in, n.x_out2, n.x_in2)
    load_cot.wait()
    cot_sib.wait_recv()
    cot_pass.wait_recv()

    def hidden_part(s):
        normed = n.normed_ffn[s]
        cot = n.cot[s]

        def body(i, carry):
            cols = span(i)
            up = dot(normed, n.wf[0, cols, :], 1, 1)
            d_act = dot(cot, n.wf[1, cols, :], 1, 1)
            cdf = 0.5 + 0.5 * lax.erf(up * (0.5**0.5))
            n.act[s, :, cols] = (up * cdf).astype(BF16)
            slope = cdf + up * (jnp.exp(-0.5 * up * up) * (2.0 * jnp.pi) ** (-0.5))
            n.d_up[s, :, cols] = (slope * d_act).astype(BF16)
            return carry

        lax.fori_loop(0, hidden // tile, body, 0)
        return dot(n.d_up[s], n.wf[0])

    shares = []
    for r in range(2):
        middle = n.raw[r].astype(F32) + branch.total(r)
        n.wide[r] = middle
        n.normed_ffn[mine(r)] = adapt(normalize(middle)[0], table_ffn)
        share = k.swap(n.normed_ffn.at[mine(r)], n.normed_ffn.at[mine(r)], k.sib)
        share.start()
        shares.append(share)
        share.wait_recv()
        back.give(r, hidden_part(theirs(r)))
        back.send_x(r, back.pair_sum(r, hidden_part(mine(r))))

    grid_down = GridReduce(k, n.g_down, n.h_down, n.p_down)
    upper, lower = pl.ds(0, hidden // 2), pl.ds(hidden // 2, hidden // 2)
    grid_up_z = GridReduceZ(k, n.g_up, upper, n.p_up_z, n.y_out_up, n.y_in_up)
    grid_up = GridReduce(k, n.g_up.at[:, lower], n.h_up, n.p_up)

    def spread(target, rows, made):
        for d in range(target.shape[0]):
            target[d, rows, :] = made[:, d * LANES : (d + 1) * LANES].astype(BF16)

    def ffn_grads(target, left, right):
        def body(i, carry):
            lhs = left[:, :, span(i)].reshape(seq, tile)
            spread(target, span(i), dot(lhs, right[...].reshape(seq, width), 0, 0))
            return carry

        lax.fori_loop(0, hidden // tile, body, 0)

    ffn_grads(n.g_down, n.act, n.cot)
    grid_down.send_y(*k.order[:3])
    ffn_grads(n.g_up, n.d_up, n.normed_ffn)
    grid_up_z.start()

    def down_part(s):
        return dot(n.act[s], n.wf[1])

    k.finish(branch.along_x[0])
    out_sum = Settle(branch, shards, n.x_out.at[0], n.s_in, down_part)
    n.output[...] = out_sum.kept.astype(BF16)

    n.d_keys[...] = jnp.zeros_like(n.d_keys)
    n.d_values[...] = jnp.zeros_like(n.d_values)
    table_grad = [jnp.zeros((1, width), F32), jnp.zeros((1, width), F32)]

    def prepare(s):
        d_attn_t = dot(n.wa[3], n.d_branch[s], 1, 1).astype(BF16)
        row = lax.broadcasted_iota(jnp.int32, (heads_wide, block), 0) // HD
        product = d_attn_t.astype(F32) * n.attn_t[s].astype(F32)
        for h in range(heads):
            rows = slice(h * HD, (h + 1) * HD)
            cols = slice(h * block, (h + 1) * block)
            n.delta[s, :, cols] = jnp.sum(product[rows], axis=0, keepdims=True)
            n.d_mixed[s, :, cols] = jnp.where(row == h, d_attn_t, 0).astype(BF16)

    def attend_back(s, first, last):
        q4 = n.q4[s]
        d_mixed = n.d_mixed[s]

        def body(c, carry):
            scores = dot(n.keys[c], q4, 1, 1)
            slot = lax.broadcasted_iota(jnp.int32, scores.shape, 0)
            limit = jnp.where(c == far, far_len, block)
            prob = jnp.where(slot < limit, jnp.exp(scores - n.log_total[s]), 0.0)
            low = prob.astype(BF16)
            d_prob = dot(n.values[c], d_mixed)
            d_scores = (prob * (d_prob - n.delta[s])).astype(BF16)
            n.d_values[c] += dot(low, d_mixed, 1, 1)
            n.d_keys[c] += dot(d_scores, q4)
            for h in range(heads):
                rows = slice(h * HD, (h + 1) * HD)
                n.d_query[s, rows, :] += dot(
                    n.keys_t[c, rows, :], d_scores[:, h * block : (h + 1) * block]
                )
            return carry

        lax.fori_loop(first, last, body, 0)

    n.d_query[...] = jnp.zeros_like(n.d_query)
    for r in range(2):
        d_values, d_gain, d_shift = norm_back(n.wide[r], table_ffn, back.total(r))
        table_grad[0] = table_grad[0] + d_gain
        table_grad[1] = table_grad[1] + d_shift
        d_middle = n.cot[mine(r)].astype(F32) + d_values
        n.wide[2 + r] = d_middle
        k.finish(shares[r])
        n.d_branch[mine(r)] = d_middle.astype(BF16)
        share = k.swap(n.d_branch.at[mine(r)], n.d_branch.at[mine(r)], k.sib)
        share.start()

        def far_part(i, carry, r=r):
            s = jnp.where(i == 0, mine(r), theirs(r))
            prepare(s)
            attend_back(s, far, far + 1)
            return carry

        lax.fori_loop(0, 1, far_part, 0)
        share.wait_recv()
        lax.fori_loop(1, 2, far_part, 0)
    def table_blocks(target, gain, shift):
        row = lax.broadcasted_iota(jnp.int32, (n.t_ffn.shape[1], width), 0)
        both = jnp.where(lax.rem(row, 2) == 0, gain, shift)
        both = jnp.where(row // 2 == code, both, 0.0)
        for d in range(target.shape[0]):
            target[d] = both[:, d * LANES : (d + 1) * LANES]

    n.packets[k.z] = n.d_values[far].astype(BF16)
    packets = LineGather(k, n.packets)
    packets.start()
    k.finish(y_key)
    n.y_out[0] = jnp.where(same_y, 0.0, n.d_keys[far]).astype(BF16)
    y_key = k.swap(n.y_out.at[0], n.y_in2.at[0], k.ypeer)
    y_key.start()
    table_blocks(n.t_ffn, table_grad[0], table_grad[1])
    grid_t_ffn = GridReduce(k, n.t_ffn, n.ht_ffn, n.pt_ffn)
    grid_t_ffn.send_y()
    grid_down.send_y(k.order[3])
    grid_up.send_y(*k.order[:3])
    gather.wait_sends()
    line_key = LineReduce(k, n.windows_k, n.passing_k)

    def rest(s):
        def body(s, carry):
            attend_back(s, 0, mp_size)
            return carry

        lax.fori_loop(s, s + 1, body, 0)

    rest(0)
    packets.serve(1)
    y_key.wait_recv()
    back_grad = n.y_in2[0].astype(F32)
    for d in k.order:
        here = jnp.where(jnp.logical_and(same_y, part_z == d), n.d_keys[far], 0.0)
        there = jnp.where(jnp.logical_and(other_y == k.y, other_z == d), back_grad, 0.0)
        n.windows_k[d] = (here + there).astype(BF16)
        line_key.begin(d)
    rest(1)
    packets.serve(2)
    line_key.step(1)
    rest(2)
    packets.serve(3)
    ours = jnp.zeros((block, heads_wide), F32)
    others = jnp.zeros((block, heads_wide), F32)
    for d in range(z_size):
        here, same_row = line_partners[d]
        packet = n.packets[d].astype(F32)
        ours = ours + jnp.where(jnp.logical_and(here, same_row), packet, 0.0)
        others = others + jnp.where(jnp.logical_and(here, jnp.logical_not(same_row)), packet, 0.0)
    k.finish(y_value)
    n.y_out[1] = others.astype(BF16)
    y_value = k.swap(n.y_out.at[1], n.y_in2.at[1], k.ypeer)
    y_value.start()
    n.d_values[far] = ours
    line_key.step(2)
    grid_up.send_y(*k.order[3:])
    rest(3)
    grid_up_z.step()
    grid_down.take()
    grid_down.wait_y()

    half_rows = 2 * heads_wide
    grid_oq = GridReduce(k, n.g_attn.at[:, 0:half_rows], n.h_oq, n.p_oq)
    grid_kv = GridReduce(k, n.g_attn.at[:, half_rows : 2 * half_rows], n.h_kv, n.p_kv)

    def add_products(left, right):
        total = dot(left[0], right[0])
        for s in range(1, mp_size):
            total = total + dot(left[s], right[s])
        return total

    spread(n.g_attn, slice(0, heads_wide), add_products(n.attn_t, n.d_branch))
    for s in range(mp_size):
        n.d_query_low[s] = (n.d_query[s] * HD ** (-0.5)).astype(BF16)
    spread(n.g_attn, slice(heads_wide, 2 * heads_wide), add_products(n.d_query_low, n.normed))

    def take_back(total):
        n.keys_t[far] = total.astype(BF16)

    line_key.finish(take_back)
    y_value.wait_recv()
    n.values_t[far] = (n.d_values[far] + n.y_in2[1].astype(F32)).astype(BF16)
    from_slot = lax.broadcasted_iota(jnp.int32, (seq, block), 1)
    to_frame = lax.broadcasted_iota(jnp.int32, (seq, block), 0)
    unwindow = (to_frame == from_slot + start).astype(F32).astype(BF16)
    for ref, low in ((n.d_keys, n.d_keys_low), (n.d_values, n.d_values_low)):
        own = ref[0:mp_size].reshape(seq, heads_wide)
        total = own + dot(unwindow, low[far])
        low[0:mp_size] = total.astype(BF16).reshape(mp_size, block, heads_wide)

    def input_part(s):
        return (
            dot(n.d_query_low[s], n.wa[0], 0, 0)
            + dot(n.d_keys_low[s], n.wa[1])
            + dot(n.d_values_low[s], n.wa[2])
        )

    k.finish(back.along_x[0])
    n.output[...] = (n.wide[k.x] + n.output[...].astype(F32) + out_sum.total()).astype(BF16)
    in_sum = Settle(back, shards, n.x_out2.at[0], n.x_in.at[0], input_part)
    n.grad_tokens[...] = in_sum.kept.astype(BF16)

    table_grad = [jnp.zeros((1, width), F32), jnp.zeros((1, width), F32)]
    for term, at in ((n.x_out2[0].astype(F32), 1 - k.x), (in_sum.kept, k.x)):
        normed = normalize(n.raw[at].astype(F32))[0]
        table_grad[0] = table_grad[0] + jnp.sum(term * normed, axis=0, keepdims=True)
        table_grad[1] = table_grad[1] + jnp.sum(term, axis=0, keepdims=True)
    table_blocks(n.t_attn, *table_grad)
    grid_t_attn = GridReduce(k, n.t_attn, n.ht_attn, n.pt_attn)
    grid_t_attn.send_y()
    flat_normed = n.normed[...].reshape(seq, width)
    for w, low in ((2, n.d_keys_low), (3, n.d_values_low)):
        made = dot(low[0:mp_size].reshape(seq, heads_wide), flat_normed, 0, 0)
        spread(n.g_attn, slice(w * heads_wide, (w + 1) * heads_wide), made)

    grid_kv.send_y()
    grid_oq.send_y()
    grid_t_ffn.take()
    grid_up.take(*k.order[:2])
    grid_t_ffn.step()
    grid_down.step()
    grid_t_attn.take()
    grid_up.take(*k.order[2:])

    quarter = heads_wide
    half_hidden = hidden // 2

    def store_ffn(s, first, more=False):
        def store(total):
            at = pl.ds(s + 2 * first, total.shape[0], stride=2)
            n.grad_ffn[at, :] = n.grad_ffn[at, :] + total if more else total

        return store

    def store_attn(*places):
        def store(total):
            for i, s in enumerate(places):
                at = pl.ds(s, quarter, stride=4)
                rows = total[i * quarter : (i + 1) * quarter]
                n.grad_attn[at, :] = rows

        return store

    def store_table(which):
        def store(total):
            n.t_out[which, 0] = total
            pair = k.swap(n.t_out.at[which, 0], n.t_in.at[which, 0], k.sib)
            pair.start()
            pair.wait_recv()
            n.t_out[which, 1] = total + n.t_in[which, 0]

        return store

    def close_table(which, total):
        piece = LANES // mp_size
        kept = total
        for m in range(1, mp_size):
            turned = pltpu.roll(total, LANES - m * piece, 1)
            kept = jnp.where(k.mp == m, turned, kept)
        n.grad_ada[which] = kept

    grid_up_z.turn(store_ffn(0, 0))
    grid_t_attn.step()
    grid_t_ffn.finish(store_table(0))
    close_table(0, n.t_out[0, 1])
    grid_t_attn.finish(store_table(1))
    table_x = k.swap(n.t_out.at[1, 1], n.t_in.at[1, 1], k.xpeer)
    table_x.start()
    grid_up.step()
    grid_down.finish(store_ffn(1, 0))
    d_normed = n.grad_tokens[...].astype(F32) + in_sum.total()
    d_values, _, _ = norm_back(n.raw[k.x].astype(F32), table_attn, d_normed)
    n.grad_tokens[...] = (n.wide[2 + k.x] + d_values).astype(BF16)
    grid_kv.take()
    grid_up.finish(store_ffn(0, half_hidden))
    table_x.wait_recv()
    close_table(1, n.t_out[1, 1] + n.t_in[1, 1])
    grid_kv.step()
    grid_oq.take()
    grid_up_z.done(store_ffn(0, 0, more=True))
    grid_kv.finish(store_attn(1, 2))
    grid_oq.step()
    grid_oq.finish(store_attn(3, 0))
    k.finish()
    packets.wait_sends()
    for unit in (line_value, line_key):
        unit.wait_sends()
    for unit in (grid_down, grid_up, grid_up_z, grid_oq, grid_kv, grid_t_ffn, grid_t_attn):
        unit.wait_sends()
    for unit in (grid_up, grid_oq, grid_kv, grid_t_ffn, grid_t_attn):
        unit.wait_y()


def layer(tokens, cotangent, w_attn, w_ffn, ada_attn, ada_ffn, ints, dp_size, mp_size):
    z_size = dp_size // 2
    block, width = tokens.shape
    heads_wide = w_attn.shape[0]
    hidden = w_ffn.shape[0]
    heads = heads_wide // HD
    table_rows = ada_attn.shape[0] * 2
    lane_block = width // dp_size

    inputs = dict(
        tokens=tokens,
        cotangent=cotangent,
        w_attn=w_attn,
        w_ffn=w_ffn,
        ada_attn=ada_attn,
        ada_ffn=ada_ffn,
        **ints,
    )
    spaces = dict.fromkeys(("tokens", "cotangent", "w_attn", "w_ffn"), pl.ANY)
    spaces.update(dict.fromkeys(ints, pltpu.SMEM))
    outputs = dict(
        output=((block, width), BF16),
        grad_tokens=((block, width), BF16),
        grad_attn=((4 * heads_wide, lane_block), F32),
        grad_ffn=((2 * hidden, lane_block), F32),
        grad_ada=((2, table_rows, lane_block), F32),
    )
    wide = (mp_size, block, width)
    two = (2, block, width)
    square = (mp_size + 1, block, heads_wide)
    low, full = {}, {}
    for name in ("normed", "cot", "normed_ffn", "act", "d_up"):
        low[name] = wide
    low.update(raw=two, wa=(4, heads_wide, width), wf=(2, hidden, width))
    low.update(stage_a=(2, 32, 4, width), stage_f=(2, 64, 2, width))
    for name in ("keys", "values", "keys_t", "values_t"):
        low[name] = square
    low.update(q4=(mp_size, heads * block, heads_wide), attn_t=(mp_size, heads_wide, block))
    for name in ("pair_out", "pair_in", "x_out", "x_in", "x_out2", "x_in2"):
        low[name] = two
    low.update(s_in=(block, width))
    for name in ("y_out", "y_in", "y_in2"):
        low[name] = (2, block, heads_wide)
    for name in ("k", "v"):
        low["windows_" + name] = (z_size, block, heads_wide)
        low["passing_" + name] = (z_size + 1, block, heads_wide)
    for name in ("up", "down"):
        low["g_" + name] = (dp_size, hidden, lane_block)
    half = 2 * heads_wide
    low.update(packets=(z_size, block, heads_wide))
    some = hidden // 2
    low.update(p_up_z=(z_size, 2, some, lane_block))
    low.update(y_out_up=(some, lane_block), y_in_up=(some, lane_block))
    for name, rows in (("up", some), ("down", hidden), ("oq", half), ("kv", half)):
        low["h_" + name] = (z_size, rows, lane_block)
        low["p_" + name] = (z_size, rows, lane_block)
    for name in ("_ffn", "_attn"):
        full["t" + name] = (dp_size, table_rows, lane_block)
        full["ht" + name] = (z_size, table_rows, lane_block)
        full["pt" + name] = (z_size, table_rows, lane_block)
    full.update(t_out=(2, 2, table_rows, lane_block), t_in=(2, 2, table_rows, lane_block))
    full.update(wide=(mp_size, block, heads * block))
    for name in ("top", "total", "log_total", "delta"):
        full[name] = (mp_size, 1, heads * block)
    full.update(mixed=(mp_size, heads_wide, block))
    full.update(d_keys=square, d_values=square)
    scratch = {name: pltpu.VMEM(shape, BF16) for name, shape in low.items()}
    scratch.update({name: pltpu.VMEM(shape, F32) for name, shape in full.items()})
    copies = 200
    scratch.update(
        load_sem=pltpu.SemaphoreType.DMA((2,)),
        stage_sem_a=pltpu.SemaphoreType.DMA((2,)),
        stage_sem_f=pltpu.SemaphoreType.DMA((2,)),
        send_sem=pltpu.SemaphoreType.DMA((copies,)),
        recv_sem=pltpu.SemaphoreType.DMA((copies,)),
    )
    names = tuple(inputs) + tuple(outputs) + tuple(scratch)
    return pl.pallas_call(
        functools.partial(layer_kernel, names, z_size),
        out_shape=tuple(jax.ShapeDtypeStruct(*shape) for shape in outputs.values()),
        in_specs=[pl.BlockSpec(memory_space=spaces.get(name, pltpu.VMEM)) for name in inputs],
        out_specs=[pl.BlockSpec(memory_space=pltpu.VMEM) for _ in outputs],
        scratch_shapes=list(scratch.values()),
        compiler_params=pltpu.CompilerParams(
            collective_id=1, has_side_effects=True, vmem_limit_bytes=60 << 20
        ),
    )(*inputs.values())


def place_kernel(count, *refs):
    moves = []
    for i in range(count):
        moves.append(pltpu.make_async_copy(refs[i], refs[count + i], refs[-1].at[i]))
        moves[i].start()
    for move in moves:
        move.wait()


def place(arrays):
    return pl.pallas_call(
        functools.partial(place_kernel, len(arrays)),
        out_shape=tuple(jax.ShapeDtypeStruct(a.shape, a.dtype) for a in arrays),
        in_specs=[pl.BlockSpec(memory_space=pltpu.VMEM)] * len(arrays),
        out_specs=[pl.BlockSpec(memory_space=pl.ANY)] * len(arrays),
        scratch_shapes=[pltpu.SemaphoreType.DMA((len(arrays),))],
    )(*arrays)


def shards(
    tokens,
    w_attn,
    w_ffn,
    ada_attn,
    ada_ffn,
    codebook,
    group_sizes,
    partner_pick,
    prompt_start,
    prompt_len,
    cotangent,
):
    tok_rows, width = tokens.shape
    mp_size = lax.axis_size("mp")
    dp_index = lax.axis_index("dp")
    mp_index = lax.axis_index("mp")
    block_tokens = tok_rows * mp_size
    seq_here = block_tokens // LEN
    head_cols = w_attn.shape[0]
    heads_here = head_cols // HD
    total_rows = codebook.shape[0]
    dp_size = lax.axis_size("dp")
    fits = width == dp_size * LANES and width == w_ffn.shape[0] == tok_rows * heads_here
    if seq_here == 1 and mp_size == 4 and fits and tok_rows == PMAX:
        ints = dict(
            codebook=codebook,
            group_sizes=group_sizes,
            partner_pick=partner_pick,
            prompt_start=prompt_start,
            prompt_len=prompt_len,
        )
        results = layer(
            tokens,
            cotangent,
            w_attn,
            w_ffn,
            ada_attn,
            ada_ffn,
            ints,
            dp_size,
            mp_size,
        )
        output, grad_tokens, grad_attn, grad_ffn = place(results[:4])
        grad_ada = results[4]
        grad_ada = grad_ada[:, :, : width // (dp_size * mp_size)]
        grad_ada = grad_ada.reshape((2,) + ada_attn.shape[:2] + grad_ada.shape[2:])
        return (
            output,
            grad_tokens,
            grad_attn.reshape(head_cols, 4, LANES),
            grad_ffn.reshape(w_ffn.shape[0], 2, LANES),
            grad_ada[1],
            grad_ada[0],
        )
    partner = partner_rows(group_sizes, partner_pick)
    first_row = dp_index * seq_here
    tok_global = (dp_index * mp_size + mp_index) * tok_rows + jnp.arange(tok_rows, dtype=jnp.int32)
    row_pick = (
        (tok_global // LEN)[:, None] == jnp.arange(total_rows, dtype=jnp.int32)[None, :]
    ).astype(jnp.int32)
    token_codes = jnp.sum(row_pick * codebook[None, :], axis=1)
    code_hot = (
        token_codes[:, None] == jnp.arange(ada_attn.shape[0], dtype=jnp.int32)[None, :]
    ).astype(jnp.float32)
    my_partner = lax.dynamic_slice_in_dim(partner, first_row, seq_here)
    my_starts = lax.dynamic_slice_in_dim(prompt_start, first_row, seq_here)
    partner_hot = (my_partner[:, None] == jnp.arange(total_rows, dtype=jnp.int32)[None, :]).astype(
        jnp.int32
    )
    partner_len = jnp.sum(partner_hot * prompt_len[None, :], axis=1)
    far_valid = jnp.arange(PMAX, dtype=jnp.int32)[None, :] < partner_len[:, None]
    inputs = tokens.astype(jnp.float32)
    normed_attn = adaptive_norm(inputs, ada_attn, code_hot).astype(jnp.bfloat16)
    normed_attn_full = lax.all_gather(normed_attn, "mp", axis=0, tiled=True)
    w_qkv = w_attn[:, 0:3, :]
    w_out = w_attn[:, 3, :]
    qkv_low = jnp.einsum(
        "td,jsd->tsj", normed_attn_full, w_qkv, preferred_element_type=jnp.float32
    ).astype(jnp.bfloat16)
    kv_rows = qkv_low[:, 1:3, :].reshape(seq_here, LEN, 2 * head_cols)
    windows = jax.vmap(
        lambda sequence, offset: lax.dynamic_slice_in_dim(sequence, offset, PMAX, 0)
    )(kv_rows, my_starts)
    shard_rows = lax.all_gather(windows, "dp", axis=0, tiled=True)
    row_ids = jnp.arange(shard_rows.shape[0], dtype=jnp.int32)
    picker = (my_partner[:, None] == row_ids[None, :]).astype(jnp.bfloat16)
    prompt_sum = jnp.einsum("kr,rpc->kpc", picker, shard_rows, preferred_element_type=jnp.float32)
    prompt_kv = prompt_sum.astype(jnp.bfloat16)
    queries = qkv_low[:, 0, :].reshape(seq_here, LEN, heads_here, HD)
    own_keys = qkv_low[:, 1, :].reshape(seq_here, LEN, heads_here, HD)
    own_values = qkv_low[:, 2, :].reshape(seq_here, LEN, heads_here, HD)
    far_keys = prompt_kv[:, :, :head_cols].reshape(seq_here, PMAX, heads_here, HD)
    far_values = prompt_kv[:, :, head_cols:].reshape(seq_here, PMAX, heads_here, HD)
    attended, log_total = lax.map(
        attend, (queries, own_keys, own_values, far_keys, far_values, far_valid)
    )
    attn_flat = attended.reshape(block_tokens, head_cols)
    middle = inputs + lax.psum_scatter(
        jnp.dot(attn_flat, w_out, preferred_element_type=jnp.float32).astype(jnp.bfloat16),
        "mp",
        scatter_dimension=0,
        tiled=True,
    ).astype(jnp.float32)
    normed_ffn = adaptive_norm(middle, ada_ffn, code_hot).astype(jnp.bfloat16)
    normed_ffn_full = lax.all_gather(normed_ffn, "mp", axis=0, tiled=True)
    w_up = w_ffn[:, 0, :]
    w_down = w_ffn[:, 1, :]
    up_proj = inner_cols(normed_ffn_full, w_up)
    activated = jax.nn.gelu(up_proj, approximate=False).astype(jnp.bfloat16)
    output = (
        middle
        + lax.psum_scatter(
            jnp.dot(activated, w_down, preferred_element_type=jnp.float32).astype(jnp.bfloat16),
            "mp",
            scatter_dimension=0,
            tiled=True,
        ).astype(jnp.float32)
    ).astype(jnp.bfloat16)
    shard_rows = lax.all_gather(cotangent, "mp", axis=0, tiled=True)
    rows_grad = inner_cols(shard_rows, w_down)
    d_act = rows_grad
    grad_down = inner_rows(activated, shard_rows)
    _, gelu_pull = jax.vjp(lambda values: jax.nn.gelu(values, approximate=False), up_proj)
    d_up = gelu_pull(d_act)[0].astype(jnp.bfloat16)
    d_normed_ffn = lax.psum_scatter(
        jnp.dot(d_up, w_up, preferred_element_type=jnp.float32).astype(jnp.bfloat16),
        "mp",
        scatter_dimension=0,
        tiled=True,
    ).astype(jnp.float32)
    grad_up = inner_rows(d_up, lax.all_gather(normed_ffn, "mp", axis=0, tiled=True))
    _, norm_ffn_pull = jax.vjp(
        lambda values, table: adaptive_norm(values, table, code_hot), middle, ada_ffn
    )
    d_middle_norm, grad_table_ffn = norm_ffn_pull(d_normed_ffn)
    d_middle = cotangent.astype(jnp.float32) + d_middle_norm
    d_branch = d_middle.astype(jnp.bfloat16)
    shard_rows = lax.all_gather(d_branch, "mp", axis=0, tiled=True)
    rows_grad = inner_cols(shard_rows, w_out)
    grad_out_proj = inner_rows(attn_flat, shard_rows)
    d_mixed = rows_grad.astype(jnp.bfloat16).reshape(seq_here, LEN, heads_here, HD)
    d_queries, d_own_keys, d_own_values, d_far_keys, d_far_values = lax.map(
        attend_back,
        (queries, own_keys, own_values, far_keys, far_values, far_valid, log_total, d_mixed),
    )
    prompt_grad = jnp.concatenate(
        [
            d_far_keys.reshape(seq_here, PMAX, head_cols),
            d_far_values.reshape(seq_here, PMAX, head_cols),
        ],
        axis=2,
    )
    row_ids = jnp.arange(lax.axis_size("dp") * seq_here, dtype=jnp.int32)
    picker = (my_partner[:, None] == row_ids[None, :]).astype(jnp.float32)
    returned_kv = lax.psum_scatter(
        jnp.einsum("kr,kpc->rpc", picker, prompt_grad, precision=highest).astype(jnp.bfloat16),
        "dp",
        scatter_dimension=0,
        tiled=True,
    ).astype(jnp.float32)
    d_kv_rows = jnp.concatenate(
        [
            d_own_keys.reshape(seq_here, LEN, head_cols),
            d_own_values.reshape(seq_here, LEN, head_cols),
        ],
        axis=2,
    )
    d_kv_rows = jax.vmap(
        lambda sequence, window, offset: lax.dynamic_update_slice_in_dim(
            sequence, lax.dynamic_slice_in_dim(sequence, offset, PMAX, 0) + window, offset, 0
        )
    )(d_kv_rows, returned_kv, my_starts)
    d_qkv = jnp.stack(
        [
            d_queries.reshape(block_tokens, head_cols),
            d_kv_rows[:, :, :head_cols].reshape(block_tokens, head_cols),
            d_kv_rows[:, :, head_cols:].reshape(block_tokens, head_cols),
        ],
        axis=1,
    ).astype(jnp.bfloat16)
    d_normed_attn = lax.psum_scatter(
        jnp.einsum("tsj,jsd->td", d_qkv, w_qkv, preferred_element_type=jnp.float32).astype(
            jnp.bfloat16
        ),
        "mp",
        scatter_dimension=0,
        tiled=True,
    ).astype(jnp.float32)
    grad_qkv = jnp.einsum(
        "tsj,td->jsd",
        d_qkv,
        lax.all_gather(normed_attn, "mp", axis=0, tiled=True),
        preferred_element_type=jnp.float32,
    )
    _, norm_attn_pull = jax.vjp(
        lambda values, table: adaptive_norm(values, table, code_hot), inputs, ada_attn
    )
    d_inputs_norm, grad_table_attn = norm_attn_pull(d_normed_attn)
    grad_tokens = (d_middle + d_inputs_norm).astype(jnp.bfloat16)
    grad_attn_local = jnp.concatenate([grad_qkv, grad_out_proj[:, None, :]], axis=1)
    grad_ffn_local = jnp.stack([grad_up, grad_down], axis=1)
    grad_attn, grad_ffn = (
        lax.psum_scatter(
            grad_attn_local.astype(jnp.bfloat16), "dp", scatter_dimension=2, tiled=True
        ).astype(jnp.float32),
        lax.psum_scatter(
            grad_ffn_local.astype(jnp.bfloat16), "dp", scatter_dimension=2, tiled=True
        ).astype(jnp.float32),
    )
    grad_ada_attn, grad_ada_ffn = (
        lax.psum_scatter(grad_table_attn, ("dp", "mp"), scatter_dimension=2, tiled=True),
        lax.psum_scatter(grad_table_ffn, ("dp", "mp"), scatter_dimension=2, tiled=True),
    )
    return (output, grad_tokens, grad_attn, grad_ffn, grad_ada_attn, grad_ada_ffn)


def solution(mesh):
    in_specs = (
        P(("dp", "mp"), None),
        P("mp", None, None),
        P("mp", None, None),
        P(),
        P(),
        P(),
        P(),
        P(),
        P(),
        P(),
        P(("dp", "mp"), None),
    )
    out_specs = (
        P(("dp", "mp"), None),
        P(("dp", "mp"), None),
        P("mp", None, "dp"),
        P("mp", None, "dp"),
        P(None, None, ("dp", "mp")),
        P(None, None, ("dp", "mp")),
    )
    return jax.shard_map(shards, mesh=mesh, in_specs=in_specs, out_specs=out_specs, check_vma=False)
```

```python
import collections
import functools

import jax
import jax.numpy as jnp
from jax import lax
from jax.experimental import pallas as pl
from jax.experimental.pallas import tpu as pltpu
from jax.sharding import PartitionSpec as P

HD = 64
LEN = 1024
PMAX = 256


epsilon = 1e-05
highest = lax.Precision.HIGHEST


def partner_rows(group_sizes, partner_pick):
    group_end = jnp.cumsum(group_sizes)
    begins = group_end - group_sizes
    row_ids = jnp.arange(partner_pick.shape[0], dtype=jnp.int32)
    owner_group = jnp.sum((group_end[None, :] <= row_ids[:, None]).astype(jnp.int32), axis=1)
    member = (
        owner_group[:, None] == jnp.arange(group_sizes.shape[0], dtype=jnp.int32)[None, :]
    ).astype(jnp.int32)
    first_row = jnp.sum(member * begins[None, :], axis=1)
    group_len = jnp.sum(member * group_sizes[None, :], axis=1)
    span_size = jnp.maximum(group_len - 1, 1)
    return first_row + (row_ids - first_row + 1 + partner_pick % span_size) % group_len


def adaptive_norm(inputs, table, code_hot):
    coefficients = jnp.dot(code_hot, table.reshape(table.shape[0], -1), precision=highest)
    coefficients = coefficients.reshape(inputs.shape[0], 2, inputs.shape[1])
    center = inputs - jnp.mean(inputs, axis=-1, keepdims=True)
    spread = jnp.mean(center * center, axis=-1, keepdims=True)
    normed = center * lax.rsqrt(spread + epsilon)
    return (1.0 + coefficients[:, 0, :]) * normed + coefficients[:, 1, :]


def inner_rows(left, right):
    return lax.dot_general(
        left, right, (((0,), (0,)), ((), ())), preferred_element_type=jnp.float32
    )


def inner_cols(left, right):
    return lax.dot_general(
        left, right, (((1,), (1,)), ((), ())), preferred_element_type=jnp.float32
    )


def row_scores(queries, key_rows, far_valid):
    key_mask = jnp.concatenate([jnp.ones((queries.shape[0],), dtype=jnp.bool_), far_valid])
    scores = jnp.einsum(
        "qhd,khd->hqk", queries, key_rows, preferred_element_type=jnp.float32
    ) * HD ** (-0.5)
    return jnp.where(key_mask[None, None, :], scores, -1000000000.0)


def attend(packed):
    queries, own_keys, own_values, far_keys, far_values, far_valid = packed
    key_rows = jnp.concatenate([own_keys, far_keys], axis=0)
    value_rows = jnp.concatenate([own_values, far_values], axis=0)
    scores = row_scores(queries, key_rows, far_valid)
    row_max = jnp.max(scores, axis=-1, keepdims=True)
    log_total = row_max + jnp.log(jnp.sum(jnp.exp(scores - row_max), axis=-1, keepdims=True))
    prob_low = jnp.exp(scores - log_total).astype(jnp.bfloat16)
    mixed = jnp.einsum("hqk,khd->qhd", prob_low, value_rows, preferred_element_type=jnp.float32)
    return (mixed.astype(jnp.bfloat16), log_total)


def attend_back(packed):
    queries, own_keys, own_values, far_keys, far_values, far_valid, log_total, d_mixed = packed
    key_rows = jnp.concatenate([own_keys, far_keys], axis=0)
    value_rows = jnp.concatenate([own_values, far_values], axis=0)
    scores = row_scores(queries, key_rows, far_valid)
    attn_prob = jnp.exp(scores - log_total)
    prob_low = attn_prob.astype(jnp.bfloat16)
    d_values = jnp.einsum("hqk,qhd->khd", prob_low, d_mixed, preferred_element_type=jnp.float32)
    d_prob = jnp.einsum("qhd,khd->hqk", d_mixed, value_rows, preferred_element_type=jnp.float32)
    row_delta = jnp.sum(attn_prob * d_prob, axis=-1, keepdims=True)
    d_scores = (attn_prob * (d_prob - row_delta)).astype(jnp.bfloat16)
    d_queries = jnp.einsum(
        "hqk,khd->qhd", d_scores, key_rows, preferred_element_type=jnp.float32
    ) * HD ** (-0.5)
    d_keys = jnp.einsum(
        "hqk,qhd->khd", d_scores, queries, preferred_element_type=jnp.float32
    ) * HD ** (-0.5)
    own_len = queries.shape[0]
    return (d_queries, d_keys[:own_len], d_values[:own_len], d_keys[own_len:], d_values[own_len:])


MESH = pl.DeviceIdType.MESH
F32 = jnp.float32
BF16 = jnp.bfloat16
LANES = 128


def dot(left, right, left_dim=1, right_dim=0):
    return lax.dot_general(
        left, right, (((left_dim,), (right_dim,)), ((), ())), preferred_element_type=F32
    )


class Links:
    def __init__(self, z_size, send_sem, recv_sem):
        self.dp = lax.axis_index("dp")
        self.mp = lax.axis_index("mp")
        self.z_size = z_size
        self.order = (z_size - 1, 0) + tuple(range(1, z_size - 1))
        self.y = lax.rem(self.dp, 2)
        self.z = self.dp // 2
        self.core = lax.rem(self.mp, 2)
        self.x = self.mp // 2
        self.sib = (self.dp, self.mp + 1 - 2 * self.core)
        self.xpeer = (self.dp, self.mp + 2 - 4 * self.x)
        self.ypeer = (self.dp + 1 - 2 * self.y, self.mp)
        self.right = (self.dp + 2, self.mp)
        self.left = (self.dp - 2, self.mp)
        self.send_sem = send_sem
        self.recv_sem = recv_sem
        self.used = 0
        self.sent = []
        self.pair_sends = {}

    def take(self, count=1):
        first = self.used
        self.used += count
        return first

    def copy(self, src, dst, number, device, landing=None):
        return pltpu.make_async_remote_copy(
            src_ref=src,
            dst_ref=dst,
            send_sem=self.send_sem.at[number],
            recv_sem=self.recv_sem.at[number if landing is None else landing],
            device_id=device,
            device_id_type=MESH,
        )

    def swap(self, src, dst, device):
        made = self.copy(src, dst, self.take(), device)
        self.sent.append(made)
        return made

    def finish(self, made=None):
        for one in list(self.sent):
            if made is None or one is made:
                one.wait_send()
        self.sent = [one for one in self.sent if made is not None and one is not made]

    def barrier(self):
        bar = pltpu.get_barrier_semaphore()
        for device in (self.sib, self.xpeer, self.ypeer):
            pl.semaphore_signal(bar, inc=1, device_id=device, device_id_type=MESH)

        @pl.when(self.z > 0)
        def _():
            pl.semaphore_signal(bar, inc=1, device_id=self.left, device_id_type=MESH)

        @pl.when(self.z < self.z_size - 1)
        def _():
            pl.semaphore_signal(bar, inc=1, device_id=self.right, device_id_type=MESH)

        inner = (self.z > 0).astype(jnp.int32) + (self.z < self.z_size - 1).astype(jnp.int32)
        pl.semaphore_wait(bar, 3 + inner)


class LineReduce:
    def __init__(self, links, held, passing):
        self.setup(links, held, passing)

    def setup(self, links, held, passing):
        self.k = links
        self.held, self.passing = held, passing
        self.nr = links.take(links.z_size)
        self.nl = links.take(links.z_size)

    def z_copy(self, d, rightward):
        k = self.k
        if rightward:
            return k.copy(self.held.at[d], self.passing.at[d], self.nr + d, k.right)
        landing = jnp.where(k.z - 1 == d, k.z_size, d)
        return k.copy(self.held.at[d], self.passing.at[landing], self.nl + d, k.left)

    def add(self, d):
        total = self.held[d].astype(F32) + self.passing[d].astype(F32)
        self.held[d] = total.astype(self.held.dtype)

    def begin(self, d):
        k = self.k
        last = k.z_size - 1
        if d > 0:

            @pl.when(k.z == 0)
            def _():
                self.z_copy(d, True).start()

        if d < last:

            @pl.when(k.z == last)
            def _():
                self.z_copy(d, False).start()

    def step(self, i):
        k = self.k
        n = k.z_size

        @pl.when(k.z == i)
        def _():
            for d in range(n - 1, i, -1):
                self.z_copy(d, True).wait_recv()
                self.add(d)
                self.z_copy(d, True).start()

        @pl.when(k.z == n - 1 - i)
        def _():
            for d in range(n - 1 - i):
                self.z_copy(d, False).wait_recv()
                self.add(d)
                self.z_copy(d, False).start()

    def finish(self, store):
        k = self.k
        n = k.z_size

        @pl.when(k.z > 0)
        def _():
            k.copy(self.held.at[k.z], self.passing.at[k.z], self.nr + k.z, k.left).wait_recv()

        @pl.when(k.z < n - 1)
        def _():
            k.copy(self.held.at[k.z], self.passing.at[n], self.nl + k.z, k.right).wait_recv()

        total = self.held[k.z].astype(F32)
        from_left = jnp.where(k.z > 0, self.passing[k.z].astype(F32), 0.0)
        from_right = jnp.where(k.z < n - 1, self.passing[n].astype(F32), 0.0)
        store(total + from_left + from_right)

    def wait_sends(self):
        k = self.k
        for d in range(k.z_size):

            @pl.when(k.z < d)
            def _(d=d):
                self.z_copy(d, True).wait_send()

            @pl.when(k.z > d)
            def _(d=d):
                self.z_copy(d, False).wait_send()


class GridReduce:
    def __init__(self, links, local, held, passing):
        n = links.z_size
        self.k = links
        self.local, self.held, self.passing = local, held, passing
        self.ny, self.ns, self.nr = links.take(n), links.take(n), links.take(n)
        self.inner = {n - 1: 1, 0: n - 2}

    def part(self, d):
        return self.held.at[d]

    def y_copy(self, d):
        k = self.k
        other = 2 * d + 1 - k.y
        return k.copy(self.local.at[other], self.held.at[d], self.ny + d, k.ypeer)

    def send_y(self, *dests):
        for d in dests or self.k.order:
            self.y_copy(d).start()

    def z_copy(self, d):
        k = self.k
        to = d
        if d in self.inner:
            to = jnp.where(k.z == k.z_size - 1 - d, self.inner[d], d)
        slot = jnp.where(to == d, k.z, to)
        device = (2 * to + k.y, k.mp)
        return k.copy(self.part(d), self.passing.at[slot], self.ns + d, device, self.nr + slot)

    def landed(self, slot):
        self.k.copy(self.part(0), self.passing.at[slot], self.ns, self.k.ypeer, self.nr + slot).wait_recv()

    def take(self, *dests):
        k = self.k
        for d in dests or k.order:
            self.y_copy(d).wait_recv()
            total = self.local[2 * d + k.y].astype(F32) + self.held[d].astype(F32)
            self.held[d] = total.astype(self.held.dtype)
            self.send_z(d)

    def send_z(self, d):
        ready = self.k.z != d
        if d in self.inner:
            ready = jnp.logical_and(ready, self.k.z != self.inner[d])

        @pl.when(ready)
        def _():
            self.z_copy(d).start()

    def step(self):
        for d, at in self.inner.items():

            @pl.when(self.k.z == at)
            def _(d=d, at=at):
                self.landed(at)
                part = self.part(d)
                part[...] = (part[...].astype(F32) + self.passing[at].astype(F32)).astype(part.dtype)
                self.z_copy(d).start()

    def finish(self, store):
        k = self.k
        n = k.z_size
        total = self.part(k.z)[...].astype(F32)
        for source in range(n):
            apart = jnp.abs(k.z - source)
            sends = jnp.logical_and(apart != 0, apart != n - 1)

            @pl.when(sends)
            def _(source=source):
                self.landed(source)

            total = total + jnp.where(sends, self.passing[source].astype(F32), 0.0)
        store(total)

    def wait_sends(self):
        for d in range(self.k.z_size):

            @pl.when(self.k.z != d)
            def _(d=d):
                self.z_copy(d).wait_send()

    def wait_y(self):
        for d in range(self.k.z_size):
            self.y_copy(d).wait_send()


class GridReduceZ(GridReduce):
    def __init__(self, links, local, rows, passing, y_out, y_in):
        n = links.z_size
        self.k = links
        self.local, self.rows, self.passing = local, rows, passing
        self.ns, self.nr = links.take(n), links.take(n)
        self.inner = {n - 1: 1, 0: n - 2}
        self.y_out, self.y_in = y_out, y_in

    def part(self, d):
        return self.local.at[pl.ds(2 * d, 2), self.rows]

    def start(self):
        for d in self.k.order:
            self.send_z(d)

    def turn(self, store):
        k = self.k

        def split(total):
            low = k.y == 0
            store(jnp.where(low, total[0], total[1]))
            self.y_out[...] = jnp.where(low, total[1], total[0]).astype(BF16)

        self.finish(split)
        self.along_y = k.swap(self.y_out, self.y_in, k.ypeer)
        self.along_y.start()

    def done(self, add):
        self.along_y.wait_recv()
        add(self.y_in[...].astype(F32))


class LineGather:
    def __init__(self, links, slots):
        self.k = links
        self.slots = slots
        self.nr = links.take(links.z_size)
        self.nl = links.take(links.z_size)

    def z_copy(self, slot, rightward):
        k = self.k
        number = (self.nr if rightward else self.nl) + slot
        place = self.slots.at[slot]
        return k.copy(place, place, number, k.right if rightward else k.left)

    def start(self):
        k = self.k

        @pl.when(k.z < k.z_size - 1)
        def _():
            self.z_copy(k.z, True).start()

        @pl.when(k.z > 0)
        def _():
            self.z_copy(k.z, False).start()

    def serve(self, distance):
        k = self.k

        @pl.when(k.z >= distance)
        def _():
            self.z_copy(k.z - distance, True).wait_recv()

            @pl.when(k.z < k.z_size - 1)
            def _():
                self.z_copy(k.z - distance, True).start()

        @pl.when(k.z + distance < k.z_size)
        def _():
            self.z_copy(k.z + distance, False).wait_recv()

            @pl.when(k.z > 0)
            def _():
                self.z_copy(k.z + distance, False).start()

    def wait_sends(self):
        k = self.k
        for slot in range(k.z_size):

            @pl.when(jnp.logical_and(k.z >= slot, k.z < k.z_size - 1))
            def _(slot=slot):
                self.z_copy(slot, True).wait_send()

            @pl.when(jnp.logical_and(k.z <= slot, k.z > 0))
            def _(slot=slot):
                self.z_copy(slot, False).wait_send()


class Exchange:
    def __init__(self, links, pair_out, pair_in, x_out, x_in):
        self.k = links
        self.pair_out, self.pair_in, self.x_out, self.x_in = pair_out, pair_in, x_out, x_in
        self.pair = {}
        self.along_x = {}

    def give(self, r, term, slot=None):
        slot = r if slot is None else slot
        if slot in self.k.pair_sends:
            self.k.finish(self.k.pair_sends[slot])
        self.pair_out[slot] = term.astype(BF16)
        made = self.k.swap(self.pair_out.at[slot], self.pair_in.at[slot], self.k.sib)
        made.start()
        self.k.pair_sends[slot] = made
        self.pair[r] = (made, slot)

    def pair_sum(self, r, term):
        made, slot = self.pair[r]
        made.wait_recv()
        return term + self.pair_in[slot].astype(F32)

    def send_x(self, r, total):
        self.x_out[r] = total.astype(BF16)
        made = self.k.swap(self.x_out.at[r], self.x_in.at[r], self.k.xpeer)
        made.start()
        self.along_x[r] = made

    def total(self, r):
        self.along_x[r].wait_recv()
        return self.x_out[r].astype(F32) + self.x_in[r].astype(F32)


class Settle:
    def __init__(self, exchange, shards, x_out, x_in, term):
        k = exchange.k
        own, sib, across, diag = shards
        exchange.give(2, term(diag), 0)
        x_out[...] = exchange.pair_sum(2, term(across)).astype(BF16)
        self.along_x = k.swap(x_out, x_in, k.xpeer)
        self.along_x.start()
        self.x_in = x_in
        exchange.give(3, term(sib), 1)
        self.kept = exchange.pair_sum(3, term(own))

    def total(self):
        self.along_x.wait_recv()
        return self.x_in[...].astype(F32)


def normalize(values):
    center = values - jnp.mean(values, axis=1, keepdims=True)
    spread = jnp.mean(center * center, axis=1, keepdims=True)
    scale = lax.rsqrt(spread + epsilon)
    return center * scale, scale


def norm_back(values, table, d_normed):
    normed, scale = normalize(values)
    dz = (1.0 + table[0:1, :]) * d_normed
    both = jnp.mean(dz * normed, axis=1, keepdims=True)
    d_values = (dz - jnp.mean(dz, axis=1, keepdims=True) - normed * both) * scale
    d_gain = jnp.sum(d_normed * normed, axis=0, keepdims=True)
    d_shift = jnp.sum(d_normed, axis=0, keepdims=True)
    return d_values, d_gain, d_shift


def layer_kernel(names, z_size, *refs):
    held = dict(zip(names, refs))
    held.update(
        d_mixed=held["act"],
        d_query=held["mixed"],
        d_branch=held["normed_ffn"],
        d_query_low=held["attn_t"],
        d_keys_low=held["keys_t"],
        d_values_low=held["values_t"],
        g_attn=held["g_down"],
    )
    n = collections.namedtuple("Buffers", held)(**held)
    k = Links(z_size, n.send_sem, n.recv_sem)
    mp_size, block, width = n.normed.shape
    seq = mp_size * block
    heads_wide = n.wa.shape[1]
    hidden = n.wf.shape[1]
    heads = heads_wide // HD
    q_wide = heads * block
    tile = block
    far = mp_size
    own_shard = 2 * k.x + k.core
    sib_shard = 2 * k.x + 1 - k.core
    x_shard = 2 * (1 - k.x) + k.core
    diag_shard = 2 * (1 - k.x) + 1 - k.core
    shards = (own_shard, sib_shard, x_shard, diag_shard)

    def mine(r):
        return 2 * r + k.core

    def theirs(r):
        return 2 * r + 1 - k.core

    def span(i, size=tile):
        return pl.ds(pl.multiple_of(i * size, size), size)

    fetches = []

    def fetch(src, dst):
        made = pltpu.make_async_copy(src, dst, n.load_sem.at[len(fetches)])
        made.start()
        fetches.append(made)
        return made

    load_tokens = fetch(n.tokens, n.raw.at[k.x])
    load_cot = fetch(n.cotangent, n.cot.at[own_shard])

    def unpack(source, stage, sems, target, first, last):
        rows = stage.shape[1]

        def piece(i):
            slot = lax.rem(i, 2)
            return pltpu.make_async_copy(
                source.at[pl.ds(i * rows, rows)], stage.at[slot], sems.at[slot]
            )

        piece(jnp.int32(first)).start()

        def body(i, carry):
            @pl.when(i + 1 < last)
            def _():
                piece(i + 1).start()

            piece(i).wait()
            for s in range(target.shape[0]):
                target[s, span(i, rows), :] = stage[lax.rem(i, 2), :, s, :]
            return carry

        lax.fori_loop(first, last, body, 0)

    pieces_a = heads_wide // n.stage_a.shape[1]
    pieces_f = hidden // n.stage_f.shape[1]

    def unpack_ffn(part, parts):
        first, last = part * pieces_f // parts, (part + 1) * pieces_f // parts
        unpack(n.w_ffn, n.stage_f, n.stage_sem_f, n.wf, first, last)

    def partner_of(row):
        begin, first, count = 0, 0, 1
        for g in range(n.group_sizes.shape[0]):
            size = n.group_sizes[g]
            inside = jnp.logical_and(row >= begin, row < begin + size)
            first = jnp.where(inside, begin, first)
            count = jnp.where(inside, size, count)
            begin = begin + size
        step = lax.rem(n.partner_pick[row], jnp.maximum(count - 1, 1))
        return jnp.clip(first + lax.rem(row - first + 1 + step, count), 0, 2 * z_size - 1)

    k.barrier()
    send_tokens = k.swap(n.tokens, n.raw.at[k.x], k.xpeer)
    send_tokens.start()
    cot_x = k.swap(n.cotangent, n.cot.at[own_shard], k.xpeer)
    cot_x.start()
    cot_sib = k.swap(n.cotangent, n.cot.at[own_shard], k.sib)
    cot_sib.start()

    code = n.codebook[k.dp]
    start = n.prompt_start[k.dp]
    partner = partner_of(k.dp)
    other_partner = partner_of(k.dp + 1 - 2 * k.y)
    part_z, part_y = partner // 2, lax.rem(partner, 2)
    line_partners = []
    for d in range(z_size):
        row = partner_of(2 * d + k.y)
        line_partners.append((row // 2 == k.z, lax.rem(row, 2) == k.y))
    other_z, other_y = other_partner // 2, lax.rem(other_partner, 2)
    far_len = n.prompt_len[partner]
    table_attn = n.ada_attn[code]
    table_ffn = n.ada_ffn[code]

    def adapt(normed, table):
        return ((1.0 + table[0:1, :]) * normed + table[1:2, :]).astype(BF16)

    def project(s):
        normed = n.normed[s]
        query = (dot(normed, n.wa[0], 1, 1) * HD ** (-0.5)).astype(BF16)
        lane = lax.broadcasted_iota(jnp.int32, (block, heads_wide), 1) // HD
        for h in range(heads):
            n.q4[s, h * block : (h + 1) * block, :] = jnp.where(lane == h, query, 0).astype(BF16)
        for ref, turned, w in ((n.keys, n.keys_t, 1), (n.values, n.values_t, 2)):
            made = dot(normed, n.wa[w], 1, 1)
            ref[s] = made.astype(BF16)
            turned[s] = made.T.astype(BF16)

    load_tokens.wait()
    n.normed[own_shard] = adapt(normalize(n.raw[k.x].astype(F32))[0], table_attn)
    normed_own = k.swap(n.normed.at[own_shard], n.normed.at[own_shard], k.sib)
    normed_own.start()
    unpack(n.w_attn, n.stage_a, n.stage_sem_a, n.wa, 0, pieces_a)
    normed_own.wait_recv()

    def project_pair(first):
        def body(i, carry):
            project(first + i)
            return carry

        lax.fori_loop(0, 2, body, 0)

    project_pair(2 * k.x)
    send_tokens.wait_recv()
    n.normed[x_shard] = adapt(normalize(n.raw[1 - k.x].astype(F32))[0], table_attn)
    normed_x = k.swap(n.normed.at[x_shard], n.normed.at[x_shard], k.sib)
    normed_x.start()
    normed_x.wait_recv()
    project_pair(2 * (1 - k.x))

    all_keys = n.keys[0:mp_size].reshape(seq, heads_wide)
    all_values = n.values[0:mp_size].reshape(seq, heads_wide)
    from_row = lax.broadcasted_iota(jnp.int32, (block, seq), 1)
    to_row = lax.broadcasted_iota(jnp.int32, (block, seq), 0)
    window = (from_row == to_row + start).astype(F32).astype(BF16)
    cuts = 2
    sub = block // cuts
    rows_of = [slice(c * sub, (c + 1) * sub) for c in range(cuts)]
    window_keys = dot(window, all_keys).astype(BF16)
    n.y_out[1] = dot(window, all_values).astype(BF16)
    gathers, y_values, line_values = [], [], []
    for c in range(cuts):
        place = pl.ds(c * sub, sub)
        y_values.append(k.swap(n.y_out.at[1, place], n.y_in.at[1, place], k.ypeer))
        y_values[c].start()
        n.windows_k[c, k.z] = window_keys[rows_of[c]]
        gathers.append(LineGather(k, n.windows_k.at[c]))
        gathers[c].start()
        line_values.append(LineReduce(k, n.windows_v.at[c], n.passing_v.at[c]))

    def attend_own(s, carry):
        q4 = n.q4[s]
        top = jnp.full((1, q_wide), -jnp.inf, F32)
        for c in range(mp_size):
            scores = dot(n.keys[c], q4, 1, 1)
            n.wide[c] = scores
            top = jnp.maximum(top, jnp.max(scores, axis=0, keepdims=True))
        total = jnp.zeros((1, q_wide), F32)
        for c in range(mp_size):
            prob = jnp.exp(n.wide[c] - top)
            total = total + jnp.sum(prob, axis=0, keepdims=True)
            low = prob.astype(BF16)
            for h in range(heads):
                rows = slice(h * HD, (h + 1) * HD)
                part = dot(n.values_t[c, rows, :], low[:, h * block : (h + 1) * block])
                n.mixed[s, rows, :] = part if c == 0 else n.mixed[s, rows, :] + part
        n.top[s] = top
        n.total[s] = total
        return carry

    def own(s):
        lax.fori_loop(s, s + 1, attend_own, 0)

    own(0)
    for c in range(cuts):
        y_values[c].wait_recv()
        ours = n.y_out[1, rows_of[c]].astype(F32)
        others = n.y_in[1, rows_of[c]].astype(F32)
        for d in k.order:
            here, same_row = line_partners[d]
            chosen = jnp.where(same_row, ours, others)
            n.windows_v[c, d] = jnp.where(here, chosen, 0.0).astype(BF16)
            line_values[c].begin(d)
    for c in range(cuts):
        gathers[c].serve(1)
    own(1)
    for c in range(cuts):
        line_values[c].step(1)
        gathers[c].serve(2)
    own(2)
    unpack_ffn(0, 4)
    y_keys = []
    for c in range(cuts):
        line_values[c].step(2)
        gathers[c].serve(3)
        wanted = jnp.zeros((sub, heads_wide), F32)
        for d in range(z_size):
            wanted = wanted + jnp.where(other_z == d, n.windows_k[c, d].astype(F32), 0.0)
        n.y_out[0, rows_of[c]] = wanted.astype(BF16)
        place = pl.ds(c * sub, sub)
        y_keys.append(k.swap(n.y_out.at[0, place], n.y_in.at[0, place], k.ypeer))
        y_keys[c].start()
    own(3)
    unpack_ffn(1, 4)

    cot_x.wait_recv()
    cot_pass = k.swap(n.cot.at[x_shard], n.cot.at[x_shard], k.sib)
    cot_pass.start()
    unpack_ffn(2, 4)
    same_y = part_y == k.y

    for c in range(cuts):

        def take_values(total, c=c):
            n.values[far, rows_of[c]] = total.astype(BF16)

        line_values[c].finish(take_values)
        y_keys[c].wait_recv()
        here = n.windows_k[c, part_z].astype(F32)
        there = n.y_in[0, rows_of[c]].astype(F32)
        n.keys[far, rows_of[c]] = jnp.where(same_y, here, there).astype(BF16)
    n.values_t[far] = n.values[far].astype(F32).T.astype(BF16)
    n.keys_t[far] = n.keys[far].astype(F32).T.astype(BF16)

    def attend_far(s):
        scores = dot(n.keys[far], n.q4[s], 1, 1)
        slot = lax.broadcasted_iota(jnp.int32, scores.shape, 0)
        scores = jnp.where(slot < far_len, scores, -1000000000.0)
        top = jnp.maximum(n.top[s], jnp.max(scores, axis=0, keepdims=True))
        scale = jnp.exp(n.top[s] - top)
        prob = jnp.exp(scores - top)
        total = n.total[s] * scale + jnp.sum(prob, axis=0, keepdims=True)
        low = prob.astype(BF16)
        for h in range(heads):
            rows = slice(h * HD, (h + 1) * HD)
            cols = slice(h * block, (h + 1) * block)
            part = n.mixed[s, rows, :] * scale[:, cols] + dot(n.values_t[far, rows, :], low[:, cols])
            n.attn_t[s, rows, :] = (part / total[:, cols]).astype(BF16)
        n.log_total[s] = top + jnp.log(total)

    def out_part(s):
        attend_far(s)
        return dot(n.attn_t[s], n.wa[3], 0, 0)

    branch = Exchange(k, n.pair_out, n.pair_in, n.x_out, n.x_in)
    for r in range(2):
        branch.give(r, out_part(theirs(r)))
        branch.send_x(r, branch.pair_sum(r, out_part(mine(r))))

    unpack_ffn(3, 4)
    back = Exchange(k, n.pair_out, n.pair_in, n.x_out2, n.x_in2)
    load_cot.wait()
    cot_sib.wait_recv()
    cot_pass.wait_recv()

    def hidden_part(s):
        normed = n.normed_ffn[s]
        cot = n.cot[s]

        def body(i, carry):
            cols = span(i)
            up = dot(normed, n.wf[0, cols, :], 1, 1)
            d_act = dot(cot, n.wf[1, cols, :], 1, 1)
            cdf = 0.5 + 0.5 * lax.erf(up * (0.5**0.5))
            n.act[s, :, cols] = (up * cdf).astype(BF16)
            slope = cdf + up * (jnp.exp(-0.5 * up * up) * (2.0 * jnp.pi) ** (-0.5))
            n.d_up[s, :, cols] = (slope * d_act).astype(BF16)
            return carry

        lax.fori_loop(0, hidden // tile, body, 0)
        return dot(n.d_up[s], n.wf[0])

    shares = []
    for r in range(2):
        middle = n.raw[r].astype(F32) + branch.total(r)
        n.wide[r] = middle
        n.normed_ffn[mine(r)] = adapt(normalize(middle)[0], table_ffn)
        share = k.swap(n.normed_ffn.at[mine(r)], n.normed_ffn.at[mine(r)], k.sib)
        share.start()
        shares.append(share)
        share.wait_recv()
        back.give(r, hidden_part(theirs(r)))
        back.send_x(r, back.pair_sum(r, hidden_part(mine(r))))

    grid_down = GridReduce(k, n.g_down, n.h_down, n.p_down)
    upper, lower = pl.ds(0, hidden // 4), pl.ds(hidden // 4, hidden * 3 // 4)
    grid_up_z = GridReduceZ(k, n.g_up, upper, n.p_up_z, n.y_out_up, n.y_in_up)
    grid_up = GridReduce(k, n.g_up.at[:, lower], n.h_up, n.p_up)

    def spread(target, rows, made):
        for d in range(target.shape[0]):
            target[d, rows, :] = made[:, d * LANES : (d + 1) * LANES].astype(BF16)

    def ffn_grads(target, left, right):
        def body(i, carry):
            lhs = left[:, :, span(i)].reshape(seq, tile)
            spread(target, span(i), dot(lhs, right[...].reshape(seq, width), 0, 0))
            return carry

        lax.fori_loop(0, hidden // tile, body, 0)

    ffn_grads(n.g_down, n.act, n.cot)
    grid_down.send_y(*k.order[:3])
    ffn_grads(n.g_up, n.d_up, n.normed_ffn)
    grid_up_z.start()

    def down_part(s):
        return dot(n.act[s], n.wf[1])

    k.finish(branch.along_x[0])
    out_sum = Settle(branch, shards, n.x_out.at[0], n.s_in, down_part)
    n.output[...] = out_sum.kept.astype(BF16)

    n.d_keys[...] = jnp.zeros_like(n.d_keys)
    n.d_values[...] = jnp.zeros_like(n.d_values)
    table_grad = [jnp.zeros((1, width), F32), jnp.zeros((1, width), F32)]

    def prepare(s):
        d_attn_t = dot(n.wa[3], n.d_branch[s], 1, 1).astype(BF16)
        row = lax.broadcasted_iota(jnp.int32, (heads_wide, block), 0) // HD
        product = d_attn_t.astype(F32) * n.attn_t[s].astype(F32)
        for h in range(heads):
            rows = slice(h * HD, (h + 1) * HD)
            cols = slice(h * block, (h + 1) * block)
            n.delta[s, :, cols] = jnp.sum(product[rows], axis=0, keepdims=True)
            n.d_mixed[s, :, cols] = jnp.where(row == h, d_attn_t, 0).astype(BF16)

    def attend_back(s, first, last):
        q4 = n.q4[s]
        d_mixed = n.d_mixed[s]

        def body(c, carry):
            scores = dot(n.keys[c], q4, 1, 1)
            slot = lax.broadcasted_iota(jnp.int32, scores.shape, 0)
            limit = jnp.where(c == far, far_len, block)
            prob = jnp.where(slot < limit, jnp.exp(scores - n.log_total[s]), 0.0)
            low = prob.astype(BF16)
            d_prob = dot(n.values[c], d_mixed)
            d_scores = (prob * (d_prob - n.delta[s])).astype(BF16)
            n.d_values[c] += dot(low, d_mixed, 1, 1)
            n.d_keys[c] += dot(d_scores, q4)
            for h in range(heads):
                rows = slice(h * HD, (h + 1) * HD)
                n.d_query[s, rows, :] += dot(
                    n.keys_t[c, rows, :], d_scores[:, h * block : (h + 1) * block]
                )
            return carry

        lax.fori_loop(first, last, body, 0)

    n.d_query[...] = jnp.zeros_like(n.d_query)
    for r in range(2):
        d_values, d_gain, d_shift = norm_back(n.wide[r], table_ffn, back.total(r))
        table_grad[0] = table_grad[0] + d_gain
        table_grad[1] = table_grad[1] + d_shift
        d_middle = n.cot[mine(r)].astype(F32) + d_values
        n.wide[2 + r] = d_middle
        k.finish(shares[r])
        n.d_branch[mine(r)] = d_middle.astype(BF16)
        share = k.swap(n.d_branch.at[mine(r)], n.d_branch.at[mine(r)], k.sib)
        share.start()

        def far_part(i, carry, r=r):
            s = jnp.where(i == 0, mine(r), theirs(r))
            prepare(s)
            attend_back(s, far, far + 1)
            return carry

        lax.fori_loop(0, 1, far_part, 0)
        share.wait_recv()
        lax.fori_loop(1, 2, far_part, 0)
    def table_blocks(target, gain, shift):
        row = lax.broadcasted_iota(jnp.int32, (n.t_ffn.shape[1], width), 0)
        both = jnp.where(lax.rem(row, 2) == 0, gain, shift)
        both = jnp.where(row // 2 == code, both, 0.0)
        for d in range(target.shape[0]):
            target[d] = both[:, d * LANES : (d + 1) * LANES]

    packets, line_keys, y_back = [], [], []
    for one in y_keys + y_values:
        k.finish(one)
    n.y_out[0] = jnp.where(same_y, 0.0, n.d_keys[far]).astype(BF16)
    for c in range(cuts):
        place = pl.ds(c * sub, sub)
        y_back.append(k.swap(n.y_out.at[0, place], n.y_in2.at[0, place], k.ypeer))
        y_back[c].start()
        n.packets[c, k.z] = n.d_values[far, rows_of[c]].astype(BF16)
        packets.append(LineGather(k, n.packets.at[c]))
        packets[c].start()
    table_blocks(n.t_ffn, table_grad[0], table_grad[1])
    grid_t_ffn = GridReduce(k, n.t_ffn, n.ht_ffn, n.pt_ffn)
    grid_t_ffn.send_y()
    grid_down.send_y(k.order[3])
    grid_up.send_y(*k.order[:3])
    for c in range(cuts):
        gathers[c].wait_sends()
        line_keys.append(LineReduce(k, n.windows_k.at[c], n.passing_k.at[c]))

    def rest(s):
        def body(s, carry):
            attend_back(s, 0, mp_size)
            return carry

        lax.fori_loop(s, s + 1, body, 0)

    rest(0)
    for c in range(cuts):
        y_back[c].wait_recv()
        ours = n.d_keys[far, rows_of[c]]
        others = n.y_in2[0, rows_of[c]].astype(F32)
        for d in k.order:
            here = jnp.where(jnp.logical_and(same_y, part_z == d), ours, 0.0)
            there = jnp.where(jnp.logical_and(other_y == k.y, other_z == d), others, 0.0)
            n.windows_k[c, d] = (here + there).astype(BF16)
            line_keys[c].begin(d)
        packets[c].serve(1)
    rest(1)
    for c in range(cuts):
        packets[c].serve(2)
        line_keys[c].step(1)
    rest(2)
    for c in range(cuts):
        packets[c].serve(3)
        ours = jnp.zeros((sub, heads_wide), F32)
        others = jnp.zeros((sub, heads_wide), F32)
        for d in range(z_size):
            here, same_row = line_partners[d]
            packet = n.packets[c, d].astype(F32)
            other_row = jnp.logical_not(same_row)
            ours = ours + jnp.where(jnp.logical_and(here, same_row), packet, 0.0)
            others = others + jnp.where(jnp.logical_and(here, other_row), packet, 0.0)
        n.y_out[1, rows_of[c]] = others.astype(BF16)
        place = pl.ds(c * sub, sub)
        y_back.append(k.swap(n.y_out.at[1, place], n.y_in2.at[1, place], k.ypeer))
        y_back[cuts + c].start()
        n.d_values[far, rows_of[c]] = ours
        line_keys[c].step(2)
    grid_up.send_y(*k.order[3:])
    rest(3)
    grid_up_z.step()
    grid_down.take()
    grid_down.wait_y()

    half_rows = 2 * heads_wide
    grid_oq = GridReduce(k, n.g_attn.at[:, 0:half_rows], n.h_oq, n.p_oq)
    grid_kv = GridReduce(k, n.g_attn.at[:, half_rows : 2 * half_rows], n.h_kv, n.p_kv)

    def add_products(left, right):
        total = dot(left[0], right[0])
        for s in range(1, mp_size):
            total = total + dot(left[s], right[s])
        return total

    spread(n.g_attn, slice(0, heads_wide), add_products(n.attn_t, n.d_branch))
    for s in range(mp_size):
        n.d_query_low[s] = (n.d_query[s] * HD ** (-0.5)).astype(BF16)
    spread(n.g_attn, slice(heads_wide, 2 * heads_wide), add_products(n.d_query_low, n.normed))

    for c in range(cuts):

        def take_back(total, c=c):
            n.keys_t[far, rows_of[c]] = total.astype(BF16)

        line_keys[c].finish(take_back)
        y_back[cuts + c].wait_recv()
        total = n.d_values[far, rows_of[c]] + n.y_in2[1, rows_of[c]].astype(F32)
        n.values_t[far, rows_of[c]] = total.astype(BF16)
    from_slot = lax.broadcasted_iota(jnp.int32, (seq, block), 1)
    to_frame = lax.broadcasted_iota(jnp.int32, (seq, block), 0)
    unwindow = (to_frame == from_slot + start).astype(F32).astype(BF16)
    for ref, low in ((n.d_keys, n.d_keys_low), (n.d_values, n.d_values_low)):
        own = ref[0:mp_size].reshape(seq, heads_wide)
        total = own + dot(unwindow, low[far])
        low[0:mp_size] = total.astype(BF16).reshape(mp_size, block, heads_wide)

    def input_part(s):
        return (
            dot(n.d_query_low[s], n.wa[0], 0, 0)
            + dot(n.d_keys_low[s], n.wa[1])
            + dot(n.d_values_low[s], n.wa[2])
        )

    k.finish(back.along_x[0])
    n.output[...] = (n.wide[k.x] + n.output[...].astype(F32) + out_sum.total()).astype(BF16)
    in_sum = Settle(back, shards, n.x_out2.at[0], n.x_in.at[0], input_part)
    n.grad_tokens[...] = in_sum.kept.astype(BF16)

    table_grad = [jnp.zeros((1, width), F32), jnp.zeros((1, width), F32)]
    for term, at in ((n.x_out2[0].astype(F32), 1 - k.x), (in_sum.kept, k.x)):
        normed = normalize(n.raw[at].astype(F32))[0]
        table_grad[0] = table_grad[0] + jnp.sum(term * normed, axis=0, keepdims=True)
        table_grad[1] = table_grad[1] + jnp.sum(term, axis=0, keepdims=True)
    table_blocks(n.t_attn, *table_grad)
    grid_t_attn = GridReduce(k, n.t_attn, n.ht_attn, n.pt_attn)
    grid_t_attn.send_y()
    flat_normed = n.normed[...].reshape(seq, width)
    for w, low in ((2, n.d_keys_low), (3, n.d_values_low)):
        made = dot(low[0:mp_size].reshape(seq, heads_wide), flat_normed, 0, 0)
        spread(n.g_attn, slice(w * heads_wide, (w + 1) * heads_wide), made)

    grid_kv.send_y()
    grid_oq.send_y()
    grid_down.step()
    grid_t_ffn.take()
    grid_up.take(*k.order[:2])
    grid_t_ffn.step()
    grid_t_attn.take()
    grid_up.take(*k.order[2:])

    quarter = heads_wide
    half_hidden = hidden // 4

    def store_ffn(s, first, more=False):
        def store(total):
            at = pl.ds(s + 2 * first, total.shape[0], stride=2)
            n.grad_ffn[at, :] = n.grad_ffn[at, :] + total if more else total

        return store

    def store_attn(*places):
        def store(total):
            for i, s in enumerate(places):
                at = pl.ds(s, quarter, stride=4)
                rows = total[i * quarter : (i + 1) * quarter]
                n.grad_attn[at, :] = rows

        return store

    def store_table(which):
        def store(total):
            n.t_out[which, 0] = total
            pair = k.swap(n.t_out.at[which, 0], n.t_in.at[which, 0], k.sib)
            pair.start()
            pair.wait_recv()
            n.t_out[which, 1] = total + n.t_in[which, 0]

        return store

    def close_table(which, total):
        piece = LANES // mp_size
        kept = total
        for m in range(1, mp_size):
            turned = pltpu.roll(total, LANES - m * piece, 1)
            kept = jnp.where(k.mp == m, turned, kept)
        n.grad_ada[which] = kept

    grid_up_z.turn(store_ffn(0, 0))
    grid_t_attn.step()
    grid_t_ffn.finish(store_table(0))
    close_table(0, n.t_out[0, 1])
    grid_t_attn.finish(store_table(1))
    table_x = k.swap(n.t_out.at[1, 1], n.t_in.at[1, 1], k.xpeer)
    table_x.start()
    grid_up.step()
    grid_down.finish(store_ffn(1, 0))
    d_normed = n.grad_tokens[...].astype(F32) + in_sum.total()
    d_values, _, _ = norm_back(n.raw[k.x].astype(F32), table_attn, d_normed)
    n.grad_tokens[...] = (n.wide[2 + k.x] + d_values).astype(BF16)
    grid_kv.take()
    grid_up.finish(store_ffn(0, half_hidden))
    table_x.wait_recv()
    close_table(1, n.t_out[1, 1] + n.t_in[1, 1])
    grid_kv.step()
    grid_oq.take()
    grid_up_z.done(store_ffn(0, 0, more=True))
    grid_kv.finish(store_attn(1, 2))
    grid_oq.step()
    grid_oq.finish(store_attn(3, 0))
    k.finish()
    for unit in packets + line_values + line_keys:
        unit.wait_sends()
    for unit in (grid_down, grid_up, grid_up_z, grid_oq, grid_kv, grid_t_ffn, grid_t_attn):
        unit.wait_sends()
    for unit in (grid_up, grid_oq, grid_kv, grid_t_ffn, grid_t_attn):
        unit.wait_y()


def layer(tokens, cotangent, w_attn, w_ffn, ada_attn, ada_ffn, ints, dp_size, mp_size):
    z_size = dp_size // 2
    block, width = tokens.shape
    heads_wide = w_attn.shape[0]
    hidden = w_ffn.shape[0]
    heads = heads_wide // HD
    table_rows = ada_attn.shape[0] * 2
    lane_block = width // dp_size

    inputs = dict(
        tokens=tokens,
        cotangent=cotangent,
        w_attn=w_attn,
        w_ffn=w_ffn,
        ada_attn=ada_attn,
        ada_ffn=ada_ffn,
        **ints,
    )
    spaces = dict.fromkeys(("tokens", "cotangent", "w_attn", "w_ffn"), pl.ANY)
    spaces.update(dict.fromkeys(ints, pltpu.SMEM))
    outputs = dict(
        output=((block, width), BF16),
        grad_tokens=((block, width), BF16),
        grad_attn=((4 * heads_wide, lane_block), F32),
        grad_ffn=((2 * hidden, lane_block), F32),
        grad_ada=((2, table_rows, lane_block), F32),
    )
    wide = (mp_size, block, width)
    two = (2, block, width)
    square = (mp_size + 1, block, heads_wide)
    low, full = {}, {}
    for name in ("normed", "cot", "normed_ffn", "act", "d_up"):
        low[name] = wide
    low.update(raw=two, wa=(4, heads_wide, width), wf=(2, hidden, width))
    low.update(stage_a=(2, 32, 4, width), stage_f=(2, 64, 2, width))
    for name in ("keys", "values", "keys_t", "values_t"):
        low[name] = square
    low.update(q4=(mp_size, heads * block, heads_wide), attn_t=(mp_size, heads_wide, block))
    for name in ("pair_out", "pair_in", "x_out", "x_in", "x_out2", "x_in2"):
        low[name] = two
    low.update(s_in=(block, width))
    for name in ("y_out", "y_in", "y_in2"):
        low[name] = (2, block, heads_wide)
    for name in ("k", "v"):
        low["windows_" + name] = (2, z_size, block // 2, heads_wide)
        low["passing_" + name] = (2, z_size + 1, block // 2, heads_wide)
    for name in ("up", "down"):
        low["g_" + name] = (dp_size, hidden, lane_block)
    half = 2 * heads_wide
    low.update(packets=(2, z_size, block // 2, heads_wide))
    some = hidden // 4
    low.update(p_up_z=(z_size, 2, some, lane_block))
    low.update(y_out_up=(some, lane_block), y_in_up=(some, lane_block))
    for name, rows in (("up", hidden - some), ("down", hidden), ("oq", half), ("kv", half)):
        low["h_" + name] = (z_size, rows, lane_block)
        low["p_" + name] = (z_size, rows, lane_block)
    for name in ("_ffn", "_attn"):
        full["t" + name] = (dp_size, table_rows, lane_block)
        full["ht" + name] = (z_size, table_rows, lane_block)
        full["pt" + name] = (z_size, table_rows, lane_block)
    full.update(t_out=(2, 2, table_rows, lane_block), t_in=(2, 2, table_rows, lane_block))
    full.update(wide=(mp_size, block, heads * block))
    for name in ("top", "total", "log_total", "delta"):
        full[name] = (mp_size, 1, heads * block)
    full.update(mixed=(mp_size, heads_wide, block))
    full.update(d_keys=square, d_values=square)
    scratch = {name: pltpu.VMEM(shape, BF16) for name, shape in low.items()}
    scratch.update({name: pltpu.VMEM(shape, F32) for name, shape in full.items()})
    copies = 240
    scratch.update(
        load_sem=pltpu.SemaphoreType.DMA((2,)),
        stage_sem_a=pltpu.SemaphoreType.DMA((2,)),
        stage_sem_f=pltpu.SemaphoreType.DMA((2,)),
        send_sem=pltpu.SemaphoreType.DMA((copies,)),
        recv_sem=pltpu.SemaphoreType.DMA((copies,)),
    )
    names = tuple(inputs) + tuple(outputs) + tuple(scratch)
    return pl.pallas_call(
        functools.partial(layer_kernel, names, z_size),
        out_shape=tuple(jax.ShapeDtypeStruct(*shape) for shape in outputs.values()),
        in_specs=[pl.BlockSpec(memory_space=spaces.get(name, pltpu.VMEM)) for name in inputs],
        out_specs=[pl.BlockSpec(memory_space=pltpu.VMEM) for _ in outputs],
        scratch_shapes=list(scratch.values()),
        compiler_params=pltpu.CompilerParams(
            collective_id=1, has_side_effects=True, vmem_limit_bytes=60 << 20
        ),
    )(*inputs.values())


def place_kernel(count, *refs):
    moves = []
    for i in range(count):
        moves.append(pltpu.make_async_copy(refs[i], refs[count + 1 + i], refs[-1].at[i]))
        moves[i].start()
    tables, first, second = refs[count], refs[-3], refs[-2]
    for at, out in enumerate((first, second)):
        out[...] = tables[at, :, : out.shape[1]]
    for move in moves:
        move.wait()


def place(arrays, tables, piece):
    table = jax.ShapeDtypeStruct((tables.shape[1], piece), tables.dtype)
    return pl.pallas_call(
        functools.partial(place_kernel, len(arrays)),
        out_shape=tuple(jax.ShapeDtypeStruct(a.shape, a.dtype) for a in arrays) + (table, table),
        in_specs=[pl.BlockSpec(memory_space=pltpu.VMEM)] * (len(arrays) + 1),
        out_specs=[pl.BlockSpec(memory_space=pl.ANY)] * len(arrays)
        + [pl.BlockSpec(memory_space=pltpu.VMEM)] * 2,
        scratch_shapes=[pltpu.SemaphoreType.DMA((len(arrays),))],
    )(*arrays, tables)


def shards(
    tokens,
    w_attn,
    w_ffn,
    ada_attn,
    ada_ffn,
    codebook,
    group_sizes,
    partner_pick,
    prompt_start,
    prompt_len,
    cotangent,
):
    tok_rows, width = tokens.shape
    mp_size = lax.axis_size("mp")
    dp_index = lax.axis_index("dp")
    mp_index = lax.axis_index("mp")
    block_tokens = tok_rows * mp_size
    seq_here = block_tokens // LEN
    head_cols = w_attn.shape[0]
    heads_here = head_cols // HD
    total_rows = codebook.shape[0]
    dp_size = lax.axis_size("dp")
    fits = width == dp_size * LANES and width == w_ffn.shape[0] == tok_rows * heads_here
    if seq_here == 1 and mp_size == 4 and fits and tok_rows == PMAX:
        ints = dict(
            codebook=codebook,
            group_sizes=group_sizes,
            partner_pick=partner_pick,
            prompt_start=prompt_start,
            prompt_len=prompt_len,
        )
        results = layer(
            tokens,
            cotangent,
            w_attn,
            w_ffn,
            ada_attn,
            ada_ffn,
            ints,
            dp_size,
            mp_size,
        )
        piece = width // (dp_size * mp_size)
        output, grad_tokens, grad_attn, grad_ffn, *grad_ada = place(results[:4], results[4], piece)
        grad_ada = [table.reshape(ada_attn.shape[:2] + (piece,)) for table in grad_ada]
        return (
            output,
            grad_tokens,
            grad_attn.reshape(head_cols, 4, LANES),
            grad_ffn.reshape(w_ffn.shape[0], 2, LANES),
            grad_ada[1],
            grad_ada[0],
        )
    partner = partner_rows(group_sizes, partner_pick)
    first_row = dp_index * seq_here
    tok_global = (dp_index * mp_size + mp_index) * tok_rows + jnp.arange(tok_rows, dtype=jnp.int32)
    row_pick = (
        (tok_global // LEN)[:, None] == jnp.arange(total_rows, dtype=jnp.int32)[None, :]
    ).astype(jnp.int32)
    token_codes = jnp.sum(row_pick * codebook[None, :], axis=1)
    code_hot = (
        token_codes[:, None] == jnp.arange(ada_attn.shape[0], dtype=jnp.int32)[None, :]
    ).astype(jnp.float32)
    my_partner = lax.dynamic_slice_in_dim(partner, first_row, seq_here)
    my_starts = lax.dynamic_slice_in_dim(prompt_start, first_row, seq_here)
    partner_hot = (my_partner[:, None] == jnp.arange(total_rows, dtype=jnp.int32)[None, :]).astype(
        jnp.int32
    )
    partner_len = jnp.sum(partner_hot * prompt_len[None, :], axis=1)
    far_valid = jnp.arange(PMAX, dtype=jnp.int32)[None, :] < partner_len[:, None]
    inputs = tokens.astype(jnp.float32)
    normed_attn = adaptive_norm(inputs, ada_attn, code_hot).astype(jnp.bfloat16)
    normed_attn_full = lax.all_gather(normed_attn, "mp", axis=0, tiled=True)
    w_qkv = w_attn[:, 0:3, :]
    w_out = w_attn[:, 3, :]
    qkv_low = jnp.einsum(
        "td,jsd->tsj", normed_attn_full, w_qkv, preferred_element_type=jnp.float32
    ).astype(jnp.bfloat16)
    kv_rows = qkv_low[:, 1:3, :].reshape(seq_here, LEN, 2 * head_cols)
    windows = jax.vmap(
        lambda sequence, offset: lax.dynamic_slice_in_dim(sequence, offset, PMAX, 0)
    )(kv_rows, my_starts)
    shard_rows = lax.all_gather(windows, "dp", axis=0, tiled=True)
    row_ids = jnp.arange(shard_rows.shape[0], dtype=jnp.int32)
    picker = (my_partner[:, None] == row_ids[None, :]).astype(jnp.bfloat16)
    prompt_sum = jnp.einsum("kr,rpc->kpc", picker, shard_rows, preferred_element_type=jnp.float32)
    prompt_kv = prompt_sum.astype(jnp.bfloat16)
    queries = qkv_low[:, 0, :].reshape(seq_here, LEN, heads_here, HD)
    own_keys = qkv_low[:, 1, :].reshape(seq_here, LEN, heads_here, HD)
    own_values = qkv_low[:, 2, :].reshape(seq_here, LEN, heads_here, HD)
    far_keys = prompt_kv[:, :, :head_cols].reshape(seq_here, PMAX, heads_here, HD)
    far_values = prompt_kv[:, :, head_cols:].reshape(seq_here, PMAX, heads_here, HD)
    attended, log_total = lax.map(
        attend, (queries, own_keys, own_values, far_keys, far_values, far_valid)
    )
    attn_flat = attended.reshape(block_tokens, head_cols)
    middle = inputs + lax.psum_scatter(
        jnp.dot(attn_flat, w_out, preferred_element_type=jnp.float32).astype(jnp.bfloat16),
        "mp",
        scatter_dimension=0,
        tiled=True,
    ).astype(jnp.float32)
    normed_ffn = adaptive_norm(middle, ada_ffn, code_hot).astype(jnp.bfloat16)
    normed_ffn_full = lax.all_gather(normed_ffn, "mp", axis=0, tiled=True)
    w_up = w_ffn[:, 0, :]
    w_down = w_ffn[:, 1, :]
    up_proj = inner_cols(normed_ffn_full, w_up)
    activated = jax.nn.gelu(up_proj, approximate=False).astype(jnp.bfloat16)
    output = (
        middle
        + lax.psum_scatter(
            jnp.dot(activated, w_down, preferred_element_type=jnp.float32).astype(jnp.bfloat16),
            "mp",
            scatter_dimension=0,
            tiled=True,
        ).astype(jnp.float32)
    ).astype(jnp.bfloat16)
    shard_rows = lax.all_gather(cotangent, "mp", axis=0, tiled=True)
    rows_grad = inner_cols(shard_rows, w_down)
    d_act = rows_grad
    grad_down = inner_rows(activated, shard_rows)
    _, gelu_pull = jax.vjp(lambda values: jax.nn.gelu(values, approximate=False), up_proj)
    d_up = gelu_pull(d_act)[0].astype(jnp.bfloat16)
    d_normed_ffn = lax.psum_scatter(
        jnp.dot(d_up, w_up, preferred_element_type=jnp.float32).astype(jnp.bfloat16),
        "mp",
        scatter_dimension=0,
        tiled=True,
    ).astype(jnp.float32)
    grad_up = inner_rows(d_up, lax.all_gather(normed_ffn, "mp", axis=0, tiled=True))
    _, norm_ffn_pull = jax.vjp(
        lambda values, table: adaptive_norm(values, table, code_hot), middle, ada_ffn
    )
    d_middle_norm, grad_table_ffn = norm_ffn_pull(d_normed_ffn)
    d_middle = cotangent.astype(jnp.float32) + d_middle_norm
    d_branch = d_middle.astype(jnp.bfloat16)
    shard_rows = lax.all_gather(d_branch, "mp", axis=0, tiled=True)
    rows_grad = inner_cols(shard_rows, w_out)
    grad_out_proj = inner_rows(attn_flat, shard_rows)
    d_mixed = rows_grad.astype(jnp.bfloat16).reshape(seq_here, LEN, heads_here, HD)
    d_queries, d_own_keys, d_own_values, d_far_keys, d_far_values = lax.map(
        attend_back,
        (queries, own_keys, own_values, far_keys, far_values, far_valid, log_total, d_mixed),
    )
    prompt_grad = jnp.concatenate(
        [
            d_far_keys.reshape(seq_here, PMAX, head_cols),
            d_far_values.reshape(seq_here, PMAX, head_cols),
        ],
        axis=2,
    )
    row_ids = jnp.arange(lax.axis_size("dp") * seq_here, dtype=jnp.int32)
    picker = (my_partner[:, None] == row_ids[None, :]).astype(jnp.float32)
    returned_kv = lax.psum_scatter(
        jnp.einsum("kr,kpc->rpc", picker, prompt_grad, precision=highest).astype(jnp.bfloat16),
        "dp",
        scatter_dimension=0,
        tiled=True,
    ).astype(jnp.float32)
    d_kv_rows = jnp.concatenate(
        [
            d_own_keys.reshape(seq_here, LEN, head_cols),
            d_own_values.reshape(seq_here, LEN, head_cols),
        ],
        axis=2,
    )
    d_kv_rows = jax.vmap(
        lambda sequence, window, offset: lax.dynamic_update_slice_in_dim(
            sequence, lax.dynamic_slice_in_dim(sequence, offset, PMAX, 0) + window, offset, 0
        )
    )(d_kv_rows, returned_kv, my_starts)
    d_qkv = jnp.stack(
        [
            d_queries.reshape(block_tokens, head_cols),
            d_kv_rows[:, :, :head_cols].reshape(block_tokens, head_cols),
            d_kv_rows[:, :, head_cols:].reshape(block_tokens, head_cols),
        ],
        axis=1,
    ).astype(jnp.bfloat16)
    d_normed_attn = lax.psum_scatter(
        jnp.einsum("tsj,jsd->td", d_qkv, w_qkv, preferred_element_type=jnp.float32).astype(
            jnp.bfloat16
        ),
        "mp",
        scatter_dimension=0,
        tiled=True,
    ).astype(jnp.float32)
    grad_qkv = jnp.einsum(
        "tsj,td->jsd",
        d_qkv,
        lax.all_gather(normed_attn, "mp", axis=0, tiled=True),
        preferred_element_type=jnp.float32,
    )
    _, norm_attn_pull = jax.vjp(
        lambda values, table: adaptive_norm(values, table, code_hot), inputs, ada_attn
    )
    d_inputs_norm, grad_table_attn = norm_attn_pull(d_normed_attn)
    grad_tokens = (d_middle + d_inputs_norm).astype(jnp.bfloat16)
    grad_attn_local = jnp.concatenate([grad_qkv, grad_out_proj[:, None, :]], axis=1)
    grad_ffn_local = jnp.stack([grad_up, grad_down], axis=1)
    grad_attn, grad_ffn = (
        lax.psum_scatter(
            grad_attn_local.astype(jnp.bfloat16), "dp", scatter_dimension=2, tiled=True
        ).astype(jnp.float32),
        lax.psum_scatter(
            grad_ffn_local.astype(jnp.bfloat16), "dp", scatter_dimension=2, tiled=True
        ).astype(jnp.float32),
    )
    grad_ada_attn, grad_ada_ffn = (
        lax.psum_scatter(grad_table_attn, ("dp", "mp"), scatter_dimension=2, tiled=True),
        lax.psum_scatter(grad_table_ffn, ("dp", "mp"), scatter_dimension=2, tiled=True),
    )
    return (output, grad_tokens, grad_attn, grad_ffn, grad_ada_attn, grad_ada_ffn)


def solution(mesh):
    in_specs = (
        P(("dp", "mp"), None),
        P("mp", None, None),
        P("mp", None, None),
        P(),
        P(),
        P(),
        P(),
        P(),
        P(),
        P(),
        P(("dp", "mp"), None),
    )
    out_specs = (
        P(("dp", "mp"), None),
        P(("dp", "mp"), None),
        P("mp", None, "dp"),
        P("mp", None, "dp"),
        P(None, None, ("dp", "mp")),
        P(None, None, ("dp", "mp")),
    )
    return jax.shard_map(shards, mesh=mesh, in_specs=in_specs, out_specs=out_specs, check_vma=False)
```
